32 devices in a mesh: ctx: 8 (over z, x), wt: 4 (over y, core).
Axes of the slice: x: 2, y: 2, z: 4, core: 2. Of those that a mesh axis runs over, the one named last changes fastest.
Arguments:
- tokens: bfloat16 [2048, 2048], P('ctx'), may hold values from -6 to 6
- cotangent: bfloat16 [2048, 2048], P('ctx'), may hold values from -6 to 6
- doc_lengths: int32 [8], replicated, may hold values from 1 to 1280, as said below
- owners: int32 [64, 1], replicated, may hold values from 0 to 7; in each aligned block of 64 rows (0 to 63, 64 to 127, ...) at most 12 rows name the same one
- master: float32 [96, 128, 8192], P('ctx', None, 'wt'), may hold values from -0.125 to 0.125
- moment_one: float32 [96, 128, 8192], P('ctx', None, 'wt'), may hold values from -180 to 180
- moment_two: float32 [96, 128, 8192], P('ctx', None, 'wt'), may hold values from 100 to 10000
Outputs:
- output: bfloat16 [2048, 2048], P('ctx')
- input_grad: float32 [2048, 2048], P('ctx')
- new_master: float32 [96, 128, 8192], P('ctx', None, 'wt')
- new_one: float32 [96, 128, 8192], P('ctx', None, 'wt')
- new_two: float32 [96, 128, 8192], P('ctx', None, 'wt')
- new_copy: bfloat16 [96, 128, 8192], P('ctx', None, 'wt')
The draws below stay inside these ranges and needn't reach their ends.
Inputs may be any that keep to these rules, and one draw needn't show every extreme that they name: `doc_lengths`: the lengths sum to 2048; the first document is the longest, exactly 1280 tokens. `owners`: every ctx index owns 1 to 12 tiles, and one owns exactly 12.
All inputs are finite; a program needn't handle non-finite values.
Results may differ from the reference program's by a relative error of at most 0.014.
Values may be sent and summed in bfloat16 or wider, within the bound.
No kernel may reach another device: no remote copies, remote signals or barrier semaphores. Data moves between devices by JAX's collectives and lax.ppermute only.
A program may use at most 320 MiB of HBM per device.

```python
import math
import jax
import jax.numpy as jnp
import numpy as np
from jax import lax

D = 2048
HEADS = 16
HEAD_DIM = 128
FF = 8192
TILE_ROWS = 128
STEP = 3
TOKENS = 2048
NDOCS = 8
LONGEST = 1280
NTILES = 64
CAP = 12
N_CTX = 8
N_WT = 4


def draw_doc_lengths(key, part):
    rest_docs = NDOCS - 1
    extra = TOKENS - LONGEST - rest_docs
    cut_points = jnp.sort(jax.random.randint(jax.random.fold_in(key, 17), (rest_docs - 1,), 0, extra + 1).astype(jnp.int32))
    edges = jnp.concatenate([jnp.zeros((1,), jnp.int32), cut_points, jnp.full((1,), extra, jnp.int32)])
    rest_lengths = (edges[1:] - edges[:-1] + 1).astype(jnp.int32)
    return jnp.concatenate([jnp.full((1,), LONGEST, jnp.int32), rest_lengths]).astype(jnp.int32)


def levels(own_key, dims, cuts, low, high):
    def one(dim, shards_of):
        heights = jax.random.uniform(jax.random.fold_in(jax.random.fold_in(own_key, 6), dim), (shards_of,), jnp.float32, low / len(cuts), high / len(cuts))
        return jnp.repeat(jnp.exp(heights), dims[dim] // shards_of).reshape((-1,) + (1,) * (len(dims) - dim - 1))

    level = one(*cuts[0])
    for cut in cuts[1:]:
        level = level * one(*cut)
    return level


def shared_out(stream_key, own, number, rows, count, top, limit, slope):
    sequence = jax.random.permutation(stream_key, count)
    heavy_load, usual = load_shares(count, rows * top, limit, slope, True), load_shares(count, rows * top, limit, slope, False)
    places = jnp.arange(count)

    def named(tallies, turn):
        used = int((tallies > 0).sum())
        fixed = max(1, used // 4)
        shifted = fixed + (places - fixed + turn * (used - fixed)) % max(1, count - fixed)
        return jnp.zeros((count,), jnp.int32).at[sequence[jnp.where(places < fixed, places, shifted)]].set(jnp.asarray(tallies, jnp.int32))

    tallies = jnp.where(number % 4 == 0, named(heavy_load, number // 4), named(usual, number - number // 4 - 1))
    mixed = jax.random.permutation(jax.random.fold_in(own, 3), count)
    giver, taker = mixed[0:count // 2 * 2:2], mixed[1:count // 2 * 2:2]
    margin = jnp.minimum(tallies[giver] - 1, limit - tallies[taker]) // 2
    margin = jnp.where((giver == sequence[0]) | (taker == sequence[0]) | (tallies[taker] == 0), 0, jnp.maximum(margin, 0))
    shifted = jax.random.randint(jax.random.fold_in(own, 4), (count // 2,), 0, 1 << 20) % (margin + 1)
    tallies = tallies.at[giver].add(-shifted).at[taker].add(shifted)
    members = jnp.searchsorted(jnp.cumsum(tallies), jnp.arange(rows * top), side="right").astype(jnp.int32)
    table = members.reshape(top, rows).T
    table = table[jax.random.permutation(jax.random.fold_in(own, 1), rows)]
    turn = jax.random.randint(jax.random.fold_in(own, 2), (rows, 1), 0, top)
    return jnp.take_along_axis(table, (jnp.arange(top)[None, :] + turn) % top, axis=1)


def load_shares(number_of, total, reach, lean, full):
    loads = [(1 << 20) // math.isqrt(grade ** lean) + 1 for grade in range(1, number_of + 1)]
    largest = reach if full else min(reach, max(-(-total // number_of), total * loads[0] // sum(loads)))
    least = 1 if total - largest >= number_of - 1 else 0
    given, rest = [largest] + [least] * (number_of - 1), total - largest - least * (number_of - 1)
    while rest > 0:
        candidates = [i for i in range(1, number_of) if given[i] < largest] or [i for i in range(1, number_of) if given[i] < reach]
        whole, left = sum([loads[i] for i in candidates]), rest
        for i in candidates:
            addition = min(reach - given[i], max(1, left * loads[i] // whole), rest)
            given[i] = given[i] + addition
            rest = rest - addition
    return np.array(given)


def bell_draw(own_key, dims, deviation, reach, shards=(), held_as=jnp.bfloat16):
    gain = levels(own_key, dims, shards, -0.22, 0.18) if shards else 1.0
    entries = jax.random.normal(own_key, dims, jnp.float32) * deviation * gain
    return jnp.minimum(jnp.maximum(entries, -reach), reach).astype(held_as)


def setup_inputs(seed: int = 0) -> dict:
    splits = jax.random.split(jax.random.key(seed), 8)
    tokens = bell_draw(splits[0], (TOKENS, D), 1.0, 6.0, ((0, 8),))
    cotangent = bell_draw(splits[1], (TOKENS, D), 1.0, 6.0, ((0, 8),))
    doc_lengths = draw_doc_lengths(jax.random.fold_in(splits[7], 71), 0)
    owners_keys = jax.random.split(jax.random.fold_in(splits[3], 1), NTILES // NTILES)
    owners_turns = jax.random.permutation(jax.random.fold_in(splits[3], 3), NTILES // NTILES)
    owners = jax.vmap(lambda own, number: shared_out(jax.random.fold_in(splits[3], 2), own, number, NTILES, N_CTX, 1, CAP, 2))(owners_keys, owners_turns).reshape((NTILES, 1))
    master = bell_draw(splits[4], (N_CTX * CAP, TILE_ROWS, N_WT * D), D ** -0.5, 0.125, ((0, 8), (2, 4)), jnp.float32)
    moment_one = bell_draw(splits[5], (N_CTX * CAP, TILE_ROWS, N_WT * D), 30.0, 180.0, ((0, 8), (2, 4)), jnp.float32)
    moment_two = jnp.clip(jnp.exp(math.log(10000.0) - 4.6051702 * jax.random.uniform(splits[6], (N_CTX * CAP, TILE_ROWS, N_WT * D), jnp.float32) ** levels(splits[6], (N_CTX * CAP, TILE_ROWS, N_WT * D), ((0, 8), (2, 4)), -0.2, 0.2)), 100.0, 10000.0)
    return {"tokens": tokens, "cotangent": cotangent, "doc_lengths": doc_lengths, "owners": owners, "master": master, "moment_one": moment_one, "moment_two": moment_two}


adam_beta = 0.5
learn_rate = 0.01
decay_rate = 0.1
adam_eps = 1e-08
norm_eps = 1e-05
neg_fill = -1e+30
rope_base = 10000.0

@jax.custom_vjp
def low(v):
    return lax.optimization_barrier(v.astype(jnp.bfloat16)).astype(jnp.float32)

@jax.custom_vjp
def low_back(v):
    return v

def low_keep(v):
    return (low(v), None)

def low_pass(kept, grad):
    return (grad,)

def back_keep(v):
    return (v, None)

def back_low(kept, grad):
    return (low(grad),)
low.defvjp(low_keep, low_pass)
low_back.defvjp(back_keep, back_low)

def layer_norm(values):
    center = values - lax.optimization_barrier(jnp.mean(values, axis=-1, keepdims=True))
    spread = lax.optimization_barrier(jnp.mean(center * center, axis=-1, keepdims=True))
    return center * lax.rsqrt(spread + norm_eps)

def rotary(values, positions):
    half_dim = values.shape[-1] // 2
    frequencies = rope_base ** (-jnp.arange(half_dim, dtype=jnp.float32) * (2.0 / values.shape[-1]))
    angles = positions.astype(jnp.float32)[:, None] * frequencies[None, :]
    cosine = jnp.cos(angles)[:, None, :]
    sine_vals = jnp.sin(angles)[:, None, :]
    first_half = values[..., :half_dim]
    second_half = values[..., half_dim:]
    return jnp.concatenate([first_half * cosine - second_half * sine_vals, second_half * cosine + first_half * sine_vals], axis=-1)

def doc_index(positions, doc_starts):
    return lax.optimization_barrier(jnp.sum((positions[:, None] >= doc_starts[None, :]).astype(jnp.int32), axis=1)) - 1

def matmul(left, right):
    return jnp.dot(left, right, precision=lax.Precision.HIGHEST, preferred_element_type=jnp.float32)

def assemble(tile_vals):
    split_tiles = tile_vals.reshape(NTILES, TILE_ROWS, N_WT, D)
    part_q = D * (D // N_WT)
    part_f = D * (FF // N_WT)
    span_list = [part_q, part_q, part_q, part_q, part_f, part_f, part_f]
    shape_list = [(D, D // N_WT), (D, D // N_WT), (D, D // N_WT), (D // N_WT, D), (D, FF // N_WT), (D, FF // N_WT), (FF // N_WT, D)]
    join_axes = [1, 1, 1, 0, 1, 1, 0]
    pieces = [[], [], [], [], [], [], []]
    for shard_idx in range(N_WT):
        flat_vals = split_tiles[:, :, shard_idx, :].reshape(-1)
        offset = 0
        for matrix_idx in range(7):
            span_len = span_list[matrix_idx]
            pieces[matrix_idx].append(flat_vals[offset:offset + span_len].reshape(shape_list[matrix_idx]))
            offset += span_len
    return tuple((jnp.concatenate(pieces[matrix_idx], axis=join_axes[matrix_idx]) for matrix_idx in range(7)))

def attention(query, keys, values, positions, doc_ids):
    block_len = min(512, TOKENS)
    n_blocks = TOKENS // block_len
    score_scale = 1.0 / math.sqrt(HEAD_DIM)
    q_blocks = query.reshape(n_blocks, block_len, HEADS, HEAD_DIM)
    pos_blocks = positions.reshape(n_blocks, block_len)
    doc_blocks = doc_ids.reshape(n_blocks, block_len)

    def one_block(inputs):
        q_part, pos_part, doc_part = inputs
        raw_scores = jnp.einsum('qhd,khd->hqk', q_part, keys, precision=lax.Precision.HIGHEST)
        raw_scores = low_back(raw_scores)
        visible_mask = (positions[None, :] <= pos_part[:, None]) & (doc_ids[None, :] == doc_part[:, None])
        scores = jnp.where(visible_mask[None], raw_scores * score_scale, neg_fill)
        row_top = lax.optimization_barrier(jnp.max(scores, axis=-1, keepdims=True))
        weights_exp = jnp.exp(scores - row_top)
        prob_vals = low(weights_exp / lax.optimization_barrier(jnp.sum(weights_exp, axis=-1, keepdims=True)))
        return jnp.einsum('hqk,khd->qhd', prob_vals, values, precision=lax.Precision.HIGHEST)
    blocks_out = lax.map(jax.checkpoint(one_block), (q_blocks, pos_blocks, doc_blocks))
    return blocks_out.reshape(TOKENS, HEADS * HEAD_DIM)

def layer_forward(inputs, tile_vals, positions, doc_ids):
    w_query, w_key, w_value, w_out, w_gate, w_up, w_down = assemble(low(tile_vals))
    normed = low(layer_norm(inputs))
    q_pre = low_back(matmul(normed, w_query)).reshape(TOKENS, HEADS, HEAD_DIM)
    k_pre = low_back(matmul(normed, w_key)).reshape(TOKENS, HEADS, HEAD_DIM)
    v_all = low(low_back(matmul(normed, w_value))).reshape(TOKENS, HEADS, HEAD_DIM)
    q_rot = low(rotary(q_pre, positions))
    k_rot = low(rotary(k_pre, positions))
    attended = attention(q_rot, k_rot, v_all, positions, doc_ids)
    attended = low(low_back(attended))
    residual = inputs + low_back(matmul(attended, w_out))
    normed_two = low(layer_norm(residual))
    gate_vals = low_back(matmul(normed_two, w_gate))
    up_vals = low_back(matmul(normed_two, w_up))
    hidden = low(gate_vals * jax.nn.sigmoid(gate_vals) * up_vals)
    return residual + low_back(matmul(hidden, w_down))

def reference(tokens, cotangent, doc_lengths, owners, master, moment_one, moment_two):
    positions = jnp.arange(TOKENS, dtype=jnp.int32)
    doc_starts = (jnp.cumsum(doc_lengths) - doc_lengths).astype(jnp.int32)
    doc_ids = doc_index(positions, doc_starts)
    owner_col = owners[:, 0]
    tile_ids = jnp.arange(NTILES, dtype=jnp.int32)
    earlier = (owner_col[None, :] == owner_col[:, None]) & (tile_ids[None, :] < tile_ids[:, None])
    slot_ids = (owner_col * CAP + lax.optimization_barrier(jnp.sum(earlier.astype(jnp.int32), axis=1))).astype(jnp.int32)
    tile_vals = master[slot_ids]

    def wrapped(inputs, tile_args):
        return layer_forward(inputs, tile_args, positions, doc_ids)
    output, pullback = jax.vjp(wrapped, tokens.astype(jnp.float32), tile_vals)
    input_grad, tile_grads = pullback(cotangent.astype(jnp.float32))
    slot_grads = jnp.zeros_like(master).at[slot_ids].set(tile_grads)
    new_one = adam_beta * moment_one + (1.0 - adam_beta) * slot_grads
    new_two = adam_beta * moment_two + (1.0 - adam_beta) * slot_grads * slot_grads
    bias_one = 1.0 - adam_beta ** STEP
    bias_two = 1.0 - adam_beta ** STEP
    step_ratio = new_one / bias_one / (jnp.sqrt(new_two / bias_two) + adam_eps)
    new_master = master - learn_rate * (step_ratio + decay_rate * master)
    return (output.astype(jnp.bfloat16), input_grad, new_master, new_one, new_two, new_master.astype(jnp.bfloat16))
```

```python
from functools import partial
import math

import jax
import jax.numpy as jnp
from jax import lax
from jax.experimental import pallas as pl
from jax.experimental.pallas import tpu as pltpu
from jax.sharding import PartitionSpec as P

HEAD_DIM = 128
STEP = 3


adam_beta = 0.5
learn_rate = 0.01
decay_rate = 0.1
adam_eps = 1e-08
norm_eps = 1e-05
neg_fill = -1e30
rope_base = 10000.0


def from_behind(x, axis, by):
    count = lax.axis_size(axis)
    pairs = [(i, i + by) for i in range(count) if 0 <= i + by < count]
    return lax.ppermute(x, axis, pairs)


def from_behind_2(value, axis, steps):
    count = lax.axis_size(axis)
    pairs = [(source, (source + steps) % count) for source in range(count)]
    return lax.ppermute(value, axis, pairs)


def layer_norm(values):
    center = values - jnp.mean(values, axis=-1, keepdims=True)
    spread = jnp.mean(center * center, axis=-1, keepdims=True)
    return center * lax.rsqrt(spread + norm_eps)


def rotary(values, positions):
    half_dim = values.shape[-1] // 2
    frequencies = rope_base ** (-jnp.arange(half_dim, dtype=jnp.float32) * (2.0 / values.shape[-1]))
    angles = positions.astype(jnp.float32)[:, None] * frequencies[None, :]
    cosine = jnp.cos(angles)[:, None, :]
    sine_vals = jnp.sin(angles)[:, None, :]
    first_half = values[..., :half_dim]
    second_half = values[..., half_dim:]
    return jnp.concatenate(
        [
            first_half * cosine - second_half * sine_vals,
            second_half * cosine + first_half * sine_vals,
        ],
        axis=-1,
    )


def doc_index(positions, doc_starts):
    return jnp.sum((positions[:, None] >= doc_starts[None, :]).astype(jnp.int32), axis=1) - 1


def heads_dot(spec, left, right):
    return jnp.einsum(spec, left, right, preferred_element_type=jnp.float32)


def general_shards(tokens, cotangent, doc_lengths, owners, master, moment_one, moment_two):
    n_ctx = lax.axis_size("ctx")
    n_wt = lax.axis_size("wt")
    ctx_index = lax.axis_index("ctx")
    tok_rows, width = tokens.shape
    cap_slots, tile_rows, tile_width = master.shape
    n_tiles = owners.shape[0]
    head_dim = HEAD_DIM
    owner_col = owners[:, 0]
    tile_ids = jnp.arange(n_tiles, dtype=jnp.int32)
    earlier = (owner_col[None, :] == owner_col[:, None]) & (tile_ids[None, :] < tile_ids[:, None])
    slot_ids = owner_col * cap_slots + jnp.sum(earlier.astype(jnp.int32), axis=1)
    every_slot = lax.all_gather(master.astype(jnp.bfloat16), "ctx", axis=0, tiled=True)
    flat_w = every_slot[slot_ids].reshape(-1)
    local_width = width // n_wt
    heads_local = local_width // head_dim
    part_q = width * local_width
    ff_local = (flat_w.shape[0] - 4 * part_q) // (3 * width)
    part_f = width * ff_local
    w_qkv = flat_w[: 3 * part_q].reshape(3, width, local_width)
    w_out = flat_w[3 * part_q : 4 * part_q].reshape(local_width, width)
    w_gateup = flat_w[4 * part_q : 4 * part_q + 2 * part_f].reshape(2, width, ff_local)
    w_down = flat_w[4 * part_q + 2 * part_f :].reshape(ff_local, width)
    positions = ctx_index * tok_rows + jnp.arange(tok_rows, dtype=jnp.int32)
    doc_starts = jnp.cumsum(doc_lengths) - doc_lengths
    q_docs = doc_index(positions, doc_starts)
    score_scale = 1.0 / math.sqrt(head_dim)
    inputs = tokens.astype(jnp.float32)
    normed, norm_back = jax.vjp(layer_norm, inputs)
    normed_low = normed.astype(jnp.bfloat16)
    qkv_vals = heads_dot("td,jde->jte", normed_low, w_qkv)
    shaped = qkv_vals.reshape(3, tok_rows, heads_local, head_dim)
    rope_here = partial(rotary, positions=positions)
    qk_rot, rope_back = jax.vjp(rope_here, jnp.concatenate([shaped[0], shaped[1]], axis=1))
    q_low = qk_rot[:, :heads_local].astype(jnp.bfloat16)
    k_low = qk_rot[:, heads_local:].astype(jnp.bfloat16)
    v_low = shaped[2].astype(jnp.bfloat16)

    def masked_scores(key_block, key_pos, key_docs):
        raw_scores = heads_dot("qhd,khd->hqk", q_low, key_block)
        visible_mask = (key_pos[None, :] <= positions[:, None]) & (
            key_docs[None, :] == q_docs[:, None]
        )
        return (jnp.where(visible_mask[None], raw_scores * score_scale, neg_fill), visible_mask)

    def over_blocks(kv_piece, first_row, update_fn, running):
        key_count = kv_piece[0].shape[0]
        block_len = math.gcd(key_count, 512)
        n_blocks = key_count // block_len
        split_kv = tuple(
            (member.reshape((n_blocks, block_len) + member.shape[1:]) for member in kv_piece)
        )

        def step_fn(block_state, inputs_here):
            block_idx, block_vals = inputs_here
            block_row = first_row + block_idx * block_len
            key_pos = block_row + jnp.arange(block_len, dtype=jnp.int32)
            key_docs = doc_index(key_pos, doc_starts)
            block_state = update_fn(block_state, block_vals, key_pos, key_docs, block_row)
            return (block_state, None)

        running, unused = lax.scan(
            step_fn, running, (jnp.arange(n_blocks, dtype=jnp.int32), split_kv)
        )
        return running

    def norm_update(block_state, block_vals, key_pos, key_docs, block_row):
        row_top, row_total = block_state
        scores, visible_mask = masked_scores(block_vals[0], key_pos, key_docs)
        new_top = jnp.maximum(row_top, jnp.max(scores, axis=-1))
        weights_exp = jnp.where(visible_mask[None], jnp.exp(scores - new_top[:, :, None]), 0.0)
        return (new_top, row_total * jnp.exp(row_top - new_top) + jnp.sum(weights_exp, axis=-1))

    start_top = jnp.full((heads_local, tok_rows), neg_fill, jnp.float32)
    start_total = jnp.zeros((heads_local, tok_rows), jnp.float32)
    row_top, row_total = over_blocks(
        (lax.all_gather(k_low, "ctx", axis=0, tiled=True),),
        jnp.int32(0),
        norm_update,
        (start_top, start_total),
    )
    log_sum = row_top + jnp.log(row_total)

    def block_probs(key_block, key_pos, key_docs):
        scores, visible_mask = masked_scores(key_block, key_pos, key_docs)
        return jnp.where(visible_mask[None], jnp.exp(scores - log_sum[:, :, None]), 0.0)

    def value_update(block_state, block_vals, key_pos, key_docs, block_row):
        prob_vals = block_probs(block_vals[0], key_pos, key_docs)
        return block_state + heads_dot(
            "hqk,khd->qhd", prob_vals.astype(jnp.bfloat16), block_vals[1]
        )

    zero_heads = jnp.zeros((tok_rows, heads_local, head_dim), jnp.float32)
    attended = over_blocks(
        (
            lax.all_gather(k_low, "ctx", axis=0, tiled=True),
            lax.all_gather(v_low, "ctx", axis=0, tiled=True),
        ),
        jnp.int32(0),
        value_update,
        zero_heads,
    )
    att_low = attended.reshape(tok_rows, local_width).astype(jnp.bfloat16)
    attn_part = jnp.dot(att_low, w_out, preferred_element_type=jnp.float32)
    residual = inputs + lax.psum(attn_part.astype(jnp.bfloat16), "wt").astype(jnp.float32)
    normed_two, norm_two_back = jax.vjp(layer_norm, residual)
    normed_two_low = normed_two.astype(jnp.bfloat16)
    gateup_vals = heads_dot("td,jde->jte", normed_two_low, w_gateup)
    gate_vals = gateup_vals[0]
    up_vals = gateup_vals[1]
    gate_sig = jax.nn.sigmoid(gate_vals)
    silu_vals = gate_vals * gate_sig
    hidden_low = (silu_vals * up_vals).astype(jnp.bfloat16)
    mlp_part = jnp.dot(hidden_low, w_down, preferred_element_type=jnp.float32)
    output = (residual + lax.psum(mlp_part.astype(jnp.bfloat16), "wt").astype(jnp.float32)).astype(
        jnp.bfloat16
    )
    out_grad = cotangent.astype(jnp.float32)
    grad_down = heads_dot("tf,td->fd", hidden_low, cotangent)
    grad_hidden = heads_dot("td,fd->tf", cotangent, w_down)
    grad_gate = grad_hidden * up_vals * gate_sig * (1.0 + gate_vals * (1.0 - gate_sig))
    grad_up = grad_hidden * silu_vals
    grad_gu_low = jnp.stack([grad_gate, grad_up]).astype(jnp.bfloat16)
    grad_gateup = heads_dot("td,jte->jde", normed_two_low, grad_gu_low)
    norm_two_part = heads_dot("jte,jde->td", grad_gu_low, w_gateup)
    norm_two_grad = lax.psum(norm_two_part.astype(jnp.bfloat16), "wt").astype(jnp.float32)
    resid_grad = out_grad + norm_two_back(norm_two_grad)[0]
    resid_low = resid_grad.astype(jnp.bfloat16)
    grad_out = heads_dot("tc,td->cd", att_low, resid_low)
    att_grad = heads_dot("td,cd->tc", resid_low, w_out)
    att_grad_low = att_grad.astype(jnp.bfloat16).reshape(tok_rows, heads_local, head_dim)
    row_delta = jnp.sum(att_grad_low * attended, axis=-1).T

    def grad_block(block_vals, key_pos, key_docs):
        prob_vals = block_probs(block_vals[0], key_pos, key_docs)
        value_grad = heads_dot("hqk,qhd->khd", prob_vals.astype(jnp.bfloat16), att_grad_low)
        prob_grad = heads_dot("qhd,khd->hqk", att_grad_low, block_vals[1])
        raw_grad = (prob_vals * (prob_grad - row_delta[:, :, None]) * score_scale).astype(
            jnp.bfloat16
        )
        query_grad = heads_dot("hqk,khd->qhd", raw_grad, block_vals[0])
        key_grad = heads_dot("hqk,qhd->khd", raw_grad, q_low)
        return (query_grad, key_grad, value_grad)

    def add_rows(target, addend):
        return target + addend

    def cycle_step(turn_idx, cycle_state):
        query_acc, key_cur, value_cur, key_acc, value_acc = cycle_state
        anchor = (ctx_index - turn_idx) % n_ctx

        def cycle_update(block_state, block_vals, key_pos, key_docs, block_row):
            q_acc, k_acc, v_acc = block_state
            query_grad, key_grad, value_grad = grad_block(block_vals, key_pos, key_docs)
            return (q_acc + query_grad, add_rows(k_acc, key_grad), add_rows(v_acc, value_grad))

        query_acc, key_acc, value_acc = over_blocks(
            (key_cur, value_cur), anchor * tok_rows, cycle_update, (query_acc, key_acc, value_acc)
        )
        key_cur, value_cur = from_behind((key_cur, value_cur), "ctx", 1)
        key_acc, value_acc = (
            from_behind_2(key_acc.astype(jnp.bfloat16), "ctx", 1).astype(key_acc.dtype),
            from_behind_2(value_acc.astype(jnp.bfloat16), "ctx", 1).astype(value_acc.dtype),
        )
        return (query_acc, key_cur, value_cur, key_acc, value_acc)

    cycle_start = (zero_heads, k_low, v_low, zero_heads, zero_heads)
    query_acc, key_last, value_last, key_acc, value_acc = lax.fori_loop(
        0, n_ctx, cycle_step, cycle_start
    )
    qk_pre_grad = rope_back(jnp.concatenate([query_acc, key_acc], axis=1))[0]
    qkv_grad_low = jnp.stack(
        [
            qk_pre_grad[:, :heads_local].reshape(tok_rows, local_width),
            qk_pre_grad[:, heads_local:].reshape(tok_rows, local_width),
            value_acc.reshape(tok_rows, local_width),
        ]
    ).astype(jnp.bfloat16)
    grad_qkv = heads_dot("td,jte->jde", normed_low, qkv_grad_low)
    norm_one_part = heads_dot("jte,jde->td", qkv_grad_low, w_qkv)
    norm_one_grad = lax.psum(norm_one_part.astype(jnp.bfloat16), "wt").astype(jnp.float32)
    input_grad = resid_grad + norm_back(norm_one_grad)[0]
    grad_tiles = jnp.concatenate(
        [grad_qkv.reshape(-1), grad_out.reshape(-1), grad_gateup.reshape(-1), grad_down.reshape(-1)]
    ).reshape(n_tiles, tile_rows, tile_width)
    slot_range = jnp.arange(n_ctx * cap_slots, dtype=jnp.int32)
    matches = slot_ids[None, :] == slot_range[:, None]
    tile_of_slot = jnp.sum(jnp.where(matches, tile_ids[None, :], 0), axis=1)
    slot_used = jnp.any(matches, axis=1)
    slot_grads = lax.psum_scatter(
        jnp.where(slot_used[:, None, None], grad_tiles[tile_of_slot], 0.0).astype(jnp.bfloat16),
        "ctx",
        scatter_dimension=0,
        tiled=True,
    ).astype(jnp.float32)
    new_one = adam_beta * moment_one + (1.0 - adam_beta) * slot_grads
    new_two = adam_beta * moment_two + (1.0 - adam_beta) * slot_grads * slot_grads
    bias_one = 1.0 - adam_beta**STEP
    bias_two = 1.0 - adam_beta**STEP
    step_ratio = new_one / bias_one / (jnp.sqrt(new_two / bias_two) + adam_eps)
    new_master = master - learn_rate * (step_ratio + decay_rate * master)
    return (output, input_grad, new_master, new_one, new_two, new_master.astype(jnp.bfloat16))


AXES = ("ctx", "wt")
LOW = jnp.bfloat16
F32 = jnp.float32


def swap(value, ctx_bits, wt_bits):
    n_ctx, n_wt = lax.axis_size("ctx"), lax.axis_size("wt")
    pairs = [
        (c * n_wt + w, (c ^ ctx_bits) * n_wt + (w ^ wt_bits))
        for c in range(n_ctx)
        for w in range(n_wt)
    ]
    return lax.ppermute(value, AXES, pairs)


def dot(left, right):
    return jnp.dot(left, right, preferred_element_type=F32)


def dot_tn(left, right):
    return lax.dot_general(left, right, (((0,), (0,)), ((), ())), preferred_element_type=F32)


def dot_nt(left, right):
    return lax.dot_general(left, right, (((1,), (1,)), ((), ())), preferred_element_type=F32)


def lane_split(value, lane_starts):
    count, rows, width = value.shape
    homes = lane_starts.shape[0] // 2

    def body(starts, src, *outs):
        for home in range(homes):
            for half in range(2):
                start = pl.multiple_of(starts[2 * home + half], 128)
                outs[home][0, :, half * 128 : half * 128 + 128] = src[
                    0, :, pl.ds(start, 128)
                ].astype(LOW)

    return pl.pallas_call(
        body,
        grid_spec=pltpu.PrefetchScalarGridSpec(
            num_scalar_prefetch=1,
            grid=(count,),
            in_specs=[pl.BlockSpec((1, rows, width), lambda i, s: (i, 0, 0))],
            out_specs=[pl.BlockSpec((1, rows, 256), lambda i, s: (i, 0, 0))] * homes,
        ),
        out_shape=[jax.ShapeDtypeStruct((count, rows, 256), LOW)] * homes,
        name="lane_split",
    )(lane_starts, value)


def lane_join(pieces, lane_starts):
    count, rows, _ = pieces[0].shape
    homes = len(pieces)
    width = homes * 256

    def body(starts, *refs):
        out = refs[-1]
        for home in range(homes):
            for half in range(2):
                start = pl.multiple_of(starts[2 * home + half], 128)
                out[0, :, pl.ds(start, 128)] = refs[home][0, :, half * 128 : half * 128 + 128]

    return pl.pallas_call(
        body,
        grid_spec=pltpu.PrefetchScalarGridSpec(
            num_scalar_prefetch=1,
            grid=(count,),
            in_specs=[pl.BlockSpec((1, rows, 256), lambda i, s: (i, 0, 0))] * homes,
            out_specs=pl.BlockSpec((1, rows, width), lambda i, s: (i, 0, 0)),
        ),
        out_shape=jax.ShapeDtypeStruct((count, rows, width), LOW),
        name="lane_join",
    )(lane_starts, *pieces)


def row_gather(sources, picked, rows, sizes):
    total = sum(sizes)
    n_src = len(sources)

    def body(which, where, *refs):
        srcs, outs, sem = refs[:n_src], refs[n_src:-1], refs[-1]
        first = 0
        for out, size in zip(outs, sizes):

            def start(j, carry, out=out, first=first):
                t = first + j
                for n in range(n_src):

                    @pl.when(which[t] == n)
                    def _(n=n):
                        pltpu.make_async_copy(srcs[n].at[where[t]], out.at[j], sem.at[t]).start()

                return carry

            lax.fori_loop(0, size, start, 0)
            first += size
        first = 0
        for out, size in zip(outs, sizes):

            def finish(j, carry, out=out, first=first):
                pltpu.make_async_copy(srcs[0].at[0], out.at[j], sem.at[first + j]).wait()
                return carry

            lax.fori_loop(0, size, finish, 0)
            first += size

    tail = sources[0].shape[1:]
    return pl.pallas_call(
        body,
        grid_spec=pltpu.PrefetchScalarGridSpec(
            num_scalar_prefetch=2,
            grid=(1,),
            in_specs=[pl.BlockSpec(memory_space=pl.ANY)] * n_src,
            out_specs=[pl.BlockSpec(memory_space=pl.ANY)] * len(sizes),
            scratch_shapes=[pltpu.SemaphoreType.DMA((total,))],
        ),
        out_shape=[jax.ShapeDtypeStruct((size,) + tail, LOW) for size in sizes],
        name="row_gather",
    )(picked, rows, *sources)


def visible_scores(query, key, q_pos, q_doc, k_pos, k_doc):
    raw = dot_nt(query, key) * (1.0 / math.sqrt(HEAD_DIM))
    seen = (k_pos <= q_pos) & (k_doc == q_doc)
    return jnp.where(seen, raw, neg_fill)


def attend(query, key, value, q_pos, q_doc, k_pos, k_doc, n_blocks):
    rows = query.shape[0]
    block = rows // n_blocks

    def body(q, k, v, qp, qd, kp, kd, out, lse):
        scores = visible_scores(q[...], k[...], qp[...], qd[...], kp[...], kd[...])
        top = jnp.max(scores, axis=1, keepdims=True)
        weights = jnp.exp(scores - top)
        total = jnp.sum(weights, axis=1, keepdims=True)
        probs = (weights * (1.0 / total)).astype(LOW)
        out[...] = dot(probs, v[...]).astype(LOW)
        lse[...] = top + jnp.log(total)

    whole = lambda arr: pl.BlockSpec(arr.shape, lambda i: (0, 0))
    part = lambda arr: pl.BlockSpec((block, arr.shape[1]), lambda i: (i, 0))
    return pl.pallas_call(
        body,
        grid=(n_blocks,),
        in_specs=[
            part(query), whole(key), whole(value), part(q_pos), part(q_doc), whole(k_pos), whole(k_doc),
        ],
        out_specs=[
            pl.BlockSpec((block, HEAD_DIM), lambda i: (i, 0)),
            pl.BlockSpec((block, 1), lambda i: (i, 0)),
        ],
        out_shape=[
            jax.ShapeDtypeStruct((rows, HEAD_DIM), LOW),
            jax.ShapeDtypeStruct((rows, 1), F32),
        ],
        name="attend",
    )(query, key, value, q_pos, q_doc, k_pos, k_doc)


def attend_back(query, key, value, out_grad, lse, q_pos, q_doc, k_pos, k_doc, n_blocks):
    rows = query.shape[0]
    block = rows // n_blocks
    n_keys = key.shape[0]

    def body(q, k, v, do, ls, qp, qd, kp, kd, dq, dk, dv):
        @pl.when(pl.program_id(0) == 0)
        def _():
            dk[...] = jnp.zeros_like(dk)
            dv[...] = jnp.zeros_like(dv)

        scores = visible_scores(q[...], k[...], qp[...], qd[...], kp[...], kd[...])
        probs = jnp.exp(scores - ls[...])
        prob_grad = dot_nt(do[...], v[...])
        delta = jnp.sum(probs * prob_grad, axis=1, keepdims=True)
        score_grad = (probs * (prob_grad - delta) * (1.0 / math.sqrt(HEAD_DIM))).astype(LOW)
        dq[...] = dot(score_grad, k[...])
        dk[...] += dot_tn(score_grad, q[...])
        dv[...] += dot_tn(probs.astype(LOW), do[...])

    whole = lambda arr: pl.BlockSpec(arr.shape, lambda i: (0, 0))
    part = lambda arr: pl.BlockSpec((block, arr.shape[1]), lambda i: (i, 0))
    kept = pl.BlockSpec((n_keys, HEAD_DIM), lambda i: (0, 0))
    return pl.pallas_call(
        body,
        grid=(n_blocks,),
        in_specs=[
            part(query), whole(key), whole(value), part(out_grad), part(lse),
            part(q_pos), part(q_doc), whole(k_pos), whole(k_doc),
        ],
        out_specs=[pl.BlockSpec((block, HEAD_DIM), lambda i: (i, 0)), kept, kept],
        out_shape=[
            jax.ShapeDtypeStruct((rows, HEAD_DIM), F32),
            jax.ShapeDtypeStruct((n_keys, HEAD_DIM), F32),
            jax.ShapeDtypeStruct((n_keys, HEAD_DIM), F32),
        ],
        name="attend_back",
    )(query, key, value, out_grad, lse, q_pos, q_doc, k_pos, k_doc)


def update(master, moment_one, moment_two, pieces, lane_starts, used):
    count, rows, width = master.shape
    homes = len(pieces)
    bias = 1.0 - adam_beta**STEP

    def body(starts, live, mas, one, two, *refs):
        grads, (new_mas, new_one, new_two, copy) = refs[:homes], refs[homes:]
        alive = live[pl.program_id(0)] > 0
        for home in range(homes):
            for half in range(2):
                at = (0, slice(None), pl.ds(pl.multiple_of(starts[2 * home + half], 128), 128))
                grad = grads[home][0, :, half * 128 : half * 128 + 128].astype(F32)
                grad = jnp.where(alive, grad, 0.0)
                first = adam_beta * one[at] + (1.0 - adam_beta) * grad
                second = adam_beta * two[at] + (1.0 - adam_beta) * grad * grad
                ratio = (first * (1.0 / bias)) / (jnp.sqrt(second * (1.0 / bias)) + adam_eps)
                old = mas[at]
                new = old - learn_rate * (ratio + decay_rate * old)
                new_mas[at] = new
                new_one[at] = first
                new_two[at] = second
                copy[at] = new.astype(LOW)

    slot = pl.BlockSpec((1, rows, width), lambda i, s, u: (i, 0, 0))
    piece = pl.BlockSpec((1, rows, 256), lambda i, s, u: (i, 0, 0))
    return pl.pallas_call(
        body,
        grid_spec=pltpu.PrefetchScalarGridSpec(
            num_scalar_prefetch=2,
            grid=(count,),
            in_specs=[slot] * 3 + [piece] * homes,
            out_specs=[slot] * 4,
        ),
        out_shape=[jax.ShapeDtypeStruct(master.shape, F32)] * 3
        + [jax.ShapeDtypeStruct(master.shape, LOW)],
        name="update",
    )(lane_starts, used, master, moment_one, moment_two, *pieces)


def gather_rows(piece):
    near = [piece] + [swap(piece, 2 * k, 0) for k in (1, 2, 3)]
    blocks = []
    for part in near:
        pair = jnp.concatenate([part, swap(part, 0, 2)])
        blocks += [pair, swap(pair, 0, 1)]
    return jnp.concatenate(blocks)


def scatter_sum(partial_sum):
    quarter = partial_sum.shape[0] // 4
    half, rows = quarter // 2, quarter // 4
    kept = [None] * 4
    for k in (3, 2, 1, 0):
        chunk = partial_sum[quarter * k : quarter * (k + 1)]
        other = swap(chunk[half:].astype(LOW), 0, 1)
        pair = chunk[:half].astype(F32) + other.astype(F32)
        other = swap(pair[rows:].astype(LOW), 0, 2)
        kept[k] = pair[:rows] + other.astype(F32)
    total = kept[0]
    for k in (1, 2, 3):
        total = total + swap(kept[k].astype(LOW), 2 * k, 0).astype(F32)
    return total


def share_rows(piece, wt_index):
    rows = piece.shape[0]
    out = jnp.zeros((4 * rows,) + piece.shape[1:], piece.dtype)
    over_y = swap(piece, 0, 2)
    for bits, part in ((0, piece), (2, over_y), (1, swap(piece, 0, 1)), (3, swap(over_y, 0, 1))):
        out = lax.dynamic_update_slice(out, part, ((wt_index ^ bits) * rows, 0))
    return out


def rotate(values, cosine, sine):
    half = values.shape[-1] // 2
    first, second = values[:, :half], values[:, half:]
    return jnp.concatenate([first * cosine - second * sine, second * cosine + first * sine], axis=1)


def fast_shards(tokens, cotangent, doc_lengths, owners, master, moment_one, moment_two):
    ctx, wt = lax.axis_index("ctx"), lax.axis_index("wt")
    n_ctx = lax.axis_size("ctx")
    z_at, x_at = ctx // 2, ctx % 2
    tok_rows, width = tokens.shape
    cap, tile_rows, _ = master.shape
    n_tiles = owners.shape[0]
    rows = tok_rows // 4
    homes = jnp.arange(8, dtype=jnp.int32) ^ ctx
    lane_starts = (
        ((2 * (homes % 2))[:, None] + jnp.arange(2, dtype=jnp.int32)) * 4 + (homes // 2)[:, None]
    ).reshape(-1) * 128

    owner_col = owners[:, 0]
    tile_ids = jnp.arange(n_tiles, dtype=jnp.int32)
    earlier = (owner_col[None, :] == owner_col[:, None]) & (tile_ids[None, :] < tile_ids[:, None])
    slot_in_owner = jnp.sum(earlier.astype(jnp.int32), axis=1)

    cut = lane_split(master, lane_starts)
    came = [cut[0]] + [swap(cut[k], k, 0) for k in range(1, 8)]
    home_qkv, home_out, home_gu, home_down = row_gather(
        came, owner_col ^ ctx, slot_in_owner, [12, 4, 32, 16]
    )
    pair_qkv = swap(home_qkv, 1, 0)
    pair_gu = swap(home_gu, 1, 0)

    def qkv_rows(tiles):
        split = tiles.reshape(3, 4, tile_rows, 2, 128)
        return split.transpose(3, 1, 2, 0, 4).reshape(1024, 384)

    w_qkv = jnp.concatenate([qkv_rows(home_qkv), qkv_rows(pair_qkv)])
    w_gu = jnp.concatenate(
        [
            home_gu[:16].reshape(width, 256),
            home_gu[16:].reshape(width, 256),
            pair_gu[:16].reshape(width, 256),
            pair_gu[16:].reshape(width, 256),
        ],
        axis=1,
    )
    bits = jnp.arange(8, dtype=jnp.int32)
    out_picks = z_at ^ (bits // 2)
    out_send = row_gather([home_out], jnp.zeros((8,), jnp.int32), out_picks, [1] * 8)
    w_out = lane_join(
        [out_send[0]] + [swap(out_send[k], k, 0) for k in range(1, 8)], lane_starts
    ).reshape(tile_rows, width)
    dest_x = x_at ^ (bits % 2)
    down_k = jnp.stack([2 * dest_x, 2 * dest_x + 1, 2 - 2 * dest_x, 3 - 2 * dest_x], axis=1)
    down_picks = (4 * down_k + out_picks[:, None]).reshape(-1)
    down_send = row_gather([home_down], jnp.zeros((32,), jnp.int32), down_picks, [4] * 8)
    w_down = lane_join(
        [down_send[0]] + [swap(down_send[k], k, 0) for k in range(1, 8)], lane_starts
    ).reshape(4 * tile_rows, width)

    block_z = z_at ^ jnp.arange(4, dtype=jnp.int32)
    block_w = wt ^ jnp.array([0, 2, 1, 3], jnp.int32)

    def group_positions(x_index):
        starts = (2 * block_z + x_index)[:, None] * tok_rows + block_w[None, :] * rows
        return (starts.reshape(-1)[:, None] + jnp.arange(rows, dtype=jnp.int32)).reshape(-1)

    q_pos = group_positions(x_at)
    k_pos = jnp.concatenate([q_pos, group_positions(1 - x_at)])
    doc_starts = jnp.cumsum(doc_lengths) - doc_lengths
    q_doc, k_doc = doc_index(q_pos, doc_starts), doc_index(k_pos, doc_starts)
    masks = (q_pos[:, None], q_doc[:, None], k_pos[None, :], k_doc[None, :])
    freqs = rope_base ** (-jnp.arange(HEAD_DIM // 2, dtype=F32) * (2.0 / HEAD_DIM))
    angles = q_pos.astype(F32)[:, None] * freqs[None, :]
    cosine, sine = jnp.cos(angles), jnp.sin(angles)

    def to_cut_order(values):
        cut_vals = values.reshape(-1, width // 4, 4).transpose(0, 2, 1).reshape(-1, width)
        flipped = jnp.concatenate([cut_vals[:, width // 2 :], cut_vals[:, : width // 2]], axis=1)
        return jnp.where(x_at == 0, cut_vals, flipped)

    def from_cut_order(values):
        flipped = jnp.concatenate([values[:, width // 2 :], values[:, : width // 2]], axis=1)
        cut_vals = jnp.where(x_at == 0, values, flipped)
        return cut_vals.reshape(-1, 4, width // 4).transpose(0, 2, 1).reshape(-1, width)

    inputs = lax.dynamic_slice(tokens, (wt * rows, 0), (rows, width)).astype(F32)
    out_grad_low = lax.dynamic_slice(cotangent, (wt * rows, 0), (rows, width))
    normed, norm_back = jax.vjp(layer_norm, inputs)
    normed_all = gather_rows(to_cut_order(normed.astype(LOW)))
    grad_all = gather_rows(out_grad_low)

    qkv = dot(normed_all, w_qkv)
    query = rotate(qkv[:, :128], cosine, sine).astype(LOW)
    key_here = rotate(qkv[:, 128:256], cosine, sine).astype(LOW)
    value_here = qkv[:, 256:].astype(LOW)
    key_value = jnp.concatenate([key_here, value_here], axis=1)
    key_value_there = swap(key_value, 1, 0)
    key = jnp.concatenate([key_here, key_value_there[:, :128]])
    value = jnp.concatenate([value_here, key_value_there[:, 128:]])
    att_low, lse = attend(query, key, value, *masks, 4)
    residual = inputs + scatter_sum(dot(att_low, w_out).astype(LOW))

    normed_two, norm_two_back = jax.vjp(layer_norm, residual)
    two_all = gather_rows(normed_two.astype(LOW))
    gu = dot(two_all, w_gu)
    gate = jnp.concatenate([gu[:, :256], gu[:, 512:768]], axis=1)
    up = jnp.concatenate([gu[:, 256:512], gu[:, 768:]], axis=1)
    gate_sig = jax.nn.sigmoid(gate)
    silu = gate * gate_sig
    hidden = (silu * up).astype(LOW)
    down = scatter_sum(dot(hidden, w_down).astype(LOW))
    output = share_rows((residual + down).astype(LOW), wt)

    hidden_grad = dot_nt(grad_all, w_down)
    grad_gate = (hidden_grad * up * gate_sig * (1.0 + gate * (1.0 - gate_sig))).astype(LOW)
    grad_up = (hidden_grad * silu).astype(LOW)
    grad_gu = jnp.concatenate(
        [grad_gate[:, :256], grad_up[:, :256], grad_gate[:, 256:], grad_up[:, 256:]], axis=1
    )
    two_grad = scatter_sum(dot_nt(grad_gu, w_gu).astype(LOW))
    grad_w_down = dot_tn(hidden, grad_all)
    grad_w_gu = dot_tn(two_all, grad_gu)

    resid_grad = out_grad_low.astype(F32) + norm_two_back(two_grad)[0]
    resid_all = gather_rows(resid_grad.astype(LOW))
    att_grad = dot_nt(resid_all, w_out).astype(LOW)
    grad_w_out = dot_tn(att_low, resid_all)
    query_grad, key_grad, value_grad = attend_back(query, key, value, att_grad, lse, *masks, 4)
    there = jnp.concatenate([key_grad[1024:], value_grad[1024:]], axis=1).astype(LOW)
    back = swap(there, 1, 0).astype(F32)
    key_grad = key_grad[:1024] + back[:, :128]
    value_grad = value_grad[:1024] + back[:, 128:]
    qkv_grad = jnp.concatenate(
        [rotate(query_grad, cosine, -sine), rotate(key_grad, cosine, -sine), value_grad], axis=1
    ).astype(LOW)
    grad_w_qkv = dot_tn(normed_all, qkv_grad)
    one_grad = from_cut_order(scatter_sum(dot_nt(qkv_grad, w_qkv).astype(LOW)))
    input_grad = resid_grad + norm_back(one_grad)[0]
    input_grad = share_rows(input_grad.astype(LOW), wt).astype(F32)

    gu_sum = grad_w_gu[:, :512] + swap(grad_w_gu[:, 512:].astype(LOW), 1, 0).astype(F32)
    grad_gu_tiles = [gu_sum[:, :256], gu_sum[:, 256:]]
    grad_gu_tiles = [part.astype(LOW).reshape(16, tile_rows, 256) for part in grad_gu_tiles]
    down_sum = grad_w_down[:256] + swap(grad_w_down[256:].astype(LOW), 1, 0).astype(F32)
    down_cut = lane_split(down_sum.reshape(2, tile_rows, width), lane_starts)
    grad_down_tiles = [down_cut[0]] + [swap(down_cut[k], k, 0) for k in range(1, 8)]
    out_cut = lane_split(grad_w_out.reshape(1, tile_rows, width), lane_starts)
    out_came = [out_cut[0]] + [swap(out_cut[k], k, 0) for k in range(1, 8)]
    grad_out_tiles = jnp.concatenate(
        [out_came[2 * m].astype(F32) + out_came[2 * m + 1].astype(F32) for m in range(4)]
    ).astype(LOW)
    qkv_sum = grad_w_qkv[:1024] + swap(grad_w_qkv[1024:].astype(LOW), 1, 0).astype(F32)
    qkv_sum = qkv_sum.astype(LOW).reshape(2, 4, tile_rows, 3, 128)
    grad_qkv_tiles = qkv_sum.transpose(3, 1, 2, 0, 4).reshape(12, tile_rows, 256)

    slot_range = jnp.arange(n_ctx * cap, dtype=jnp.int32)
    slot_ids = owner_col * cap + slot_in_owner
    matches = slot_ids[None, :] == slot_range[:, None]
    tile_of_slot = jnp.sum(jnp.where(matches, tile_ids[None, :], 0), axis=1)
    slot_used = jnp.any(matches, axis=1).astype(jnp.int32)
    down_tile = tile_ids - 48
    down_home = 2 * (down_tile % 4) + (down_tile // 8)
    pick_of_tile = jnp.where(
        tile_ids < 12,
        0,
        jnp.where(
            tile_ids < 16,
            1,
            jnp.where(tile_ids < 32, 2, jnp.where(tile_ids < 48, 3, 4 + (down_home ^ ctx))),
        ),
    )
    row_of_tile = jnp.where(
        tile_ids < 12,
        tile_ids,
        jnp.where(
            tile_ids < 16,
            (tile_ids - 12) ^ z_at,
            jnp.where(tile_ids < 48, tile_ids % 16, (down_tile // 4) % 2),
        ),
    )
    home_tiles = tile_of_slot.reshape(n_ctx, cap)[homes].reshape(-1)
    send = row_gather(
        [grad_qkv_tiles, grad_out_tiles] + grad_gu_tiles + grad_down_tiles,
        pick_of_tile[home_tiles],
        row_of_tile[home_tiles],
        [cap] * n_ctx,
    )
    pieces = [send[0]] + [swap(send[k], k, 0) for k in range(1, 8)]
    used_here = lax.dynamic_slice(slot_used, (ctx * cap,), (cap,))
    new_master, new_one, new_two, new_copy = update(
        master, moment_one, moment_two, pieces, lane_starts, used_here
    )
    return (output, input_grad, new_master, new_one, new_two, new_copy)


def choose_shards(*args):
    sizes = (lax.axis_size("ctx"), lax.axis_size("wt"), args[0].shape, args[4].shape[1:])
    if sizes == (8, 4, (256, 2048), (128, 2048)) and args[3].shape[0] == 64:
        return fast_shards(*args)
    return general_shards(*args)


def solution(mesh):
    placed = (
        P("ctx", None),
        P("ctx", None),
        P(),
        P(),
        P("ctx", None, "wt"),
        P("ctx", None, "wt"),
        P("ctx", None, "wt"),
    )
    return jax.shard_map(
        choose_shards,
        mesh=mesh,
        in_specs=placed,
        out_specs=(
            P("ctx", None),
            P("ctx", None),
            P("ctx", None, "wt"),
            P("ctx", None, "wt"),
            P("ctx", None, "wt"),
            P("ctx", None, "wt"),
        ),
        check_vma=False,
    )
```

```python
from functools import partial
import math

import jax
import jax.numpy as jnp
from jax import lax
from jax.experimental import pallas as pl
from jax.experimental.pallas import tpu as pltpu
from jax.sharding import PartitionSpec as P

HEAD_DIM = 128
STEP = 3


adam_beta = 0.5
learn_rate = 0.01
decay_rate = 0.1
adam_eps = 1e-08
norm_eps = 1e-05
neg_fill = -1e30
rope_base = 10000.0


def from_behind(x, axis, by):
    count = lax.axis_size(axis)
    pairs = [(i, i + by) for i in range(count) if 0 <= i + by < count]
    return lax.ppermute(x, axis, pairs)


def from_behind_2(value, axis, steps):
    count = lax.axis_size(axis)
    pairs = [(source, (source + steps) % count) for source in range(count)]
    return lax.ppermute(value, axis, pairs)


def layer_norm(values):
    center = values - jnp.mean(values, axis=-1, keepdims=True)
    spread = jnp.mean(center * center, axis=-1, keepdims=True)
    return center * lax.rsqrt(spread + norm_eps)


def rotary(values, positions):
    half_dim = values.shape[-1] // 2
    frequencies = rope_base ** (-jnp.arange(half_dim, dtype=jnp.float32) * (2.0 / values.shape[-1]))
    angles = positions.astype(jnp.float32)[:, None] * frequencies[None, :]
    cosine = jnp.cos(angles)[:, None, :]
    sine_vals = jnp.sin(angles)[:, None, :]
    first_half = values[..., :half_dim]
    second_half = values[..., half_dim:]
    return jnp.concatenate(
        [
            first_half * cosine - second_half * sine_vals,
            second_half * cosine + first_half * sine_vals,
        ],
        axis=-1,
    )


def doc_index(positions, doc_starts):
    return jnp.sum((positions[:, None] >= doc_starts[None, :]).astype(jnp.int32), axis=1) - 1


def heads_dot(spec, left, right):
    return jnp.einsum(spec, left, right, preferred_element_type=jnp.float32)


def general_shards(tokens, cotangent, doc_lengths, owners, master, moment_one, moment_two):
    n_ctx = lax.axis_size("ctx")
    n_wt = lax.axis_size("wt")
    ctx_index = lax.axis_index("ctx")
    tok_rows, width = tokens.shape
    cap_slots, tile_rows, tile_width = master.shape
    n_tiles = owners.shape[0]
    head_dim = HEAD_DIM
    owner_col = owners[:, 0]
    tile_ids = jnp.arange(n_tiles, dtype=jnp.int32)
    earlier = (owner_col[None, :] == owner_col[:, None]) & (tile_ids[None, :] < tile_ids[:, None])
    slot_ids = owner_col * cap_slots + jnp.sum(earlier.astype(jnp.int32), axis=1)
    every_slot = lax.all_gather(master.astype(jnp.bfloat16), "ctx", axis=0, tiled=True)
    flat_w = every_slot[slot_ids].reshape(-1)
    local_width = width // n_wt
    heads_local = local_width // head_dim
    part_q = width * local_width
    ff_local = (flat_w.shape[0] - 4 * part_q) // (3 * width)
    part_f = width * ff_local
    w_qkv = flat_w[: 3 * part_q].reshape(3, width, local_width)
    w_out = flat_w[3 * part_q : 4 * part_q].reshape(local_width, width)
    w_gateup = flat_w[4 * part_q : 4 * part_q + 2 * part_f].reshape(2, width, ff_local)
    w_down = flat_w[4 * part_q + 2 * part_f :].reshape(ff_local, width)
    positions = ctx_index * tok_rows + jnp.arange(tok_rows, dtype=jnp.int32)
    doc_starts = jnp.cumsum(doc_lengths) - doc_lengths
    q_docs = doc_index(positions, doc_starts)
    score_scale = 1.0 / math.sqrt(head_dim)
    inputs = tokens.astype(jnp.float32)
    normed, norm_back = jax.vjp(layer_norm, inputs)
    normed_low = normed.astype(jnp.bfloat16)
    qkv_vals = heads_dot("td,jde->jte", normed_low, w_qkv)
    shaped = qkv_vals.reshape(3, tok_rows, heads_local, head_dim)
    rope_here = partial(rotary, positions=positions)
    qk_rot, rope_back = jax.vjp(rope_here, jnp.concatenate([shaped[0], shaped[1]], axis=1))
    q_low = qk_rot[:, :heads_local].astype(jnp.bfloat16)
    k_low = qk_rot[:, heads_local:].astype(jnp.bfloat16)
    v_low = shaped[2].astype(jnp.bfloat16)

    def masked_scores(key_block, key_pos, key_docs):
        raw_scores = heads_dot("qhd,khd->hqk", q_low, key_block)
        visible_mask = (key_pos[None, :] <= positions[:, None]) & (
            key_docs[None, :] == q_docs[:, None]
        )
        return (jnp.where(visible_mask[None], raw_scores * score_scale, neg_fill), visible_mask)

    def over_blocks(kv_piece, first_row, update_fn, running):
        key_count = kv_piece[0].shape[0]
        block_len = math.gcd(key_count, 512)
        n_blocks = key_count // block_len
        split_kv = tuple(
            (member.reshape((n_blocks, block_len) + member.shape[1:]) for member in kv_piece)
        )

        def step_fn(block_state, inputs_here):
            block_idx, block_vals = inputs_here
            block_row = first_row + block_idx * block_len
            key_pos = block_row + jnp.arange(block_len, dtype=jnp.int32)
            key_docs = doc_index(key_pos, doc_starts)
            block_state = update_fn(block_state, block_vals, key_pos, key_docs, block_row)
            return (block_state, None)

        running, unused = lax.scan(
            step_fn, running, (jnp.arange(n_blocks, dtype=jnp.int32), split_kv)
        )
        return running

    def norm_update(block_state, block_vals, key_pos, key_docs, block_row):
        row_top, row_total = block_state
        scores, visible_mask = masked_scores(block_vals[0], key_pos, key_docs)
        new_top = jnp.maximum(row_top, jnp.max(scores, axis=-1))
        weights_exp = jnp.where(visible_mask[None], jnp.exp(scores - new_top[:, :, None]), 0.0)
        return (new_top, row_total * jnp.exp(row_top - new_top) + jnp.sum(weights_exp, axis=-1))

    start_top = jnp.full((heads_local, tok_rows), neg_fill, jnp.float32)
    start_total = jnp.zeros((heads_local, tok_rows), jnp.float32)
    row_top, row_total = over_blocks(
        (lax.all_gather(k_low, "ctx", axis=0, tiled=True),),
        jnp.int32(0),
        norm_update,
        (start_top, start_total),
    )
    log_sum = row_top + jnp.log(row_total)

    def block_probs(key_block, key_pos, key_docs):
        scores, visible_mask = masked_scores(key_block, key_pos, key_docs)
        return jnp.where(visible_mask[None], jnp.exp(scores - log_sum[:, :, None]), 0.0)

    def value_update(block_state, block_vals, key_pos, key_docs, block_row):
        prob_vals = block_probs(block_vals[0], key_pos, key_docs)
        return block_state + heads_dot(
            "hqk,khd->qhd", prob_vals.astype(jnp.bfloat16), block_vals[1]
        )

    zero_heads = jnp.zeros((tok_rows, heads_local, head_dim), jnp.float32)
    attended = over_blocks(
        (
            lax.all_gather(k_low, "ctx", axis=0, tiled=True),
            lax.all_gather(v_low, "ctx", axis=0, tiled=True),
        ),
        jnp.int32(0),
        value_update,
        zero_heads,
    )
    att_low = attended.reshape(tok_rows, local_width).astype(jnp.bfloat16)
    attn_part = jnp.dot(att_low, w_out, preferred_element_type=jnp.float32)
    residual = inputs + lax.psum(attn_part.astype(jnp.bfloat16), "wt").astype(jnp.float32)
    normed_two, norm_two_back = jax.vjp(layer_norm, residual)
    normed_two_low = normed_two.astype(jnp.bfloat16)
    gateup_vals = heads_dot("td,jde->jte", normed_two_low, w_gateup)
    gate_vals = gateup_vals[0]
    up_vals = gateup_vals[1]
    gate_sig = jax.nn.sigmoid(gate_vals)
    silu_vals = gate_vals * gate_sig
    hidden_low = (silu_vals * up_vals).astype(jnp.bfloat16)
    mlp_part = jnp.dot(hidden_low, w_down, preferred_element_type=jnp.float32)
    output = (residual + lax.psum(mlp_part.astype(jnp.bfloat16), "wt").astype(jnp.float32)).astype(
        jnp.bfloat16
    )
    out_grad = cotangent.astype(jnp.float32)
    grad_down = heads_dot("tf,td->fd", hidden_low, cotangent)
    grad_hidden = heads_dot("td,fd->tf", cotangent, w_down)
    grad_gate = grad_hidden * up_vals * gate_sig * (1.0 + gate_vals * (1.0 - gate_sig))
    grad_up = grad_hidden * silu_vals
    grad_gu_low = jnp.stack([grad_gate, grad_up]).astype(jnp.bfloat16)
    grad_gateup = heads_dot("td,jte->jde", normed_two_low, grad_gu_low)
    norm_two_part = heads_dot("jte,jde->td", grad_gu_low, w_gateup)
    norm_two_grad = lax.psum(norm_two_part.astype(jnp.bfloat16), "wt").astype(jnp.float32)
    resid_grad = out_grad + norm_two_back(norm_two_grad)[0]
    resid_low = resid_grad.astype(jnp.bfloat16)
    grad_out = heads_dot("tc,td->cd", att_low, resid_low)
    att_grad = heads_dot("td,cd->tc", resid_low, w_out)
    att_grad_low = att_grad.astype(jnp.bfloat16).reshape(tok_rows, heads_local, head_dim)
    row_delta = jnp.sum(att_grad_low * attended, axis=-1).T

    def grad_block(block_vals, key_pos, key_docs):
        prob_vals = block_probs(block_vals[0], key_pos, key_docs)
        value_grad = heads_dot("hqk,qhd->khd", prob_vals.astype(jnp.bfloat16), att_grad_low)
        prob_grad = heads_dot("qhd,khd->hqk", att_grad_low, block_vals[1])
        raw_grad = (prob_vals * (prob_grad - row_delta[:, :, None]) * score_scale).astype(
            jnp.bfloat16
        )
        query_grad = heads_dot("hqk,khd->qhd", raw_grad, block_vals[0])
        key_grad = heads_dot("hqk,qhd->khd", raw_grad, q_low)
        return (query_grad, key_grad, value_grad)

    def add_rows(target, addend):
        return target + addend

    def cycle_step(turn_idx, cycle_state):
        query_acc, key_cur, value_cur, key_acc, value_acc = cycle_state
        anchor = (ctx_index - turn_idx) % n_ctx

        def cycle_update(block_state, block_vals, key_pos, key_docs, block_row):
            q_acc, k_acc, v_acc = block_state
            query_grad, key_grad, value_grad = grad_block(block_vals, key_pos, key_docs)
            return (q_acc + query_grad, add_rows(k_acc, key_grad), add_rows(v_acc, value_grad))

        query_acc, key_acc, value_acc = over_blocks(
            (key_cur, value_cur), anchor * tok_rows, cycle_update, (query_acc, key_acc, value_acc)
        )
        key_cur, value_cur = from_behind((key_cur, value_cur), "ctx", 1)
        key_acc, value_acc = (
            from_behind_2(key_acc.astype(jnp.bfloat16), "ctx", 1).astype(key_acc.dtype),
            from_behind_2(value_acc.astype(jnp.bfloat16), "ctx", 1).astype(value_acc.dtype),
        )
        return (query_acc, key_cur, value_cur, key_acc, value_acc)

    cycle_start = (zero_heads, k_low, v_low, zero_heads, zero_heads)
    query_acc, key_last, value_last, key_acc, value_acc = lax.fori_loop(
        0, n_ctx, cycle_step, cycle_start
    )
    qk_pre_grad = rope_back(jnp.concatenate([query_acc, key_acc], axis=1))[0]
    qkv_grad_low = jnp.stack(
        [
            qk_pre_grad[:, :heads_local].reshape(tok_rows, local_width),
            qk_pre_grad[:, heads_local:].reshape(tok_rows, local_width),
            value_acc.reshape(tok_rows, local_width),
        ]
    ).astype(jnp.bfloat16)
    grad_qkv = heads_dot("td,jte->jde", normed_low, qkv_grad_low)
    norm_one_part = heads_dot("jte,jde->td", qkv_grad_low, w_qkv)
    norm_one_grad = lax.psum(norm_one_part.astype(jnp.bfloat16), "wt").astype(jnp.float32)
    input_grad = resid_grad + norm_back(norm_one_grad)[0]
    grad_tiles = jnp.concatenate(
        [grad_qkv.reshape(-1), grad_out.reshape(-1), grad_gateup.reshape(-1), grad_down.reshape(-1)]
    ).reshape(n_tiles, tile_rows, tile_width)
    slot_range = jnp.arange(n_ctx * cap_slots, dtype=jnp.int32)
    matches = slot_ids[None, :] == slot_range[:, None]
    tile_of_slot = jnp.sum(jnp.where(matches, tile_ids[None, :], 0), axis=1)
    slot_used = jnp.any(matches, axis=1)
    slot_grads = lax.psum_scatter(
        jnp.where(slot_used[:, None, None], grad_tiles[tile_of_slot], 0.0).astype(jnp.bfloat16),
        "ctx",
        scatter_dimension=0,
        tiled=True,
    ).astype(jnp.float32)
    new_one = adam_beta * moment_one + (1.0 - adam_beta) * slot_grads
    new_two = adam_beta * moment_two + (1.0 - adam_beta) * slot_grads * slot_grads
    bias_one = 1.0 - adam_beta**STEP
    bias_two = 1.0 - adam_beta**STEP
    step_ratio = new_one / bias_one / (jnp.sqrt(new_two / bias_two) + adam_eps)
    new_master = master - learn_rate * (step_ratio + decay_rate * master)
    return (output, input_grad, new_master, new_one, new_two, new_master.astype(jnp.bfloat16))


AXES = ("ctx", "wt")
LOW = jnp.bfloat16
F32 = jnp.float32


def swap(value, ctx_bits, wt_bits):
    n_ctx, n_wt = lax.axis_size("ctx"), lax.axis_size("wt")
    pairs = [
        (c * n_wt + w, (c ^ ctx_bits) * n_wt + (w ^ wt_bits))
        for c in range(n_ctx)
        for w in range(n_wt)
    ]
    return lax.ppermute(value, AXES, pairs)


def dot(left, right):
    return jnp.dot(left, right, preferred_element_type=F32)


def dot_tn(left, right):
    return lax.dot_general(left, right, (((0,), (0,)), ((), ())), preferred_element_type=F32)


def dot_nt(left, right):
    return lax.dot_general(left, right, (((1,), (1,)), ((), ())), preferred_element_type=F32)


def lane_split(value, lane_starts):
    count, rows, width = value.shape
    homes = lane_starts.shape[0] // 2

    def body(starts, src, *outs):
        for home in range(homes):
            for half in range(2):
                start = pl.multiple_of(starts[2 * home + half], 128)
                outs[home][0, :, half * 128 : half * 128 + 128] = src[
                    0, :, pl.ds(start, 128)
                ].astype(LOW)

    return pl.pallas_call(
        body,
        grid_spec=pltpu.PrefetchScalarGridSpec(
            num_scalar_prefetch=1,
            grid=(count,),
            in_specs=[pl.BlockSpec((1, rows, width), lambda i, s: (i, 0, 0))],
            out_specs=[pl.BlockSpec((1, rows, 256), lambda i, s: (i, 0, 0))] * homes,
        ),
        out_shape=[jax.ShapeDtypeStruct((count, rows, 256), LOW)] * homes,
        name="lane_split",
    )(lane_starts, value)


def lane_join(pieces, lane_starts):
    count, rows, _ = pieces[0].shape
    homes = len(pieces)
    width = homes * 256

    def body(starts, *refs):
        out = refs[-1]
        for home in range(homes):
            for half in range(2):
                start = pl.multiple_of(starts[2 * home + half], 128)
                out[0, :, pl.ds(start, 128)] = refs[home][0, :, half * 128 : half * 128 + 128]

    return pl.pallas_call(
        body,
        grid_spec=pltpu.PrefetchScalarGridSpec(
            num_scalar_prefetch=1,
            grid=(count,),
            in_specs=[pl.BlockSpec((1, rows, 256), lambda i, s: (i, 0, 0))] * homes,
            out_specs=pl.BlockSpec((1, rows, width), lambda i, s: (i, 0, 0)),
        ),
        out_shape=jax.ShapeDtypeStruct((count, rows, width), LOW),
        name="lane_join",
    )(lane_starts, *pieces)


def row_gather(sources, picked, rows, sizes):
    n_src = len(sources)

    def body(which, where, *refs):
        srcs, outs = refs[:n_src], refs[n_src:]
        first = 0
        for out, size in zip(outs, sizes):

            def copy(j, carry, out=out, first=first):
                t = first + j
                for n in range(n_src):

                    @pl.when(which[t] == n)
                    def _(n=n):
                        out[j] = srcs[n][where[t]]

                return carry

            lax.fori_loop(0, size, copy, 0)
            first += size

    tail = sources[0].shape[1:]
    vmem = pl.BlockSpec(memory_space=pltpu.VMEM)
    smem = pl.BlockSpec(memory_space=pltpu.SMEM)
    return pl.pallas_call(
        body,
        in_specs=[smem, smem] + [vmem] * n_src,
        out_specs=[vmem] * len(sizes),
        out_shape=[jax.ShapeDtypeStruct((size,) + tail, LOW) for size in sizes],
        name="row_gather",
    )(picked, rows, *sources)


def visible_scores(query, key, q_pos, q_doc, k_pos, k_doc):
    raw = dot_nt(query, key) * (1.0 / math.sqrt(HEAD_DIM))
    seen = (k_pos <= q_pos) & (k_doc == q_doc)
    return jnp.where(seen, raw, neg_fill)


def attend(query, key, value, q_pos, q_doc, k_pos, k_doc, n_blocks):
    rows = query.shape[0]
    block = rows // n_blocks

    def body(q, k, v, qp, qd, kp, kd, out, lse):
        scores = visible_scores(q[...], k[...], qp[...], qd[...], kp[...], kd[...])
        top = jnp.max(scores, axis=1, keepdims=True)
        weights = jnp.exp(scores - top)
        total = jnp.sum(weights, axis=1, keepdims=True)
        probs = (weights * (1.0 / total)).astype(LOW)
        out[...] = dot(probs, v[...]).astype(LOW)
        lse[...] = top + jnp.log(total)

    whole = lambda arr: pl.BlockSpec(arr.shape, lambda i: (0, 0))
    part = lambda arr: pl.BlockSpec((block, arr.shape[1]), lambda i: (i, 0))
    return pl.pallas_call(
        body,
        grid=(n_blocks,),
        in_specs=[
            part(query), whole(key), whole(value), part(q_pos), part(q_doc), whole(k_pos), whole(k_doc),
        ],
        out_specs=[
            pl.BlockSpec((block, HEAD_DIM), lambda i: (i, 0)),
            pl.BlockSpec((block, 1), lambda i: (i, 0)),
        ],
        out_shape=[
            jax.ShapeDtypeStruct((rows, HEAD_DIM), LOW),
            jax.ShapeDtypeStruct((rows, 1), F32),
        ],
        name="attend",
    )(query, key, value, q_pos, q_doc, k_pos, k_doc)


def attend_back(query, key, value, out_grad, lse, q_pos, q_doc, k_pos, k_doc, n_blocks):
    rows = query.shape[0]
    block = rows // n_blocks
    n_keys = key.shape[0]

    def body(q, k, v, do, ls, qp, qd, kp, kd, dq, dk, dv):
        @pl.when(pl.program_id(0) == 0)
        def _():
            dk[...] = jnp.zeros_like(dk)
            dv[...] = jnp.zeros_like(dv)

        scores = visible_scores(q[...], k[...], qp[...], qd[...], kp[...], kd[...])
        probs = jnp.exp(scores - ls[...])
        prob_grad = dot_nt(do[...], v[...])
        delta = jnp.sum(probs * prob_grad, axis=1, keepdims=True)
        score_grad = (probs * (prob_grad - delta) * (1.0 / math.sqrt(HEAD_DIM))).astype(LOW)
        dq[...] = dot(score_grad, k[...])
        dk[...] += dot_tn(score_grad, q[...])
        dv[...] += dot_tn(probs.astype(LOW), do[...])

    whole = lambda arr: pl.BlockSpec(arr.shape, lambda i: (0, 0))
    part = lambda arr: pl.BlockSpec((block, arr.shape[1]), lambda i: (i, 0))
    kept = pl.BlockSpec((n_keys, HEAD_DIM), lambda i: (0, 0))
    return pl.pallas_call(
        body,
        grid=(n_blocks,),
        in_specs=[
            part(query), whole(key), whole(value), part(out_grad), part(lse),
            part(q_pos), part(q_doc), whole(k_pos), whole(k_doc),
        ],
        out_specs=[pl.BlockSpec((block, HEAD_DIM), lambda i: (i, 0)), kept, kept],
        out_shape=[
            jax.ShapeDtypeStruct((rows, HEAD_DIM), F32),
            jax.ShapeDtypeStruct((n_keys, HEAD_DIM), F32),
            jax.ShapeDtypeStruct((n_keys, HEAD_DIM), F32),
        ],
        name="attend_back",
    )(query, key, value, out_grad, lse, q_pos, q_doc, k_pos, k_doc)


def update(master, moment_one, moment_two, pieces, lane_starts, used):
    count, rows, width = master.shape
    homes = len(pieces)
    bias = 1.0 - adam_beta**STEP

    def body(starts, live, mas, one, two, *refs):
        grads, (new_mas, new_one, new_two, copy) = refs[:homes], refs[homes:]
        alive = live[pl.program_id(0)] > 0
        for home in range(homes):
            for half in range(2):
                at = (0, slice(None), pl.ds(pl.multiple_of(starts[2 * home + half], 128), 128))
                grad = grads[home][0, :, half * 128 : half * 128 + 128].astype(F32)
                grad = jnp.where(alive, grad, 0.0)
                first = adam_beta * one[at] + (1.0 - adam_beta) * grad
                second = adam_beta * two[at] + (1.0 - adam_beta) * grad * grad
                ratio = (first * (1.0 / bias)) / (jnp.sqrt(second * (1.0 / bias)) + adam_eps)
                old = mas[at]
                new = old - learn_rate * (ratio + decay_rate * old)
                new_mas[at] = new
                new_one[at] = first
                new_two[at] = second
                copy[at] = new.astype(LOW)

    slot = pl.BlockSpec((1, rows, width), lambda i, s, u: (i, 0, 0))
    piece = pl.BlockSpec((1, rows, 256), lambda i, s, u: (i, 0, 0))
    return pl.pallas_call(
        body,
        grid_spec=pltpu.PrefetchScalarGridSpec(
            num_scalar_prefetch=2,
            grid=(count,),
            in_specs=[slot] * 3 + [piece] * homes,
            out_specs=[slot] * 4,
        ),
        out_shape=[jax.ShapeDtypeStruct(master.shape, F32)] * 3
        + [jax.ShapeDtypeStruct(master.shape, LOW)],
        name="update",
    )(lane_starts, used, master, moment_one, moment_two, *pieces)


def gather_rows(piece):
    near = [piece] + [swap(piece, 2 * k, 0) for k in (1, 2, 3)]
    blocks = []
    for part in near:
        pair = jnp.concatenate([part, swap(part, 0, 2)])
        blocks += [pair, swap(pair, 0, 1)]
    return jnp.concatenate(blocks)


def scatter_sum(partial_sum):
    quarter = partial_sum.shape[0] // 4
    half, rows = quarter // 2, quarter // 4
    kept = [None] * 4
    for k in (3, 2, 1, 0):
        chunk = partial_sum[quarter * k : quarter * (k + 1)]
        other = swap(chunk[half:].astype(LOW), 0, 1)
        pair = chunk[:half].astype(F32) + other.astype(F32)
        other = swap(pair[rows:].astype(LOW), 0, 2)
        kept[k] = pair[:rows] + other.astype(F32)
    total = kept[0]
    for k in (1, 2, 3):
        total = total + swap(kept[k].astype(LOW), 2 * k, 0).astype(F32)
    return total


def share_rows(piece, wt_index):
    rows = piece.shape[0]
    out = jnp.zeros((4 * rows,) + piece.shape[1:], piece.dtype)
    over_y = swap(piece, 0, 2)
    for bits, part in ((0, piece), (2, over_y), (1, swap(piece, 0, 1)), (3, swap(over_y, 0, 1))):
        out = lax.dynamic_update_slice(out, part, ((wt_index ^ bits) * rows, 0))
    return out


def rotate(values, cosine, sine):
    half = values.shape[-1] // 2
    first, second = values[:, :half], values[:, half:]
    return jnp.concatenate([first * cosine - second * sine, second * cosine + first * sine], axis=1)


def fast_shards(tokens, cotangent, doc_lengths, owners, master, moment_one, moment_two):
    ctx, wt = lax.axis_index("ctx"), lax.axis_index("wt")
    n_ctx = lax.axis_size("ctx")
    z_at, x_at = ctx // 2, ctx % 2
    tok_rows, width = tokens.shape
    cap, tile_rows, _ = master.shape
    n_tiles = owners.shape[0]
    rows = tok_rows // 4
    homes = jnp.arange(8, dtype=jnp.int32) ^ ctx
    lane_starts = (
        ((2 * (homes % 2))[:, None] + jnp.arange(2, dtype=jnp.int32)) * 4 + (homes // 2)[:, None]
    ).reshape(-1) * 128

    owner_col = owners[:, 0]
    tile_ids = jnp.arange(n_tiles, dtype=jnp.int32)
    earlier = (owner_col[None, :] == owner_col[:, None]) & (tile_ids[None, :] < tile_ids[:, None])
    slot_in_owner = jnp.sum(earlier.astype(jnp.int32), axis=1)

    cut = lane_split(master, lane_starts)
    came = [cut[0]] + [swap(cut[k], k, 0) for k in range(1, 8)]
    bits = jnp.arange(8, dtype=jnp.int32)
    dest_z, dest_x = z_at ^ (bits // 2), x_at ^ (bits % 2)
    down_k = jnp.stack([2 * dest_x, 2 * dest_x + 1, 2 - 2 * dest_x, 3 - 2 * dest_x], axis=1)
    wanted = jnp.concatenate(
        [
            jnp.arange(12, dtype=jnp.int32),
            jnp.arange(16, 48, dtype=jnp.int32),
            12 + dest_z[::2],
            (48 + 4 * down_k + dest_z[:, None]).reshape(-1),
        ]
    )
    home_qkv, home_gu, *sends = row_gather(
        came, (owner_col ^ ctx)[wanted], slot_in_owner[wanted], [12, 32] + [1] * 4 + [4] * 8
    )
    out_send, down_send = sends[:4], sends[4:]
    pair_qkv = swap(home_qkv, 1, 0)
    pair_gu = swap(home_gu, 1, 0)

    def qkv_rows(tiles):
        split = tiles.reshape(3, 4, tile_rows, 2, 128)
        return split.transpose(3, 1, 2, 0, 4).reshape(1024, 384)

    w_qkv = jnp.concatenate([qkv_rows(home_qkv), qkv_rows(pair_qkv)])
    w_gu = jnp.concatenate(
        [
            home_gu[:16].reshape(width, 256),
            home_gu[16:].reshape(width, 256),
            pair_gu[:16].reshape(width, 256),
            pair_gu[16:].reshape(width, 256),
        ],
        axis=1,
    )
    w_out = lane_join(
        [out_send[0]] + [swap(out_send[k // 2], k, 0) for k in range(1, 8)], lane_starts
    ).reshape(tile_rows, width)
    w_down = lane_join(
        [down_send[0]] + [swap(down_send[k], k, 0) for k in range(1, 8)], lane_starts
    ).reshape(4 * tile_rows, width)

    block_z = z_at ^ jnp.arange(4, dtype=jnp.int32)
    block_w = wt ^ jnp.array([0, 2, 1, 3], jnp.int32)

    def group_positions(x_index):
        starts = (2 * block_z + x_index)[:, None] * tok_rows + block_w[None, :] * rows
        return (starts.reshape(-1)[:, None] + jnp.arange(rows, dtype=jnp.int32)).reshape(-1)

    q_pos = group_positions(x_at)
    k_pos = jnp.concatenate([q_pos, group_positions(1 - x_at)])
    doc_starts = jnp.cumsum(doc_lengths) - doc_lengths
    q_doc, k_doc = doc_index(q_pos, doc_starts), doc_index(k_pos, doc_starts)
    masks = (q_pos[:, None], q_doc[:, None], k_pos[None, :], k_doc[None, :])
    freqs = rope_base ** (-jnp.arange(HEAD_DIM // 2, dtype=F32) * (2.0 / HEAD_DIM))
    angles = q_pos.astype(F32)[:, None] * freqs[None, :]
    cosine, sine = jnp.cos(angles), jnp.sin(angles)

    def to_cut_order(values):
        cut_vals = values.reshape(-1, width // 4, 4).transpose(0, 2, 1).reshape(-1, width)
        flipped = jnp.concatenate([cut_vals[:, width // 2 :], cut_vals[:, : width // 2]], axis=1)
        return jnp.where(x_at == 0, cut_vals, flipped)

    def from_cut_order(values):
        flipped = jnp.concatenate([values[:, width // 2 :], values[:, : width // 2]], axis=1)
        cut_vals = jnp.where(x_at == 0, values, flipped)
        return cut_vals.reshape(-1, 4, width // 4).transpose(0, 2, 1).reshape(-1, width)

    inputs = lax.dynamic_slice(tokens, (wt * rows, 0), (rows, width)).astype(F32)
    out_grad_low = lax.dynamic_slice(cotangent, (wt * rows, 0), (rows, width))
    normed, norm_back = jax.vjp(layer_norm, inputs)
    normed_all = gather_rows(to_cut_order(normed.astype(LOW)))
    grad_all = gather_rows(out_grad_low)

    qkv = dot(normed_all, w_qkv)
    query = rotate(qkv[:, :128], cosine, sine).astype(LOW)
    key_here = rotate(qkv[:, 128:256], cosine, sine).astype(LOW)
    value_here = qkv[:, 256:].astype(LOW)
    key_value = jnp.concatenate([key_here, value_here], axis=1)
    key_value_there = swap(key_value, 1, 0)
    key = jnp.concatenate([key_here, key_value_there[:, :128]])
    value = jnp.concatenate([value_here, key_value_there[:, 128:]])
    att_low, lse = attend(query, key, value, *masks, 4)
    residual = inputs + scatter_sum(dot(att_low, w_out).astype(LOW))

    normed_two, norm_two_back = jax.vjp(layer_norm, residual)
    two_all = gather_rows(normed_two.astype(LOW))
    gu = dot(two_all, w_gu)
    gate = jnp.concatenate([gu[:, :256], gu[:, 512:768]], axis=1)
    up = jnp.concatenate([gu[:, 256:512], gu[:, 768:]], axis=1)
    gate_sig = jax.nn.sigmoid(gate)
    silu = gate * gate_sig
    hidden = (silu * up).astype(LOW)
    down = scatter_sum(dot(hidden, w_down).astype(LOW))
    output = share_rows((residual + down).astype(LOW), wt)

    hidden_grad = dot_nt(grad_all, w_down)
    grad_gate = (hidden_grad * up * gate_sig * (1.0 + gate * (1.0 - gate_sig))).astype(LOW)
    grad_up = (hidden_grad * silu).astype(LOW)
    grad_gu = jnp.concatenate(
        [grad_gate[:, :256], grad_up[:, :256], grad_gate[:, 256:], grad_up[:, 256:]], axis=1
    )
    two_grad = scatter_sum(dot_nt(grad_gu, w_gu).astype(LOW))
    grad_w_down = dot_tn(hidden, grad_all)
    grad_w_gu = dot_tn(two_all, grad_gu)

    resid_grad = out_grad_low.astype(F32) + norm_two_back(two_grad)[0]
    resid_all = gather_rows(resid_grad.astype(LOW))
    att_grad = dot_nt(resid_all, w_out).astype(LOW)
    grad_w_out = dot_tn(att_low, resid_all)
    query_grad, key_grad, value_grad = attend_back(query, key, value, att_grad, lse, *masks, 4)
    there = jnp.concatenate([key_grad[1024:], value_grad[1024:]], axis=1).astype(LOW)
    back = swap(there, 1, 0).astype(F32)
    key_grad = key_grad[:1024] + back[:, :128]
    value_grad = value_grad[:1024] + back[:, 128:]
    qkv_grad = jnp.concatenate(
        [rotate(query_grad, cosine, -sine), rotate(key_grad, cosine, -sine), value_grad], axis=1
    ).astype(LOW)
    grad_w_qkv = dot_tn(normed_all, qkv_grad)
    one_grad = from_cut_order(scatter_sum(dot_nt(qkv_grad, w_qkv).astype(LOW)))
    input_grad = resid_grad + norm_back(one_grad)[0]
    input_grad = share_rows(input_grad.astype(LOW), wt).astype(F32)

    gu_sum = grad_w_gu[:, :512] + swap(grad_w_gu[:, 512:].astype(LOW), 1, 0).astype(F32)
    grad_gu_tiles = [gu_sum[:, :256], gu_sum[:, 256:]]
    grad_gu_tiles = [part.astype(LOW).reshape(16, tile_rows, 256) for part in grad_gu_tiles]
    down_sum = grad_w_down[:256] + swap(grad_w_down[256:].astype(LOW), 1, 0).astype(F32)
    down_cut = lane_split(down_sum.reshape(2, tile_rows, width), lane_starts)
    grad_down_tiles = [down_cut[0]] + [swap(down_cut[k], k, 0) for k in range(1, 8)]
    out_cut = lane_split(grad_w_out.reshape(1, tile_rows, width), lane_starts)
    out_came = [out_cut[0]] + [swap(out_cut[k], k, 0) for k in range(1, 8)]
    grad_out_tiles = jnp.concatenate(
        [out_came[2 * m].astype(F32) + out_came[2 * m + 1].astype(F32) for m in range(4)]
    ).astype(LOW)
    qkv_sum = grad_w_qkv[:1024] + swap(grad_w_qkv[1024:].astype(LOW), 1, 0).astype(F32)
    qkv_sum = qkv_sum.astype(LOW).reshape(2, 4, tile_rows, 3, 128)
    grad_qkv_tiles = qkv_sum.transpose(3, 1, 2, 0, 4).reshape(12, tile_rows, 256)

    slot_range = jnp.arange(n_ctx * cap, dtype=jnp.int32)
    slot_ids = owner_col * cap + slot_in_owner
    matches = slot_ids[None, :] == slot_range[:, None]
    tile_of_slot = jnp.sum(jnp.where(matches, tile_ids[None, :], 0), axis=1)
    slot_used = jnp.any(matches, axis=1).astype(jnp.int32)
    down_tile = tile_ids - 48
    down_home = 2 * (down_tile % 4) + (down_tile // 8)
    pick_of_tile = jnp.where(
        tile_ids < 12,
        0,
        jnp.where(
            tile_ids < 16,
            1,
            jnp.where(tile_ids < 32, 2, jnp.where(tile_ids < 48, 3, 4 + (down_home ^ ctx))),
        ),
    )
    row_of_tile = jnp.where(
        tile_ids < 12,
        tile_ids,
        jnp.where(
            tile_ids < 16,
            (tile_ids - 12) ^ z_at,
            jnp.where(tile_ids < 48, tile_ids % 16, (down_tile // 4) % 2),
        ),
    )
    home_tiles = tile_of_slot.reshape(n_ctx, cap)[homes].reshape(-1)
    send = row_gather(
        [grad_qkv_tiles, grad_out_tiles] + grad_gu_tiles + grad_down_tiles,
        pick_of_tile[home_tiles],
        row_of_tile[home_tiles],
        [cap] * n_ctx,
    )
    pieces = [send[0]] + [swap(send[k], k, 0) for k in range(1, 8)]
    used_here = lax.dynamic_slice(slot_used, (ctx * cap,), (cap,))
    new_master, new_one, new_two, new_copy = update(
        master, moment_one, moment_two, pieces, lane_starts, used_here
    )
    return (output, input_grad, new_master, new_one, new_two, new_copy)


def choose_shards(*args):
    sizes = (lax.axis_size("ctx"), lax.axis_size("wt"), args[0].shape, args[4].shape[1:])
    if sizes == (8, 4, (256, 2048), (128, 2048)) and args[3].shape[0] == 64:
        return fast_shards(*args)
    return general_shards(*args)


def solution(mesh):
    placed = (
        P("ctx", None),
        P("ctx", None),
        P(),
        P(),
        P("ctx", None, "wt"),
        P("ctx", None, "wt"),
        P("ctx", None, "wt"),
    )
    return jax.shard_map(
        choose_shards,
        mesh=mesh,
        in_specs=placed,
        out_specs=(
            P("ctx", None),
            P("ctx", None),
            P("ctx", None, "wt"),
            P("ctx", None, "wt"),
            P("ctx", None, "wt"),
            P("ctx", None, "wt"),
        ),
        check_vma=False,
    )
```

```python
from functools import partial
import math

import jax
import jax.numpy as jnp
from jax import lax
from jax.experimental import pallas as pl
from jax.experimental.pallas import tpu as pltpu
from jax.sharding import PartitionSpec as P

HEAD_DIM = 128
STEP = 3


adam_beta = 0.5
learn_rate = 0.01
decay_rate = 0.1
adam_eps = 1e-08
norm_eps = 1e-05
neg_fill = -1e30
rope_base = 10000.0


def from_behind(x, axis, by):
    count = lax.axis_size(axis)
    pairs = [(i, i + by) for i in range(count) if 0 <= i + by < count]
    return lax.ppermute(x, axis, pairs)


def from_behind_2(value, axis, steps):
    count = lax.axis_size(axis)
    pairs = [(source, (source + steps) % count) for source in range(count)]
    return lax.ppermute(value, axis, pairs)


def layer_norm(values):
    center = values - jnp.mean(values, axis=-1, keepdims=True)
    spread = jnp.mean(center * center, axis=-1, keepdims=True)
    return center * lax.rsqrt(spread + norm_eps)


def rotary(values, positions):
    half_dim = values.shape[-1] // 2
    frequencies = rope_base ** (-jnp.arange(half_dim, dtype=jnp.float32) * (2.0 / values.shape[-1]))
    angles = positions.astype(jnp.float32)[:, None] * frequencies[None, :]
    cosine = jnp.cos(angles)[:, None, :]
    sine_vals = jnp.sin(angles)[:, None, :]
    first_half = values[..., :half_dim]
    second_half = values[..., half_dim:]
    return jnp.concatenate(
        [
            first_half * cosine - second_half * sine_vals,
            second_half * cosine + first_half * sine_vals,
        ],
        axis=-1,
    )


def doc_index(positions, doc_starts):
    return jnp.sum((positions[:, None] >= doc_starts[None, :]).astype(jnp.int32), axis=1) - 1


def heads_dot(spec, left, right):
    return jnp.einsum(spec, left, right, preferred_element_type=jnp.float32)


def general_shards(tokens, cotangent, doc_lengths, owners, master, moment_one, moment_two):
    n_ctx = lax.axis_size("ctx")
    n_wt = lax.axis_size("wt")
    ctx_index = lax.axis_index("ctx")
    tok_rows, width = tokens.shape
    cap_slots, tile_rows, tile_width = master.shape
    n_tiles = owners.shape[0]
    head_dim = HEAD_DIM
    owner_col = owners[:, 0]
    tile_ids = jnp.arange(n_tiles, dtype=jnp.int32)
    earlier = (owner_col[None, :] == owner_col[:, None]) & (tile_ids[None, :] < tile_ids[:, None])
    slot_ids = owner_col * cap_slots + jnp.sum(earlier.astype(jnp.int32), axis=1)
    every_slot = lax.all_gather(master.astype(jnp.bfloat16), "ctx", axis=0, tiled=True)
    flat_w = every_slot[slot_ids].reshape(-1)
    local_width = width // n_wt
    heads_local = local_width // head_dim
    part_q = width * local_width
    ff_local = (flat_w.shape[0] - 4 * part_q) // (3 * width)
    part_f = width * ff_local
    w_qkv = flat_w[: 3 * part_q].reshape(3, width, local_width)
    w_out = flat_w[3 * part_q : 4 * part_q].reshape(local_width, width)
    w_gateup = flat_w[4 * part_q : 4 * part_q + 2 * part_f].reshape(2, width, ff_local)
    w_down = flat_w[4 * part_q + 2 * part_f :].reshape(ff_local, width)
    positions = ctx_index * tok_rows + jnp.arange(tok_rows, dtype=jnp.int32)
    doc_starts = jnp.cumsum(doc_lengths) - doc_lengths
    q_docs = doc_index(positions, doc_starts)
    score_scale = 1.0 / math.sqrt(head_dim)
    inputs = tokens.astype(jnp.float32)
    normed, norm_back = jax.vjp(layer_norm, inputs)
    normed_low = normed.astype(jnp.bfloat16)
    qkv_vals = heads_dot("td,jde->jte", normed_low, w_qkv)
    shaped = qkv_vals.reshape(3, tok_rows, heads_local, head_dim)
    rope_here = partial(rotary, positions=positions)
    qk_rot, rope_back = jax.vjp(rope_here, jnp.concatenate([shaped[0], shaped[1]], axis=1))
    q_low = qk_rot[:, :heads_local].astype(jnp.bfloat16)
    k_low = qk_rot[:, heads_local:].astype(jnp.bfloat16)
    v_low = shaped[2].astype(jnp.bfloat16)

    def masked_scores(key_block, key_pos, key_docs):
        raw_scores = heads_dot("qhd,khd->hqk", q_low, key_block)
        visible_mask = (key_pos[None, :] <= positions[:, None]) & (
            key_docs[None, :] == q_docs[:, None]
        )
        return (jnp.where(visible_mask[None], raw_scores * score_scale, neg_fill), visible_mask)

    def over_blocks(kv_piece, first_row, update_fn, running):
        key_count = kv_piece[0].shape[0]
        block_len = math.gcd(key_count, 512)
        n_blocks = key_count // block_len
        split_kv = tuple(
            (member.reshape((n_blocks, block_len) + member.shape[1:]) for member in kv_piece)
        )

        def step_fn(block_state, inputs_here):
            block_idx, block_vals = inputs_here
            block_row = first_row + block_idx * block_len
            key_pos = block_row + jnp.arange(block_len, dtype=jnp.int32)
            key_docs = doc_index(key_pos, doc_starts)
            block_state = update_fn(block_state, block_vals, key_pos, key_docs, block_row)
            return (block_state, None)

        running, unused = lax.scan(
            step_fn, running, (jnp.arange(n_blocks, dtype=jnp.int32), split_kv)
        )
        return running

    def norm_update(block_state, block_vals, key_pos, key_docs, block_row):
        row_top, row_total = block_state
        scores, visible_mask = masked_scores(block_vals[0], key_pos, key_docs)
        new_top = jnp.maximum(row_top, jnp.max(scores, axis=-1))
        weights_exp = jnp.where(visible_mask[None], jnp.exp(scores - new_top[:, :, None]), 0.0)
        return (new_top, row_total * jnp.exp(row_top - new_top) + jnp.sum(weights_exp, axis=-1))

    start_top = jnp.full((heads_local, tok_rows), neg_fill, jnp.float32)
    start_total = jnp.zeros((heads_local, tok_rows), jnp.float32)
    row_top, row_total = over_blocks(
        (lax.all_gather(k_low, "ctx", axis=0, tiled=True),),
        jnp.int32(0),
        norm_update,
        (start_top, start_total),
    )
    log_sum = row_top + jnp.log(row_total)

    def block_probs(key_block, key_pos, key_docs):
        scores, visible_mask = masked_scores(key_block, key_pos, key_docs)
        return jnp.where(visible_mask[None], jnp.exp(scores - log_sum[:, :, None]), 0.0)

    def value_update(block_state, block_vals, key_pos, key_docs, block_row):
        prob_vals = block_probs(block_vals[0], key_pos, key_docs)
        return block_state + heads_dot(
            "hqk,khd->qhd", prob_vals.astype(jnp.bfloat16), block_vals[1]
        )

    zero_heads = jnp.zeros((tok_rows, heads_local, head_dim), jnp.float32)
    attended = over_blocks(
        (
            lax.all_gather(k_low, "ctx", axis=0, tiled=True),
            lax.all_gather(v_low, "ctx", axis=0, tiled=True),
        ),
        jnp.int32(0),
        value_update,
        zero_heads,
    )
    att_low = attended.reshape(tok_rows, local_width).astype(jnp.bfloat16)
    attn_part = jnp.dot(att_low, w_out, preferred_element_type=jnp.float32)
    residual = inputs + lax.psum(attn_part.astype(jnp.bfloat16), "wt").astype(jnp.float32)
    normed_two, norm_two_back = jax.vjp(layer_norm, residual)
    normed_two_low = normed_two.astype(jnp.bfloat16)
    gateup_vals = heads_dot("td,jde->jte", normed_two_low, w_gateup)
    gate_vals = gateup_vals[0]
    up_vals = gateup_vals[1]
    gate_sig = jax.nn.sigmoid(gate_vals)
    silu_vals = gate_vals * gate_sig
    hidden_low = (silu_vals * up_vals).astype(jnp.bfloat16)
    mlp_part = jnp.dot(hidden_low, w_down, preferred_element_type=jnp.float32)
    output = (residual + lax.psum(mlp_part.astype(jnp.bfloat16), "wt").astype(jnp.float32)).astype(
        jnp.bfloat16
    )
    out_grad = cotangent.astype(jnp.float32)
    grad_down = heads_dot("tf,td->fd", hidden_low, cotangent)
    grad_hidden = heads_dot("td,fd->tf", cotangent, w_down)
    grad_gate = grad_hidden * up_vals * gate_sig * (1.0 + gate_vals * (1.0 - gate_sig))
    grad_up = grad_hidden * silu_vals
    grad_gu_low = jnp.stack([grad_gate, grad_up]).astype(jnp.bfloat16)
    grad_gateup = heads_dot("td,jte->jde", normed_two_low, grad_gu_low)
    norm_two_part = heads_dot("jte,jde->td", grad_gu_low, w_gateup)
    norm_two_grad = lax.psum(norm_two_part.astype(jnp.bfloat16), "wt").astype(jnp.float32)
    resid_grad = out_grad + norm_two_back(norm_two_grad)[0]
    resid_low = resid_grad.astype(jnp.bfloat16)
    grad_out = heads_dot("tc,td->cd", att_low, resid_low)
    att_grad = heads_dot("td,cd->tc", resid_low, w_out)
    att_grad_low = att_grad.astype(jnp.bfloat16).reshape(tok_rows, heads_local, head_dim)
    row_delta = jnp.sum(att_grad_low * attended, axis=-1).T

    def grad_block(block_vals, key_pos, key_docs):
        prob_vals = block_probs(block_vals[0], key_pos, key_docs)
        value_grad = heads_dot("hqk,qhd->khd", prob_vals.astype(jnp.bfloat16), att_grad_low)
        prob_grad = heads_dot("qhd,khd->hqk", att_grad_low, block_vals[1])
        raw_grad = (prob_vals * (prob_grad - row_delta[:, :, None]) * score_scale).astype(
            jnp.bfloat16
        )
        query_grad = heads_dot("hqk,khd->qhd", raw_grad, block_vals[0])
        key_grad = heads_dot("hqk,qhd->khd", raw_grad, q_low)
        return (query_grad, key_grad, value_grad)

    def add_rows(target, addend):
        return target + addend

    def cycle_step(turn_idx, cycle_state):
        query_acc, key_cur, value_cur, key_acc, value_acc = cycle_state
        anchor = (ctx_index - turn_idx) % n_ctx

        def cycle_update(block_state, block_vals, key_pos, key_docs, block_row):
            q_acc, k_acc, v_acc = block_state
            query_grad, key_grad, value_grad = grad_block(block_vals, key_pos, key_docs)
            return (q_acc + query_grad, add_rows(k_acc, key_grad), add_rows(v_acc, value_grad))

        query_acc, key_acc, value_acc = over_blocks(
            (key_cur, value_cur), anchor * tok_rows, cycle_update, (query_acc, key_acc, value_acc)
        )
        key_cur, value_cur = from_behind((key_cur, value_cur), "ctx", 1)
        key_acc, value_acc = (
            from_behind_2(key_acc.astype(jnp.bfloat16), "ctx", 1).astype(key_acc.dtype),
            from_behind_2(value_acc.astype(jnp.bfloat16), "ctx", 1).astype(value_acc.dtype),
        )
        return (query_acc, key_cur, value_cur, key_acc, value_acc)

    cycle_start = (zero_heads, k_low, v_low, zero_heads, zero_heads)
    query_acc, key_last, value_last, key_acc, value_acc = lax.fori_loop(
        0, n_ctx, cycle_step, cycle_start
    )
    qk_pre_grad = rope_back(jnp.concatenate([query_acc, key_acc], axis=1))[0]
    qkv_grad_low = jnp.stack(
        [
            qk_pre_grad[:, :heads_local].reshape(tok_rows, local_width),
            qk_pre_grad[:, heads_local:].reshape(tok_rows, local_width),
            value_acc.reshape(tok_rows, local_width),
        ]
    ).astype(jnp.bfloat16)
    grad_qkv = heads_dot("td,jte->jde", normed_low, qkv_grad_low)
    norm_one_part = heads_dot("jte,jde->td", qkv_grad_low, w_qkv)
    norm_one_grad = lax.psum(norm_one_part.astype(jnp.bfloat16), "wt").astype(jnp.float32)
    input_grad = resid_grad + norm_back(norm_one_grad)[0]
    grad_tiles = jnp.concatenate(
        [grad_qkv.reshape(-1), grad_out.reshape(-1), grad_gateup.reshape(-1), grad_down.reshape(-1)]
    ).reshape(n_tiles, tile_rows, tile_width)
    slot_range = jnp.arange(n_ctx * cap_slots, dtype=jnp.int32)
    matches = slot_ids[None, :] == slot_range[:, None]
    tile_of_slot = jnp.sum(jnp.where(matches, tile_ids[None, :], 0), axis=1)
    slot_used = jnp.any(matches, axis=1)
    slot_grads = lax.psum_scatter(
        jnp.where(slot_used[:, None, None], grad_tiles[tile_of_slot], 0.0).astype(jnp.bfloat16),
        "ctx",
        scatter_dimension=0,
        tiled=True,
    ).astype(jnp.float32)
    new_one = adam_beta * moment_one + (1.0 - adam_beta) * slot_grads
    new_two = adam_beta * moment_two + (1.0 - adam_beta) * slot_grads * slot_grads
    bias_one = 1.0 - adam_beta**STEP
    bias_two = 1.0 - adam_beta**STEP
    step_ratio = new_one / bias_one / (jnp.sqrt(new_two / bias_two) + adam_eps)
    new_master = master - learn_rate * (step_ratio + decay_rate * master)
    return (output, input_grad, new_master, new_one, new_two, new_master.astype(jnp.bfloat16))


AXES = ("ctx", "wt")
LOW = jnp.bfloat16
F32 = jnp.float32


def swap(value, ctx_bits, wt_bits):
    n_ctx, n_wt = lax.axis_size("ctx"), lax.axis_size("wt")
    pairs = [
        (c * n_wt + w, (c ^ ctx_bits) * n_wt + (w ^ wt_bits))
        for c in range(n_ctx)
        for w in range(n_wt)
    ]
    return lax.ppermute(value, AXES, pairs)


def dot(left, right):
    return jnp.dot(left, right, preferred_element_type=F32)


def dot_tn(left, right):
    return lax.dot_general(left, right, (((0,), (0,)), ((), ())), preferred_element_type=F32)


def dot_nt(left, right):
    return lax.dot_general(left, right, (((1,), (1,)), ((), ())), preferred_element_type=F32)


def lane_split(value, lane_starts):
    count, rows, width = value.shape
    homes = lane_starts.shape[0] // 2

    def body(starts, src, *outs):
        for home in range(homes):
            for half in range(2):
                start = pl.multiple_of(starts[2 * home + half], 128)
                outs[home][0, :, half * 128 : half * 128 + 128] = src[
                    0, :, pl.ds(start, 128)
                ].astype(LOW)

    return pl.pallas_call(
        body,
        grid_spec=pltpu.PrefetchScalarGridSpec(
            num_scalar_prefetch=1,
            grid=(count,),
            in_specs=[pl.BlockSpec((1, rows, width), lambda i, s: (i, 0, 0))],
            out_specs=[pl.BlockSpec((1, rows, 256), lambda i, s: (i, 0, 0))] * homes,
        ),
        out_shape=[jax.ShapeDtypeStruct((count, rows, 256), LOW)] * homes,
        name="lane_split",
    )(lane_starts, value)


def lane_join(own, other, lane_starts):
    homes, count, rows, _ = own.shape
    width = homes * 512

    def body(starts, own_ref, other_ref, out):
        for home in range(homes):
            for side, ref in ((0, own_ref), (1, other_ref)):
                for half in range(2):
                    start = pl.multiple_of(starts[4 * home + 2 * side + half], 128)
                    out[0, :, pl.ds(start, 128)] = ref[home, 0, :, half * 128 : half * 128 + 128]

    return pl.pallas_call(
        body,
        grid_spec=pltpu.PrefetchScalarGridSpec(
            num_scalar_prefetch=1,
            grid=(count,),
            in_specs=[
                pl.BlockSpec((homes, 1, rows, 256), lambda i, s: (0, i, 0, 0)),
                pl.BlockSpec(
                    (homes, 1, rows, 256), lambda i, s: (0, (i + count // 2) % count, 0, 0)
                ),
            ],
            out_specs=pl.BlockSpec((1, rows, width), lambda i, s: (i, 0, 0)),
        ),
        out_shape=jax.ShapeDtypeStruct((count, rows, width), LOW),
        name="lane_join",
    )(lane_starts, own, other)


def lane_halves(value, lane_starts):
    count, rows, width = value.shape
    homes = width // 512

    def body(starts, src, own_ref, other_ref):
        for home in range(homes):
            for side, ref in ((0, own_ref), (1, other_ref)):
                for half in range(2):
                    start = pl.multiple_of(starts[4 * home + 2 * side + half], 128)
                    ref[home, 0, :, half * 128 : half * 128 + 128] = src[
                        0, :, pl.ds(start, 128)
                    ].astype(ref.dtype)

    return pl.pallas_call(
        body,
        grid_spec=pltpu.PrefetchScalarGridSpec(
            num_scalar_prefetch=1,
            grid=(count,),
            in_specs=[pl.BlockSpec((1, rows, width), lambda i, s: (i, 0, 0))],
            out_specs=[
                pl.BlockSpec((homes, 1, rows, 256), lambda i, s: (0, i, 0, 0)),
                pl.BlockSpec(
                    (homes, 1, rows, 256), lambda i, s: (0, (i + count // 2) % count, 0, 0)
                ),
            ],
        ),
        out_shape=[
            jax.ShapeDtypeStruct((homes, count, rows, 256), dtype) for dtype in (F32, LOW)
        ],
        name="lane_halves",
    )(lane_starts, value)


def return_halves(grad, lane_starts):
    own, other = lane_halves(grad, lane_starts)
    back = swap(other, 1, 0)
    sums = [(own[m] + back[m].astype(F32)).astype(LOW) for m in range(4)]
    return [sums[0]] + [swap(sums[m], 2 * m, 0) for m in (1, 2, 3)]


VMEM_SPEC = pl.BlockSpec(memory_space=pltpu.VMEM)
SMEM_SPEC = pl.BlockSpec(memory_space=pltpu.SMEM)
ANY_SPEC = pl.BlockSpec(memory_space=pl.ANY)


def pick_qkv(came, picked, rows):
    n_src = len(came)

    def body(which, where, *refs):
        srcs, out = refs[:n_src], refs[n_src]

        def copy(tile, carry):
            for n in range(n_src):

                @pl.when(which[tile] == n)
                def _(n=n):
                    for half in range(2):
                        row = pl.multiple_of(half * 512 + (tile % 4) * 128, 128)
                        lane = pl.multiple_of((tile // 4) * 128, 128)
                        out[pl.ds(row, 128), pl.ds(lane, 128)] = srcs[n][
                            where[tile], :, half * 128 : half * 128 + 128
                        ]

            return carry

        lax.fori_loop(0, 12, copy, 0)

    return pl.pallas_call(
        body,
        in_specs=[SMEM_SPEC, SMEM_SPEC] + [VMEM_SPEC] * n_src,
        out_specs=VMEM_SPEC,
        out_shape=jax.ShapeDtypeStruct((1024, 384), LOW),
        name="pick_qkv",
    )(picked, rows, *came)


def row_gather(sources, picked, rows, sizes):
    total = sum(sizes)
    n_src = len(sources)

    def body(which, where, *refs):
        srcs, outs, sem = refs[:n_src], refs[n_src:-1], refs[-1]
        first = 0
        for out, size in zip(outs, sizes):

            def start(j, carry, out=out, first=first):
                t = first + j
                for n in range(n_src):

                    @pl.when(which[t] == n)
                    def _(n=n):
                        pltpu.make_async_copy(srcs[n].at[where[t]], out.at[j], sem.at[t]).start()

                return carry

            lax.fori_loop(0, size, start, 0)
            first += size
        first = 0
        for out, size in zip(outs, sizes):

            def finish(j, carry, out=out, first=first):
                pltpu.make_async_copy(srcs[0].at[0], out.at[j], sem.at[first + j]).wait()
                return carry

            lax.fori_loop(0, size, finish, 0)
            first += size

    tail = sources[0].shape[1:]
    return pl.pallas_call(
        body,
        in_specs=[SMEM_SPEC, SMEM_SPEC] + [VMEM_SPEC] * n_src,
        out_specs=[ANY_SPEC] * len(sizes),
        out_shape=[jax.ShapeDtypeStruct((size,) + tail, LOW) for size in sizes],
        scratch_shapes=[pltpu.SemaphoreType.DMA((total,))],
        name="row_gather",
    )(picked, rows, *sources)


def send_tile(src, tile, to, row, outs, sem):
    for n, out in enumerate(outs):

        @pl.when(to[tile] == n)
        def _(out=out):
            pltpu.make_async_copy(src, out.at[row[tile]], sem.at[tile]).start()


def place_mlp(gate_up, downs, to, row, place, count, size):
    def body(to_ref, row_ref, z_ref, gu_ref, *refs):
        down_refs, outs, sem = refs[:4], refs[4:-1], refs[-1]
        down_tile = lambda m, k: 48 + 4 * ((k + 2 * z_ref[1]) % 4) + (z_ref[0] ^ m)

        def start(j, carry):
            at = pl.ds(pl.multiple_of(128 * j, 128), 128)
            for half in range(2):
                src = gu_ref.at[at, pl.ds(256 * half, 256)]
                send_tile(src, 16 + 16 * half + j, to_ref, row_ref, outs, sem)
            return carry

        lax.fori_loop(0, 16, start, 0)
        for m in range(4):

            def start_down(k, carry, m=m):
                send_tile(down_refs[m].at[k], down_tile(m, k), to_ref, row_ref, outs, sem)
                return carry

            lax.fori_loop(0, 4, start_down, 0)

        def finish(tile, carry):
            pltpu.make_async_copy(down_refs[0].at[0], outs[0].at[0], sem.at[tile]).wait()
            return carry

        lax.fori_loop(16, 64, finish, 0)

    return pl.pallas_call(
        body,
        in_specs=[SMEM_SPEC] * 3 + [VMEM_SPEC] * 5,
        out_specs=[ANY_SPEC] * count,
        out_shape=[jax.ShapeDtypeStruct((size, 128, 256), LOW)] * count,
        scratch_shapes=[pltpu.SemaphoreType.DMA((64,))],
        name="place_mlp",
    )(to, row, place, gate_up, *downs)


def place_attention(buffers, qkv, outs_from, to, row, place):
    count = len(buffers)

    def body(to_ref, row_ref, z_ref, qkv_ref, *refs):
        out_refs, outs = refs[:4], refs[4 + count : 4 + 2 * count]
        tiles, sem = refs[-2:]

        def start(tile, carry):
            lane = pl.multiple_of((tile // 4) * 128, 128)
            for half in range(2):
                at = pl.ds(pl.multiple_of(half * 512 + (tile % 4) * 128, 128), 128)
                tiles[tile, :, half * 128 : half * 128 + 128] = qkv_ref[at, pl.ds(lane, 128)]
            return carry

        lax.fori_loop(0, 12, start, 0)

        def start_copy(tile, carry):
            send_tile(tiles.at[tile], tile, to_ref, row_ref, outs, sem)
            return carry

        for m in range(4):
            send_tile(out_refs[m].at[0], 12 + (z_ref[0] ^ m), to_ref, row_ref, outs, sem)
        lax.fori_loop(0, 12, start_copy, 0)

        def finish(tile, carry):
            pltpu.make_async_copy(tiles.at[0], outs[0].at[0], sem.at[tile]).wait()
            return carry

        lax.fori_loop(0, 16, finish, 0)

    return pl.pallas_call(
        body,
        in_specs=[SMEM_SPEC] * 3 + [VMEM_SPEC] * 5 + [ANY_SPEC] * count,
        out_specs=[ANY_SPEC] * count,
        out_shape=[jax.ShapeDtypeStruct(buf.shape, buf.dtype) for buf in buffers],
        scratch_shapes=[pltpu.VMEM((12, 128, 256), LOW), pltpu.SemaphoreType.DMA((16,))],
        input_output_aliases={8 + n: n for n in range(count)},
        name="place_attention",
    )(to, row, place, qkv, *outs_from, *buffers)


def after(value, *earlier):
    return lax.optimization_barrier((value,) + earlier)[0]


def key_scores(q, here, there, masks):
    qp, qd, kp, kd = masks
    raw = jnp.concatenate([dot_nt(q, here[:, :128]), dot_nt(q, there[:, :128])], axis=1)
    seen = (kp[...] <= qp[...]) & (kd[...] == qd[...])
    return jnp.where(seen, raw * (1.0 / math.sqrt(HEAD_DIM)), neg_fill)


def attend(query, here, there, masks, n_blocks):
    rows = query.shape[0]
    block = rows // n_blocks

    def body(q, kv, kv_there, qp, qd, kp, kd, out, lse):
        scores = key_scores(q[...], kv[...], kv_there[...], (qp, qd, kp, kd))
        top = jnp.max(scores, axis=1, keepdims=True)
        weights = jnp.exp(scores - top)
        total = jnp.sum(weights, axis=1, keepdims=True)
        probs = (weights * (1.0 / total)).astype(LOW)
        mixed = dot(probs[:, :rows], kv[:, 128:]) + dot(probs[:, rows:], kv_there[:, 128:])
        out[...] = mixed.astype(LOW)
        lse[...] = top + jnp.log(total)

    whole = lambda arr: pl.BlockSpec(arr.shape, lambda i: (0, 0))
    part = lambda arr: pl.BlockSpec((block, arr.shape[1]), lambda i: (i, 0))
    q_pos, q_doc, k_pos, k_doc = masks
    return pl.pallas_call(
        body,
        grid=(n_blocks,),
        in_specs=[
            part(query), whole(here), whole(there), part(q_pos), part(q_doc), whole(k_pos), whole(k_doc),
        ],
        out_specs=[
            pl.BlockSpec((block, HEAD_DIM), lambda i: (i, 0)),
            pl.BlockSpec((block, 1), lambda i: (i, 0)),
        ],
        out_shape=[
            jax.ShapeDtypeStruct((rows, HEAD_DIM), LOW),
            jax.ShapeDtypeStruct((rows, 1), F32),
        ],
        name="attend",
    )(query, here, there, *masks)


def attend_back(query, here, there, out_grad, lse, masks, n_blocks):
    rows = query.shape[0]
    block = rows // n_blocks

    def body(q, kv, kv_there, do, ls, qp, qd, kp, kd, dq, d_here, d_there, acc):
        step = pl.program_id(0)

        @pl.when(step == 0)
        def _():
            d_here[...] = jnp.zeros_like(d_here)
            acc[...] = jnp.zeros_like(acc)

        scores = key_scores(q[...], kv[...], kv_there[...], (qp, qd, kp, kd))
        probs = jnp.exp(scores - ls[...])
        prob_grad = jnp.concatenate(
            [dot_nt(do[...], kv[:, 128:]), dot_nt(do[...], kv_there[:, 128:])], axis=1
        )
        delta = jnp.sum(probs * prob_grad, axis=1, keepdims=True)
        score_grad = (probs * (prob_grad - delta) * (1.0 / math.sqrt(HEAD_DIM))).astype(LOW)
        probs_low = probs.astype(LOW)
        dq[...] = dot(score_grad[:, :rows], kv[:, :128]) + dot(
            score_grad[:, rows:], kv_there[:, :128]
        )
        for first, out in ((0, d_here), (rows, acc)):
            out[:, :128] += dot_tn(score_grad[:, first : first + rows], q[...])
            out[:, 128:] += dot_tn(probs_low[:, first : first + rows], do[...])

        @pl.when(step == n_blocks - 1)
        def _():
            d_there[...] = acc[...].astype(LOW)

    whole = lambda arr: pl.BlockSpec(arr.shape, lambda i: (0, 0))
    part = lambda arr: pl.BlockSpec((block, arr.shape[1]), lambda i: (i, 0))
    kept = pl.BlockSpec((rows, 2 * HEAD_DIM), lambda i: (0, 0))
    q_pos, q_doc, k_pos, k_doc = masks
    return pl.pallas_call(
        body,
        grid=(n_blocks,),
        in_specs=[
            part(query), whole(here), whole(there), part(out_grad), part(lse),
            part(q_pos), part(q_doc), whole(k_pos), whole(k_doc),
        ],
        out_specs=[pl.BlockSpec((block, HEAD_DIM), lambda i: (i, 0)), kept, kept],
        out_shape=[
            jax.ShapeDtypeStruct((rows, HEAD_DIM), F32),
            jax.ShapeDtypeStruct((rows, 2 * HEAD_DIM), F32),
            jax.ShapeDtypeStruct((rows, 2 * HEAD_DIM), LOW),
        ],
        scratch_shapes=[pltpu.VMEM((rows, 2 * HEAD_DIM), F32)],
        name="attend_back",
    )(query, here, there, out_grad, lse, *masks)


def update(state, pieces, lane_starts, used, first, done):
    rows, width = state[0].shape[1:]
    count, homes = pieces[0].shape[0], len(pieces)
    bias = 1.0 - adam_beta**STEP

    def body(starts, live, mas, one, two, *refs):
        grads, (new_mas, new_one, new_two, copy) = refs[:homes], refs[-4:]
        alive = live[pl.program_id(0) + first] > 0
        for home in range(homes):
            for half in range(2):
                at = (0, slice(None), pl.ds(pl.multiple_of(starts[2 * home + half], 128), 128))
                grad = grads[home][0, :, half * 128 : half * 128 + 128].astype(F32)
                grad = jnp.where(alive, grad, 0.0)
                mean = adam_beta * one[at] + (1.0 - adam_beta) * grad
                square = adam_beta * two[at] + (1.0 - adam_beta) * grad * grad
                ratio = (mean * (1.0 / bias)) / (jnp.sqrt(square * (1.0 / bias)) + adam_eps)
                old = mas[at]
                new = old - learn_rate * (ratio + decay_rate * old)
                new_mas[at] = new
                new_one[at] = mean
                new_two[at] = square
                copy[at] = new.astype(LOW)

    slot = pl.BlockSpec((1, rows, width), lambda i, s, u: (i + first, 0, 0))
    piece = pl.BlockSpec((1, rows, 256), lambda i, s, u: (i, 0, 0))
    shape = state[0].shape
    return pl.pallas_call(
        body,
        grid_spec=pltpu.PrefetchScalarGridSpec(
            num_scalar_prefetch=2,
            grid=(count,),
            in_specs=[slot] * 3 + [piece] * homes + [ANY_SPEC] * len(done),
            out_specs=[slot] * 4,
        ),
        out_shape=[jax.ShapeDtypeStruct(shape, F32)] * 3 + [jax.ShapeDtypeStruct(shape, LOW)],
        input_output_aliases={5 + homes + n: n for n in range(len(done))},
        name="update",
    )(lane_starts, used, *state, *pieces, *done)


def gather_rows(piece):
    near = [piece] + [swap(piece, 2 * k, 0) for k in (1, 2, 3)]
    blocks = []
    for part in near:
        pair = jnp.concatenate([part, swap(part, 0, 2)])
        blocks += [pair, swap(pair, 0, 1)]
    return jnp.concatenate(blocks)


def scatter_sum(partial_sum):
    quarter = partial_sum.shape[0] // 4
    half, rows = quarter // 2, quarter // 4
    kept = [None] * 4
    begun = None
    for k in (3, 2, 1, 0):
        chunk = partial_sum[quarter * k : quarter * (k + 1)]
        other = swap(chunk[half:].astype(LOW), 0, 1)
        begun = other if begun is None else begun
        pair = chunk[:half].astype(F32) + other.astype(F32)
        other = swap(pair[rows:].astype(LOW), 0, 2)
        kept[k] = pair[:rows] + other.astype(F32)
    total = kept[0]
    for k in (1, 2, 3):
        total = total + swap(kept[k].astype(LOW), 2 * k, 0).astype(F32)
    return total, begun


def share_rows(piece, wt_index):
    rows = piece.shape[0]
    out = jnp.zeros((4 * rows,) + piece.shape[1:], piece.dtype)
    over_y = swap(piece, 0, 2)
    for bits, part in ((0, piece), (2, over_y), (1, swap(piece, 0, 1)), (3, swap(over_y, 0, 1))):
        out = lax.dynamic_update_slice(out, part, ((wt_index ^ bits) * rows, 0))
    return out


def rotate(values, cosine, sine):
    half = values.shape[-1] // 2
    first, second = values[:, :half], values[:, half:]
    return jnp.concatenate([first * cosine - second * sine, second * cosine + first * sine], axis=1)


def fast_shards(tokens, cotangent, doc_lengths, owners, master, moment_one, moment_two):
    ctx, wt = lax.axis_index("ctx"), lax.axis_index("wt")
    n_ctx = lax.axis_size("ctx")
    z_at, x_at = ctx // 2, ctx % 2
    tok_rows, width = tokens.shape
    cap, tile_rows, _ = master.shape
    n_tiles = owners.shape[0]
    rows = tok_rows // 4
    bits = jnp.arange(4, dtype=jnp.int32)
    homes = jnp.arange(8, dtype=jnp.int32) ^ ctx
    lane_starts = (
        ((2 * (homes % 2))[:, None] + jnp.arange(2, dtype=jnp.int32)) * 4 + (homes // 2)[:, None]
    ).reshape(-1) * 128

    owner_col = owners[:, 0]
    tile_ids = jnp.arange(n_tiles, dtype=jnp.int32)
    earlier = (owner_col[None, :] == owner_col[:, None]) & (tile_ids[None, :] < tile_ids[:, None])
    slot_in_owner = jnp.sum(earlier.astype(jnp.int32), axis=1)
    owner_bits = owner_col ^ ctx

    cut = lane_split(master, lane_starts)
    came = [cut[0]] + [swap(cut[k], k, 0) for k in range(1, 8)]
    w_qkv = pick_qkv(came, owner_bits[:12], slot_in_owner[:12])
    w_qkv_pair = swap(w_qkv, 1, 0)
    wanted = jnp.concatenate(
        [
            jnp.arange(16, 48, dtype=jnp.int32),
            12 + (z_at ^ bits),
            (48 + 4 * ((bits + 2 * x_at) % 4)[None, :] + (z_at ^ bits)[:, None]).reshape(-1),
        ]
    )
    wanted = after(wanted, w_qkv)
    home_gu, *sends = row_gather(
        came, owner_bits[wanted], slot_in_owner[wanted], [32] + [1] * 4 + [4] * 4
    )
    out_here = jnp.stack([sends[0]] + [swap(sends[m], 2 * m, 0) for m in (1, 2, 3)])
    w_out = lane_join(out_here, swap(out_here, 1, 0), lane_starts).reshape(tile_rows, width)
    down_here = jnp.stack([sends[4]] + [swap(sends[4 + m], 2 * m, 0) for m in (1, 2, 3)])

    block_z = z_at ^ bits
    block_w = wt ^ jnp.array([0, 2, 1, 3], jnp.int32)

    def group_positions(x_index):
        starts = (2 * block_z + x_index)[:, None] * tok_rows + block_w[None, :] * rows
        return (starts.reshape(-1)[:, None] + jnp.arange(rows, dtype=jnp.int32)).reshape(-1)

    q_pos = group_positions(x_at)
    k_pos = jnp.concatenate([q_pos, group_positions(1 - x_at)])
    doc_starts = jnp.cumsum(doc_lengths) - doc_lengths
    q_doc, k_doc = doc_index(q_pos, doc_starts), doc_index(k_pos, doc_starts)
    masks = (q_pos[:, None], q_doc[:, None], k_pos[None, :], k_doc[None, :])
    freqs = rope_base ** (-jnp.arange(HEAD_DIM // 2, dtype=F32) * (2.0 / HEAD_DIM))
    angles = q_pos.astype(F32)[:, None] * freqs[None, :]
    cosine, sine = jnp.cos(angles), jnp.sin(angles)

    def to_cut_order(values):
        cut_vals = values.reshape(-1, width // 4, 4).transpose(0, 2, 1).reshape(-1, width)
        flipped = jnp.concatenate([cut_vals[:, width // 2 :], cut_vals[:, : width // 2]], axis=1)
        return jnp.where(x_at == 0, cut_vals, flipped)

    def from_cut_order(values):
        flipped = jnp.concatenate([values[:, width // 2 :], values[:, : width // 2]], axis=1)
        cut_vals = jnp.where(x_at == 0, values, flipped)
        return cut_vals.reshape(-1, 4, width // 4).transpose(0, 2, 1).reshape(-1, width)

    tokens_later = after(tokens, cut[0])
    inputs = lax.dynamic_slice(tokens_later, (wt * rows, 0), (rows, width)).astype(F32)
    out_grad_low = lax.dynamic_slice(cotangent, (wt * rows, 0), (rows, width))
    normed, norm_back = jax.vjp(layer_norm, inputs)
    normed_all = gather_rows(to_cut_order(normed.astype(LOW)))
    grad_all = gather_rows(after(out_grad_low, w_qkv))

    half = width // 2
    qkv = dot(normed_all[:, :half], w_qkv) + dot(normed_all[:, half:], w_qkv_pair)
    query = rotate(qkv[:, :128], cosine, sine).astype(LOW)
    kv_here = jnp.concatenate(
        [rotate(qkv[:, 128:256], cosine, sine).astype(LOW), qkv[:, 256:].astype(LOW)], axis=1
    )
    kv_there = swap(kv_here, 1, 0)
    att_low, lse = attend(query, kv_here, kv_there, masks, 4)

    gu_later, down_later = lax.optimization_barrier((home_gu, down_here, kv_there))[:2]
    pair_gu = swap(gu_later, 1, 0)
    w_down = lane_join(down_here, swap(down_later, 1, 0), lane_starts).reshape(512, width)
    w_gu = jnp.concatenate(
        [part.reshape(width, 256) for half_gu in (home_gu, pair_gu) for part in (half_gu[:16], half_gu[16:])],
        axis=1,
    )
    att_out, _ = scatter_sum(dot(att_low, w_out).astype(LOW))
    residual = inputs + att_out

    normed_two, norm_two_back = jax.vjp(layer_norm, residual)
    two_all = gather_rows(normed_two.astype(LOW))
    gu = dot(two_all, w_gu)
    gate = jnp.concatenate([gu[:, :256], gu[:, 512:768]], axis=1)
    up = jnp.concatenate([gu[:, 256:512], gu[:, 768:]], axis=1)
    gate_sig = jax.nn.sigmoid(gate)
    silu = gate * gate_sig
    hidden = (silu * up).astype(LOW)

    hidden_grad = dot_nt(grad_all, w_down)
    grad_gate = (hidden_grad * up * gate_sig * (1.0 + gate * (1.0 - gate_sig))).astype(LOW)
    grad_up = (hidden_grad * silu).astype(LOW)
    grad_gu = jnp.concatenate(
        [grad_gate[:, :256], grad_up[:, :256], grad_gate[:, 256:], grad_up[:, 256:]], axis=1
    )
    two_grad, begun = scatter_sum(dot_nt(grad_gu, w_gu).astype(LOW))
    hidden_later, grad_gu_later = lax.optimization_barrier((hidden, grad_gu, begun))[:2]
    grad_w_gu = dot_tn(two_all, grad_gu_later)
    gu_back = swap(grad_w_gu[:, 512:].astype(LOW), 1, 0)
    grad_w_down = dot_tn(hidden_later, grad_all)
    down_part = dot(hidden_later, w_down).astype(LOW)

    resid_grad = out_grad_low.astype(F32) + norm_two_back(two_grad)[0]
    resid_all = gather_rows(resid_grad.astype(LOW))
    down, _ = scatter_sum(after(down_part, two_grad))
    output = share_rows((residual + down).astype(LOW), wt)
    gu_sum = (grad_w_gu[:, :512] + gu_back.astype(F32)).astype(LOW)
    down_came = return_halves(grad_w_down.reshape(4, tile_rows, width), lane_starts)

    part_slots = cap // 2
    send_to = owner_bits + 8 * (slot_in_owner // part_slots)
    send_row = slot_in_owner % part_slots
    place = jnp.stack([z_at, x_at])
    sends = place_mlp(gu_sum, down_came, send_to, send_row, place, 16, part_slots)

    att_grad = dot_nt(resid_all, w_out).astype(LOW)
    query_grad, kv_grad, kv_grad_there = attend_back(
        query, kv_here, kv_there, att_grad, lse, masks, 4
    )
    kv_grad = kv_grad + swap(kv_grad_there, 1, 0).astype(F32)
    out_came = return_halves(
        dot_tn(att_low, resid_all).reshape(1, tile_rows, width), lane_starts
    )
    qkv_grad = jnp.concatenate(
        [
            rotate(query_grad, cosine, -sine),
            rotate(kv_grad[:, :128], cosine, -sine),
            kv_grad[:, 128:],
        ],
        axis=1,
    ).astype(LOW)
    qkv_back = swap(dot_tn(normed_all[:, half:], qkv_grad).astype(LOW), 1, 0)
    qkv_sum = (dot_tn(normed_all[:, :half], qkv_grad) + qkv_back.astype(F32)).astype(LOW)
    sends = place_attention(sends, qkv_sum, out_came, send_to, send_row, place)

    qkv_grad_later = after(qkv_grad, sends[0])
    one_part = jnp.concatenate(
        [dot_nt(qkv_grad_later, w_qkv), dot_nt(qkv_grad_later, w_qkv_pair)], axis=1
    )
    one_grad = from_cut_order(scatter_sum(one_part.astype(LOW))[0])
    input_grad = resid_grad + norm_back(one_grad)[0]
    input_grad = share_rows(input_grad.astype(LOW), wt).astype(F32)

    slot_range = jnp.arange(cap, dtype=jnp.int32) + ctx * cap
    used = jnp.any(
        (owner_col * cap + slot_in_owner)[None, :] == slot_range[:, None], axis=1
    ).astype(jnp.int32)
    state, done = (master, moment_one, moment_two), ()
    for part in range(2):
        mine = sends[8 * part : 8 * part + 8]
        pieces = [mine[0]] + [swap(mine[k], k, 0) for k in range(1, 8)]
        done = tuple(update(state, pieces, lane_starts, used, part * part_slots, done))
    return (output, input_grad) + done


def choose_shards(*args):
    sizes = (lax.axis_size("ctx"), lax.axis_size("wt"), args[0].shape, args[4].shape[1:])
    if sizes == (8, 4, (256, 2048), (128, 2048)) and args[3].shape[0] == 64:
        return fast_shards(*args)
    return general_shards(*args)


def solution(mesh):
    placed = (
        P("ctx", None),
        P("ctx", None),
        P(),
        P(),
        P("ctx", None, "wt"),
        P("ctx", None, "wt"),
        P("ctx", None, "wt"),
    )
    return jax.shard_map(
        choose_shards,
        mesh=mesh,
        in_specs=placed,
        out_specs=(
            P("ctx", None),
            P("ctx", None),
            P("ctx", None, "wt"),
            P("ctx", None, "wt"),
            P("ctx", None, "wt"),
            P("ctx", None, "wt"),
        ),
        check_vma=False,
    )
```

```python
from functools import partial
import math

import jax
import jax.numpy as jnp
from jax import lax
from jax.experimental import pallas as pl
from jax.experimental.pallas import tpu as pltpu
from jax.sharding import PartitionSpec as P

HEAD_DIM = 128
STEP = 3


adam_beta = 0.5
learn_rate = 0.01
decay_rate = 0.1
adam_eps = 1e-08
norm_eps = 1e-05
neg_fill = -1e30
rope_base = 10000.0


def from_behind(x, axis, by):
    count = lax.axis_size(axis)
    pairs = [(i, i + by) for i in range(count) if 0 <= i + by < count]
    return lax.ppermute(x, axis, pairs)


def from_behind_2(value, axis, steps):
    count = lax.axis_size(axis)
    pairs = [(source, (source + steps) % count) for source in range(count)]
    return lax.ppermute(value, axis, pairs)


def layer_norm(values):
    center = values - jnp.mean(values, axis=-1, keepdims=True)
    spread = jnp.mean(center * center, axis=-1, keepdims=True)
    return center * lax.rsqrt(spread + norm_eps)


def rotary(values, positions):
    half_dim = values.shape[-1] // 2
    frequencies = rope_base ** (-jnp.arange(half_dim, dtype=jnp.float32) * (2.0 / values.shape[-1]))
    angles = positions.astype(jnp.float32)[:, None] * frequencies[None, :]
    cosine = jnp.cos(angles)[:, None, :]
    sine_vals = jnp.sin(angles)[:, None, :]
    first_half = values[..., :half_dim]
    second_half = values[..., half_dim:]
    return jnp.concatenate(
        [
            first_half * cosine - second_half * sine_vals,
            second_half * cosine + first_half * sine_vals,
        ],
        axis=-1,
    )


def doc_index(positions, doc_starts):
    return jnp.sum((positions[:, None] >= doc_starts[None, :]).astype(jnp.int32), axis=1) - 1


def heads_dot(spec, left, right):
    return jnp.einsum(spec, left, right, preferred_element_type=jnp.float32)


def general_shards(tokens, cotangent, doc_lengths, owners, master, moment_one, moment_two):
    n_ctx = lax.axis_size("ctx")
    n_wt = lax.axis_size("wt")
    ctx_index = lax.axis_index("ctx")
    tok_rows, width = tokens.shape
    cap_slots, tile_rows, tile_width = master.shape
    n_tiles = owners.shape[0]
    head_dim = HEAD_DIM
    owner_col = owners[:, 0]
    tile_ids = jnp.arange(n_tiles, dtype=jnp.int32)
    earlier = (owner_col[None, :] == owner_col[:, None]) & (tile_ids[None, :] < tile_ids[:, None])
    slot_ids = owner_col * cap_slots + jnp.sum(earlier.astype(jnp.int32), axis=1)
    every_slot = lax.all_gather(master.astype(jnp.bfloat16), "ctx", axis=0, tiled=True)
    flat_w = every_slot[slot_ids].reshape(-1)
    local_width = width // n_wt
    heads_local = local_width // head_dim
    part_q = width * local_width
    ff_local = (flat_w.shape[0] - 4 * part_q) // (3 * width)
    part_f = width * ff_local
    w_qkv = flat_w[: 3 * part_q].reshape(3, width, local_width)
    w_out = flat_w[3 * part_q : 4 * part_q].reshape(local_width, width)
    w_gateup = flat_w[4 * part_q : 4 * part_q + 2 * part_f].reshape(2, width, ff_local)
    w_down = flat_w[4 * part_q + 2 * part_f :].reshape(ff_local, width)
    positions = ctx_index * tok_rows + jnp.arange(tok_rows, dtype=jnp.int32)
    doc_starts = jnp.cumsum(doc_lengths) - doc_lengths
    q_docs = doc_index(positions, doc_starts)
    score_scale = 1.0 / math.sqrt(head_dim)
    inputs = tokens.astype(jnp.float32)
    normed, norm_back = jax.vjp(layer_norm, inputs)
    normed_low = normed.astype(jnp.bfloat16)
    qkv_vals = heads_dot("td,jde->jte", normed_low, w_qkv)
    shaped = qkv_vals.reshape(3, tok_rows, heads_local, head_dim)
    rope_here = partial(rotary, positions=positions)
    qk_rot, rope_back = jax.vjp(rope_here, jnp.concatenate([shaped[0], shaped[1]], axis=1))
    q_low = qk_rot[:, :heads_local].astype(jnp.bfloat16)
    k_low = qk_rot[:, heads_local:].astype(jnp.bfloat16)
    v_low = shaped[2].astype(jnp.bfloat16)

    def masked_scores(key_block, key_pos, key_docs):
        raw_scores = heads_dot("qhd,khd->hqk", q_low, key_block)
        visible_mask = (key_pos[None, :] <= positions[:, None]) & (
            key_docs[None, :] == q_docs[:, None]
        )
        return (jnp.where(visible_mask[None], raw_scores * score_scale, neg_fill), visible_mask)

    def over_blocks(kv_piece, first_row, update_fn, running):
        key_count = kv_piece[0].shape[0]
        block_len = math.gcd(key_count, 512)
        n_blocks = key_count // block_len
        split_kv = tuple(
            (member.reshape((n_blocks, block_len) + member.shape[1:]) for member in kv_piece)
        )

        def step_fn(block_state, inputs_here):
            block_idx, block_vals = inputs_here
            block_row = first_row + block_idx * block_len
            key_pos = block_row + jnp.arange(block_len, dtype=jnp.int32)
            key_docs = doc_index(key_pos, doc_starts)
            block_state = update_fn(block_state, block_vals, key_pos, key_docs, block_row)
            return (block_state, None)

        running, _ = lax.scan(step_fn, running, (jnp.arange(n_blocks, dtype=jnp.int32), split_kv))
        return running

    def norm_update(block_state, block_vals, key_pos, key_docs, block_row):
        row_top, row_total = block_state
        scores, visible_mask = masked_scores(block_vals[0], key_pos, key_docs)
        new_top = jnp.maximum(row_top, jnp.max(scores, axis=-1))
        weights_exp = jnp.where(visible_mask[None], jnp.exp(scores - new_top[:, :, None]), 0.0)
        return (new_top, row_total * jnp.exp(row_top - new_top) + jnp.sum(weights_exp, axis=-1))

    start_top = jnp.full((heads_local, tok_rows), neg_fill, jnp.float32)
    start_total = jnp.zeros((heads_local, tok_rows), jnp.float32)
    row_top, row_total = over_blocks(
        (lax.all_gather(k_low, "ctx", axis=0, tiled=True),),
        jnp.int32(0),
        norm_update,
        (start_top, start_total),
    )
    log_sum = row_top + jnp.log(row_total)

    def block_probs(key_block, key_pos, key_docs):
        scores, visible_mask = masked_scores(key_block, key_pos, key_docs)
        return jnp.where(visible_mask[None], jnp.exp(scores - log_sum[:, :, None]), 0.0)

    def value_update(block_state, block_vals, key_pos, key_docs, block_row):
        prob_vals = block_probs(block_vals[0], key_pos, key_docs)
        return block_state + heads_dot(
            "hqk,khd->qhd", prob_vals.astype(jnp.bfloat16), block_vals[1]
        )

    zero_heads = jnp.zeros((tok_rows, heads_local, head_dim), jnp.float32)
    attended = over_blocks(
        (
            lax.all_gather(k_low, "ctx", axis=0, tiled=True),
            lax.all_gather(v_low, "ctx", axis=0, tiled=True),
        ),
        jnp.int32(0),
        value_update,
        zero_heads,
    )
    att_low = attended.reshape(tok_rows, local_width).astype(jnp.bfloat16)
    attn_part = jnp.dot(att_low, w_out, preferred_element_type=jnp.float32)
    residual = inputs + lax.psum(attn_part.astype(jnp.bfloat16), "wt").astype(jnp.float32)
    normed_two, norm_two_back = jax.vjp(layer_norm, residual)
    normed_two_low = normed_two.astype(jnp.bfloat16)
    gateup_vals = heads_dot("td,jde->jte", normed_two_low, w_gateup)
    gate_vals = gateup_vals[0]
    up_vals = gateup_vals[1]
    gate_sig = jax.nn.sigmoid(gate_vals)
    silu_vals = gate_vals * gate_sig
    hidden_low = (silu_vals * up_vals).astype(jnp.bfloat16)
    mlp_part = jnp.dot(hidden_low, w_down, preferred_element_type=jnp.float32)
    output = (residual + lax.psum(mlp_part.astype(jnp.bfloat16), "wt").astype(jnp.float32)).astype(
        jnp.bfloat16
    )
    out_grad = cotangent.astype(jnp.float32)
    grad_down = heads_dot("tf,td->fd", hidden_low, cotangent)
    grad_hidden = heads_dot("td,fd->tf", cotangent, w_down)
    grad_gate = grad_hidden * up_vals * gate_sig * (1.0 + gate_vals * (1.0 - gate_sig))
    grad_up = grad_hidden * silu_vals
    grad_gu_low = jnp.stack([grad_gate, grad_up]).astype(jnp.bfloat16)
    grad_gateup = heads_dot("td,jte->jde", normed_two_low, grad_gu_low)
    norm_two_part = heads_dot("jte,jde->td", grad_gu_low, w_gateup)
    norm_two_grad = lax.psum(norm_two_part.astype(jnp.bfloat16), "wt").astype(jnp.float32)
    resid_grad = out_grad + norm_two_back(norm_two_grad)[0]
    resid_low = resid_grad.astype(jnp.bfloat16)
    grad_out = heads_dot("tc,td->cd", att_low, resid_low)
    att_grad = heads_dot("td,cd->tc", resid_low, w_out)
    att_grad_low = att_grad.astype(jnp.bfloat16).reshape(tok_rows, heads_local, head_dim)
    row_delta = jnp.sum(att_grad_low * attended, axis=-1).T

    def grad_block(block_vals, key_pos, key_docs):
        prob_vals = block_probs(block_vals[0], key_pos, key_docs)
        value_grad = heads_dot("hqk,qhd->khd", prob_vals.astype(jnp.bfloat16), att_grad_low)
        prob_grad = heads_dot("qhd,khd->hqk", att_grad_low, block_vals[1])
        raw_grad = (prob_vals * (prob_grad - row_delta[:, :, None]) * score_scale).astype(
            jnp.bfloat16
        )
        query_grad = heads_dot("hqk,khd->qhd", raw_grad, block_vals[0])
        key_grad = heads_dot("hqk,qhd->khd", raw_grad, q_low)
        return (query_grad, key_grad, value_grad)

    def add_rows(target, addend):
        return target + addend

    def cycle_step(turn_idx, cycle_state):
        query_acc, key_cur, value_cur, key_acc, value_acc = cycle_state
        anchor = (ctx_index - turn_idx) % n_ctx

        def cycle_update(block_state, block_vals, key_pos, key_docs, block_row):
            q_acc, k_acc, v_acc = block_state
            query_grad, key_grad, value_grad = grad_block(block_vals, key_pos, key_docs)
            return (q_acc + query_grad, add_rows(k_acc, key_grad), add_rows(v_acc, value_grad))

        query_acc, key_acc, value_acc = over_blocks(
            (key_cur, value_cur), anchor * tok_rows, cycle_update, (query_acc, key_acc, value_acc)
        )
        key_cur, value_cur = from_behind((key_cur, value_cur), "ctx", 1)
        key_acc, value_acc = (
            from_behind_2(key_acc.astype(jnp.bfloat16), "ctx", 1).astype(key_acc.dtype),
            from_behind_2(value_acc.astype(jnp.bfloat16), "ctx", 1).astype(value_acc.dtype),
        )
        return (query_acc, key_cur, value_cur, key_acc, value_acc)

    cycle_start = (zero_heads, k_low, v_low, zero_heads, zero_heads)
    query_acc, _, _, key_acc, value_acc = lax.fori_loop(0, n_ctx, cycle_step, cycle_start)
    qk_pre_grad = rope_back(jnp.concatenate([query_acc, key_acc], axis=1))[0]
    qkv_grad_low = jnp.stack(
        [
            qk_pre_grad[:, :heads_local].reshape(tok_rows, local_width),
            qk_pre_grad[:, heads_local:].reshape(tok_rows, local_width),
            value_acc.reshape(tok_rows, local_width),
        ]
    ).astype(jnp.bfloat16)
    grad_qkv = heads_dot("td,jte->jde", normed_low, qkv_grad_low)
    norm_one_part = heads_dot("jte,jde->td", qkv_grad_low, w_qkv)
    norm_one_grad = lax.psum(norm_one_part.astype(jnp.bfloat16), "wt").astype(jnp.float32)
    input_grad = resid_grad + norm_back(norm_one_grad)[0]
    grad_tiles = jnp.concatenate(
        [grad_qkv.reshape(-1), grad_out.reshape(-1), grad_gateup.reshape(-1), grad_down.reshape(-1)]
    ).reshape(n_tiles, tile_rows, tile_width)
    slot_range = jnp.arange(n_ctx * cap_slots, dtype=jnp.int32)
    matches = slot_ids[None, :] == slot_range[:, None]
    tile_of_slot = jnp.sum(jnp.where(matches, tile_ids[None, :], 0), axis=1)
    slot_used = jnp.any(matches, axis=1)
    slot_grads = lax.psum_scatter(
        jnp.where(slot_used[:, None, None], grad_tiles[tile_of_slot], 0.0).astype(jnp.bfloat16),
        "ctx",
        scatter_dimension=0,
        tiled=True,
    ).astype(jnp.float32)
    new_one = adam_beta * moment_one + (1.0 - adam_beta) * slot_grads
    new_two = adam_beta * moment_two + (1.0 - adam_beta) * slot_grads * slot_grads
    bias_one = 1.0 - adam_beta**STEP
    bias_two = 1.0 - adam_beta**STEP
    step_ratio = new_one / bias_one / (jnp.sqrt(new_two / bias_two) + adam_eps)
    new_master = master - learn_rate * (step_ratio + decay_rate * master)
    return (output, input_grad, new_master, new_one, new_two, new_master.astype(jnp.bfloat16))


AXES = ("ctx", "wt")
LOW = jnp.bfloat16
F32 = jnp.float32


def swap(value, ctx_bits, wt_bits):
    n_ctx, n_wt = lax.axis_size("ctx"), lax.axis_size("wt")
    pairs = [
        (c * n_wt + w, (c ^ ctx_bits) * n_wt + (w ^ wt_bits))
        for c in range(n_ctx)
        for w in range(n_wt)
    ]
    return lax.ppermute(value, AXES, pairs)


def shift_z(value, step, starts):
    n_wt = lax.axis_size("wt")
    pairs = [
        ((2 * z + x) * n_wt + w, (2 * (z + step) + x) * n_wt + w)
        for z in starts
        for x in range(2)
        for w in range(n_wt)
    ]
    return lax.ppermute(value, AXES, pairs)


def dot(left, right):
    return jnp.dot(left, right, preferred_element_type=F32)


def dot_tn(left, right):
    return lax.dot_general(left, right, (((0,), (0,)), ((), ())), preferred_element_type=F32)


def dot_nt(left, right):
    return lax.dot_general(left, right, (((1,), (1,)), ((), ())), preferred_element_type=F32)


def lane_split(value, lane_starts):
    count, rows, width = value.shape
    homes = lane_starts.shape[0] // 2

    def body(starts, src, *outs):
        for home in range(homes):
            for half in range(2):
                start = pl.multiple_of(starts[2 * home + half], 128)
                outs[home][0, :, half * 128 : half * 128 + 128] = src[
                    0, :, pl.ds(start, 128)
                ].astype(LOW)

    return pl.pallas_call(
        body,
        grid_spec=pltpu.PrefetchScalarGridSpec(
            num_scalar_prefetch=1,
            grid=(count,),
            in_specs=[pl.BlockSpec((1, rows, width), lambda i, s: (i, 0, 0))],
            out_specs=[pl.BlockSpec((1, rows, 256), lambda i, s: (i, 0, 0))] * homes,
        ),
        out_shape=[jax.ShapeDtypeStruct((count, rows, 256), LOW)] * homes,
        name="lane_split",
    )(lane_starts, value)


def lane_join(own, other, lane_starts):
    homes, count, rows, _ = own.shape
    width = homes * 512

    def body(starts, own_ref, other_ref, out):
        for home in range(homes):
            for side, ref in ((0, own_ref), (1, other_ref)):
                for half in range(2):
                    start = pl.multiple_of(starts[4 * home + 2 * side + half], 128)
                    out[0, :, pl.ds(start, 128)] = ref[home, 0, :, half * 128 : half * 128 + 128]

    return pl.pallas_call(
        body,
        grid_spec=pltpu.PrefetchScalarGridSpec(
            num_scalar_prefetch=1,
            grid=(count,),
            in_specs=[
                pl.BlockSpec((homes, 1, rows, 256), lambda i, s: (0, i, 0, 0)),
                pl.BlockSpec(
                    (homes, 1, rows, 256), lambda i, s: (0, (i + count // 2) % count, 0, 0)
                ),
            ],
            out_specs=pl.BlockSpec((1, rows, width), lambda i, s: (i, 0, 0)),
        ),
        out_shape=jax.ShapeDtypeStruct((count, rows, width), LOW),
        name="lane_join",
    )(lane_starts, own, other)


def lane_halves(value, lane_starts):
    count, rows, width = value.shape
    homes = width // 512

    def body(starts, src, own_ref, other_ref):
        for home in range(homes):
            for side, ref in ((0, own_ref), (1, other_ref)):
                for half in range(2):
                    start = pl.multiple_of(starts[4 * home + 2 * side + half], 128)
                    ref[home, 0, :, half * 128 : half * 128 + 128] = src[
                        0, :, pl.ds(start, 128)
                    ].astype(ref.dtype)

    return pl.pallas_call(
        body,
        grid_spec=pltpu.PrefetchScalarGridSpec(
            num_scalar_prefetch=1,
            grid=(count,),
            in_specs=[pl.BlockSpec((1, rows, width), lambda i, s: (i, 0, 0))],
            out_specs=[
                pl.BlockSpec((homes, 1, rows, 256), lambda i, s: (0, i, 0, 0)),
                pl.BlockSpec(
                    (homes, 1, rows, 256), lambda i, s: (0, (i + count // 2) % count, 0, 0)
                ),
            ],
        ),
        out_shape=[
            jax.ShapeDtypeStruct((homes, count, rows, 256), dtype) for dtype in (F32, LOW)
        ],
        name="lane_halves",
    )(lane_starts, value)


def return_halves(grad, lane_starts):
    own, other = lane_halves(grad, lane_starts)
    back = swap(other, 1, 0)
    sums = [(own[m] + back[m].astype(F32)).astype(LOW) for m in range(4)]
    return [sums[0]] + [swap(sums[m], 2 * m, 0) for m in (1, 2, 3)]


VMEM_SPEC = pl.BlockSpec(memory_space=pltpu.VMEM)
SMEM_SPEC = pl.BlockSpec(memory_space=pltpu.SMEM)
ANY_SPEC = pl.BlockSpec(memory_space=pl.ANY)


def pick_qkv(came, picked, rows):
    n_src = len(came)

    def body(which, where, *refs):
        srcs, out = refs[:n_src], refs[n_src]

        def copy(tile, carry):
            for n in range(n_src):

                @pl.when(which[tile] == n)
                def _(n=n):
                    for half in range(2):
                        row = pl.multiple_of(half * 512 + (tile % 4) * 128, 128)
                        lane = pl.multiple_of((tile // 4) * 128, 128)
                        out[pl.ds(row, 128), pl.ds(lane, 128)] = srcs[n][
                            where[tile], :, half * 128 : half * 128 + 128
                        ]

            return carry

        lax.fori_loop(0, 12, copy, 0)

    return pl.pallas_call(
        body,
        in_specs=[SMEM_SPEC, SMEM_SPEC] + [VMEM_SPEC] * n_src,
        out_specs=VMEM_SPEC,
        out_shape=jax.ShapeDtypeStruct((1024, 384), LOW),
        name="pick_qkv",
    )(picked, rows, *came)


def row_gather(sources, picked, rows, sizes):
    total = sum(sizes)
    n_src = len(sources)

    def body(which, where, *refs):
        srcs, outs, sem = refs[:n_src], refs[n_src:-1], refs[-1]
        first = 0
        for out, size in zip(outs, sizes):

            def start(j, carry, out=out, first=first):
                t = first + j
                for n in range(n_src):

                    @pl.when(which[t] == n)
                    def _(n=n):
                        pltpu.make_async_copy(srcs[n].at[where[t]], out.at[j], sem.at[t]).start()

                return carry

            lax.fori_loop(0, size, start, 0)
            first += size
        first = 0
        for out, size in zip(outs, sizes):

            def finish(j, carry, out=out, first=first):
                pltpu.make_async_copy(srcs[0].at[0], out.at[j], sem.at[first + j]).wait()
                return carry

            lax.fori_loop(0, size, finish, 0)
            first += size

    tail = sources[0].shape[1:]
    return pl.pallas_call(
        body,
        in_specs=[SMEM_SPEC, SMEM_SPEC] + [VMEM_SPEC] * n_src,
        out_specs=[ANY_SPEC] * len(sizes),
        out_shape=[jax.ShapeDtypeStruct((size,) + tail, LOW) for size in sizes],
        scratch_shapes=[pltpu.SemaphoreType.DMA((total,))],
        name="row_gather",
    )(picked, rows, *sources)


def send_tile(src, tile, to, row, outs, sem):
    for n, out in enumerate(outs):

        @pl.when(to[tile] == n)
        def _(out=out):
            pltpu.make_async_copy(src, out.at[row[tile]], sem.at[tile]).start()


def place_mlp(gate_up, downs, to, row, place, count, size):
    def body(to_ref, row_ref, z_ref, gu_ref, *refs):
        down_refs, outs, sem = refs[:4], refs[4:-1], refs[-1]
        down_tile = lambda m, k: 48 + 4 * ((k + 2 * z_ref[1]) % 4) + (z_ref[0] ^ m)

        def start(j, carry):
            at = pl.ds(pl.multiple_of(128 * j, 128), 128)
            for half in range(2):
                src = gu_ref.at[at, pl.ds(256 * half, 256)]
                send_tile(src, 16 + 16 * half + j, to_ref, row_ref, outs, sem)
            return carry

        lax.fori_loop(0, 16, start, 0)
        for m in range(4):

            def start_down(k, carry, m=m):
                send_tile(down_refs[m].at[k], down_tile(m, k), to_ref, row_ref, outs, sem)
                return carry

            lax.fori_loop(0, 4, start_down, 0)

        def finish(tile, carry):
            pltpu.make_async_copy(down_refs[0].at[0], outs[0].at[0], sem.at[tile]).wait()
            return carry

        lax.fori_loop(16, 64, finish, 0)

    return pl.pallas_call(
        body,
        in_specs=[SMEM_SPEC] * 3 + [VMEM_SPEC] * 5,
        out_specs=[ANY_SPEC] * count,
        out_shape=[jax.ShapeDtypeStruct((size, 128, 256), LOW)] * count,
        scratch_shapes=[pltpu.SemaphoreType.DMA((64,))],
        name="place_mlp",
    )(to, row, place, gate_up, *downs)


def place_attention(buffers, qkv, outs_from, to, row, place):
    count = len(buffers)

    def body(to_ref, row_ref, z_ref, qkv_ref, *refs):
        out_refs, outs = refs[:4], refs[4 + count : 4 + 2 * count]
        tiles, sem = refs[-2:]

        def start(tile, carry):
            lane = pl.multiple_of((tile // 4) * 128, 128)
            for half in range(2):
                at = pl.ds(pl.multiple_of(half * 512 + (tile % 4) * 128, 128), 128)
                tiles[tile, :, half * 128 : half * 128 + 128] = qkv_ref[at, pl.ds(lane, 128)]
            return carry

        lax.fori_loop(0, 12, start, 0)

        def start_copy(tile, carry):
            send_tile(tiles.at[tile], tile, to_ref, row_ref, outs, sem)
            return carry

        for m in range(4):
            send_tile(out_refs[m].at[0], 12 + (z_ref[0] ^ m), to_ref, row_ref, outs, sem)
        lax.fori_loop(0, 12, start_copy, 0)

        def finish(tile, carry):
            pltpu.make_async_copy(tiles.at[0], outs[0].at[0], sem.at[tile]).wait()
            return carry

        lax.fori_loop(0, 16, finish, 0)

    return pl.pallas_call(
        body,
        in_specs=[SMEM_SPEC] * 3 + [VMEM_SPEC] * 5 + [ANY_SPEC] * count,
        out_specs=[ANY_SPEC] * count,
        out_shape=[jax.ShapeDtypeStruct(buf.shape, buf.dtype) for buf in buffers],
        scratch_shapes=[pltpu.VMEM((12, 128, 256), LOW), pltpu.SemaphoreType.DMA((16,))],
        input_output_aliases={8 + n: n for n in range(count)},
        name="place_attention",
    )(to, row, place, qkv, *outs_from, *buffers)


def after(value, *earlier):
    return lax.optimization_barrier((value,) + earlier)[0]


def key_scores(q, here, there, masks):
    qp, qd, kp, kd = masks
    raw = jnp.concatenate([dot_nt(q, here[:, :128]), dot_nt(q, there[:, :128])], axis=1)
    seen = (kp[...] <= qp[...]) & (kd[...] == qd[...])
    return jnp.where(seen, raw * (1.0 / math.sqrt(HEAD_DIM)), neg_fill)


def attend(query, here, there, masks, n_blocks):
    rows = query.shape[0]
    block = rows // n_blocks

    def body(q, kv, kv_there, qp, qd, kp, kd, out, lse):
        scores = key_scores(q[...], kv[...], kv_there[...], (qp, qd, kp, kd))
        top = jnp.max(scores, axis=1, keepdims=True)
        weights = jnp.exp(scores - top)
        total = jnp.sum(weights, axis=1, keepdims=True)
        probs = (weights * (1.0 / total)).astype(LOW)
        mixed = dot(probs[:, :rows], kv[:, 128:]) + dot(probs[:, rows:], kv_there[:, 128:])
        out[...] = mixed.astype(LOW)
        lse[...] = top + jnp.log(total)

    whole = lambda arr: pl.BlockSpec(arr.shape, lambda i: (0, 0))
    part = lambda arr: pl.BlockSpec((block, arr.shape[1]), lambda i: (i, 0))
    q_pos, q_doc, k_pos, k_doc = masks
    return pl.pallas_call(
        body,
        grid=(n_blocks,),
        in_specs=[
            part(query), whole(here), whole(there), part(q_pos), part(q_doc), whole(k_pos), whole(k_doc),
        ],
        out_specs=[
            pl.BlockSpec((block, HEAD_DIM), lambda i: (i, 0)),
            pl.BlockSpec((block, 1), lambda i: (i, 0)),
        ],
        out_shape=[
            jax.ShapeDtypeStruct((rows, HEAD_DIM), LOW),
            jax.ShapeDtypeStruct((rows, 1), F32),
        ],
        name="attend",
    )(query, here, there, *masks)


def attend_back(query, here, there, out_grad, lse, masks, n_blocks):
    rows = query.shape[0]
    block = rows // n_blocks

    def body(q, kv, kv_there, do, ls, qp, qd, kp, kd, dq, d_here, d_there, acc):
        step = pl.program_id(0)

        @pl.when(step == 0)
        def _():
            d_here[...] = jnp.zeros_like(d_here)
            acc[...] = jnp.zeros_like(acc)

        scores = key_scores(q[...], kv[...], kv_there[...], (qp, qd, kp, kd))
        probs = jnp.exp(scores - ls[...])
        prob_grad = jnp.concatenate(
            [dot_nt(do[...], kv[:, 128:]), dot_nt(do[...], kv_there[:, 128:])], axis=1
        )
        delta = jnp.sum(probs * prob_grad, axis=1, keepdims=True)
        score_grad = (probs * (prob_grad - delta) * (1.0 / math.sqrt(HEAD_DIM))).astype(LOW)
        probs_low = probs.astype(LOW)
        dq[...] = dot(score_grad[:, :rows], kv[:, :128]) + dot(
            score_grad[:, rows:], kv_there[:, :128]
        )
        for first, out in ((0, d_here), (rows, acc)):
            out[:, :128] += dot_tn(score_grad[:, first : first + rows], q[...])
            out[:, 128:] += dot_tn(probs_low[:, first : first + rows], do[...])

        @pl.when(step == n_blocks - 1)
        def _():
            d_there[...] = acc[...].astype(LOW)

    whole = lambda arr: pl.BlockSpec(arr.shape, lambda i: (0, 0))
    part = lambda arr: pl.BlockSpec((block, arr.shape[1]), lambda i: (i, 0))
    kept = pl.BlockSpec((rows, 2 * HEAD_DIM), lambda i: (0, 0))
    q_pos, q_doc, k_pos, k_doc = masks
    return pl.pallas_call(
        body,
        grid=(n_blocks,),
        in_specs=[
            part(query), whole(here), whole(there), part(out_grad), part(lse),
            part(q_pos), part(q_doc), whole(k_pos), whole(k_doc),
        ],
        out_specs=[pl.BlockSpec((block, HEAD_DIM), lambda i: (i, 0)), kept, kept],
        out_shape=[
            jax.ShapeDtypeStruct((rows, HEAD_DIM), F32),
            jax.ShapeDtypeStruct((rows, 2 * HEAD_DIM), F32),
            jax.ShapeDtypeStruct((rows, 2 * HEAD_DIM), LOW),
        ],
        scratch_shapes=[pltpu.VMEM((rows, 2 * HEAD_DIM), F32)],
        name="attend_back",
    )(query, here, there, out_grad, lse, *masks)


def update(state, pieces, lane_starts, used, first, done):
    rows, width = state[0].shape[1:]
    count, homes = pieces[0].shape[0], len(pieces)
    bias = 1.0 - adam_beta**STEP

    def body(starts, live, mas, one, two, *refs):
        grads, (new_mas, new_one, new_two, copy) = refs[:homes], refs[-4:]
        alive = live[pl.program_id(0) + first] > 0
        for home in range(homes):
            for half in range(2):
                at = (0, slice(None), pl.ds(pl.multiple_of(starts[2 * home + half], 128), 128))
                grad = grads[home][0, :, half * 128 : half * 128 + 128].astype(F32)
                grad = jnp.where(alive, grad, 0.0)
                mean = adam_beta * one[at] + (1.0 - adam_beta) * grad
                square = adam_beta * two[at] + (1.0 - adam_beta) * grad * grad
                ratio = (mean * (1.0 / bias)) / (jnp.sqrt(square * (1.0 / bias)) + adam_eps)
                old = mas[at]
                new = old - learn_rate * (ratio + decay_rate * old)
                new_mas[at] = new
                new_one[at] = mean
                new_two[at] = square
                copy[at] = new.astype(LOW)

    slot = pl.BlockSpec((1, rows, width), lambda i, s, u: (i + first, 0, 0))
    piece = pl.BlockSpec((1, rows, 256), lambda i, s, u: (i, 0, 0))
    shape = state[0].shape
    return pl.pallas_call(
        body,
        grid_spec=pltpu.PrefetchScalarGridSpec(
            num_scalar_prefetch=2,
            grid=(count,),
            in_specs=[slot] * 3 + [piece] * homes + [ANY_SPEC] * len(done),
            out_specs=[slot] * 4,
        ),
        out_shape=[jax.ShapeDtypeStruct(shape, F32)] * 3 + [jax.ShapeDtypeStruct(shape, LOW)],
        input_output_aliases={5 + homes + n: n for n in range(len(done))},
        name="update",
    )(lane_starts, used, *state, *pieces, *done)


def z_hops(piece, z_at):
    ups, downs = [piece], [piece]
    for step in (1, 2, 3):
        ups.append(shift_z(ups[-1], 1, range(step - 1, 3)))
        downs.append(shift_z(downs[-1], -1, range(1, 5 - step)))
    return [
        piece,
        jnp.where(z_at % 2 == 0, downs[1], ups[1]),
        jnp.where(z_at < 2, downs[2], ups[2]),
        jnp.where(
            z_at < 2,
            jnp.where(z_at == 0, downs[3], downs[1]),
            jnp.where(z_at == 2, ups[1], ups[3]),
        ),
    ]


def z_sums(kept, z_at):
    def own(target):
        bits = z_at ^ target
        return jnp.where(bits == 1, kept[1], jnp.where(bits == 2, kept[2], kept[3]))

    up = down = 0.0
    for far in (3, 2, 1):
        up = shift_z((own(z_at + far) + up).astype(LOW), 1, range(0, 4 - far)).astype(F32)
        down = shift_z((own(z_at - far) + down).astype(LOW), -1, range(far, 4)).astype(F32)
    return kept[0] + up + down


def gather_rows(piece, z_at=None):
    if z_at is None:
        near = [piece] + [swap(piece, 2 * k, 0) for k in (1, 2, 3)]
    else:
        near = z_hops(piece, z_at)
    blocks = []
    for part in near:
        pair = jnp.concatenate([part, swap(part, 0, 2)])
        blocks += [pair, swap(pair, 0, 1)]
    return jnp.concatenate(blocks)


def scatter_sum(partial_sum, z_at=None):
    quarter = partial_sum.shape[0] // 4
    half, rows = quarter // 2, quarter // 4
    kept = [None] * 4
    for k in (3, 2, 1, 0):
        chunk = partial_sum[quarter * k : quarter * (k + 1)]
        other = swap(chunk[half:].astype(LOW), 0, 1)
        pair = chunk[:half].astype(F32) + other.astype(F32)
        other = swap(pair[rows:].astype(LOW), 0, 2)
        kept[k] = pair[:rows] + other.astype(F32)
    if z_at is not None:
        return z_sums(kept, z_at), kept[0]
    total = kept[0]
    for k in (1, 2, 3):
        total = total + swap(kept[k].astype(LOW), 2 * k, 0).astype(F32)
    return total, kept[0]


def share_rows(piece, wt_index):
    rows = piece.shape[0]
    out = jnp.zeros((4 * rows,) + piece.shape[1:], piece.dtype)
    over_y = swap(piece, 0, 2)
    for bits, part in ((0, piece), (2, over_y), (1, swap(piece, 0, 1)), (3, swap(over_y, 0, 1))):
        out = lax.dynamic_update_slice(out, part, ((wt_index ^ bits) * rows, 0))
    return out


def rotate(values, cosine, sine):
    half = values.shape[-1] // 2
    first, second = values[:, :half], values[:, half:]
    return jnp.concatenate([first * cosine - second * sine, second * cosine + first * sine], axis=1)


def fast_shards(tokens, cotangent, doc_lengths, owners, master, moment_one, moment_two):
    ctx, wt = lax.axis_index("ctx"), lax.axis_index("wt")
    z_at, x_at = ctx // 2, ctx % 2
    tok_rows, width = tokens.shape
    cap, tile_rows, _ = master.shape
    n_tiles = owners.shape[0]
    rows = tok_rows // 4
    bits = jnp.arange(4, dtype=jnp.int32)
    homes = jnp.arange(8, dtype=jnp.int32) ^ ctx
    lane_starts = (
        ((2 * (homes % 2))[:, None] + jnp.arange(2, dtype=jnp.int32)) * 4 + (homes // 2)[:, None]
    ).reshape(-1) * 128

    owner_col = owners[:, 0]
    tile_ids = jnp.arange(n_tiles, dtype=jnp.int32)
    earlier = (owner_col[None, :] == owner_col[:, None]) & (tile_ids[None, :] < tile_ids[:, None])
    slot_in_owner = jnp.sum(earlier.astype(jnp.int32), axis=1)
    owner_bits = owner_col ^ ctx

    def to_cut_order(values):
        cut_vals = values.reshape(-1, width // 4, 4).transpose(0, 2, 1).reshape(-1, width)
        flipped = jnp.concatenate([cut_vals[:, width // 2 :], cut_vals[:, : width // 2]], axis=1)
        return jnp.where(x_at == 0, cut_vals, flipped)

    def from_cut_order(values):
        flipped = jnp.concatenate([values[:, width // 2 :], values[:, : width // 2]], axis=1)
        cut_vals = jnp.where(x_at == 0, values, flipped)
        return cut_vals.reshape(-1, 4, width // 4).transpose(0, 2, 1).reshape(-1, width)

    cut = lane_split(master, lane_starts)
    came = [cut[0]] + [swap(cut[k], k, 0) for k in range(1, 8)]
    tokens_later, grads_later = after(tokens, cut[0]), after(cotangent, cut[0])
    inputs = lax.dynamic_slice(tokens_later, (wt * rows, 0), (rows, width)).astype(F32)
    out_grad_low = lax.dynamic_slice(grads_later, (wt * rows, 0), (rows, width))
    normed, norm_back = jax.vjp(layer_norm, inputs)
    normed_cut = to_cut_order(normed.astype(LOW))
    normed_all = gather_rows(normed_cut, z_at)
    grad_all = gather_rows(out_grad_low, z_at)
    came[7], normed_all, grad_all = lax.optimization_barrier((came[7], normed_all, grad_all))
    w_qkv = pick_qkv(came, owner_bits[:12], slot_in_owner[:12])
    w_qkv_pair = swap(w_qkv, 1, 0)
    wanted = jnp.concatenate(
        [
            jnp.arange(16, 48, dtype=jnp.int32),
            12 + (z_at ^ bits),
            (48 + 4 * ((bits + 2 * x_at) % 4)[None, :] + (z_at ^ bits)[:, None]).reshape(-1),
        ]
    )
    wanted = after(wanted, w_qkv)
    home_gu, *sends = row_gather(
        came, owner_bits[wanted], slot_in_owner[wanted], [32] + [1] * 4 + [4] * 4
    )
    out_came = [sends[0]] + [swap(sends[m], 2 * m, 0) for m in (1, 2, 3)]
    down_here = [sends[4]] + [swap(sends[4 + m], 2 * m, 0) for m in (1, 2, 3)]
    down_here = jnp.stack(down_here)

    block_z = z_at ^ bits
    block_w = wt ^ jnp.array([0, 2, 1, 3], jnp.int32)

    def group_positions(x_index):
        starts = (2 * block_z + x_index)[:, None] * tok_rows + block_w[None, :] * rows
        return (starts.reshape(-1)[:, None] + jnp.arange(rows, dtype=jnp.int32)).reshape(-1)

    q_pos = group_positions(x_at)
    k_pos = jnp.concatenate([q_pos, group_positions(1 - x_at)])
    doc_starts = jnp.cumsum(doc_lengths) - doc_lengths
    q_doc, k_doc = doc_index(q_pos, doc_starts), doc_index(k_pos, doc_starts)
    masks = (q_pos[:, None], q_doc[:, None], k_pos[None, :], k_doc[None, :])
    freqs = rope_base ** (-jnp.arange(HEAD_DIM // 2, dtype=F32) * (2.0 / HEAD_DIM))
    angles = q_pos.astype(F32)[:, None] * freqs[None, :]
    cosine, sine = jnp.cos(angles), jnp.sin(angles)

    half = width // 2
    qkv = dot(normed_all[:, :half], w_qkv) + dot(normed_all[:, half:], w_qkv_pair)
    query = rotate(qkv[:, :128], cosine, sine).astype(LOW)
    kv_here = jnp.concatenate(
        [rotate(qkv[:, 128:256], cosine, sine).astype(LOW), qkv[:, 256:].astype(LOW)], axis=1
    )
    kv_there = swap(kv_here, 1, 0)
    out_here = after(jnp.stack(out_came), kv_here)
    out_there = swap(out_here, 1, 0)
    att_low, lse = attend(query, kv_here, kv_there, masks, 4)
    w_out = lane_join(out_here, out_there, lane_starts).reshape(tile_rows, width)

    pair_gu = swap(after(home_gu, kv_there), 1, 0)
    w_down = lane_join(down_here, swap(after(down_here, kv_there), 1, 0), lane_starts)
    w_down = w_down.reshape(512, width)
    w_gu = jnp.concatenate(
        [part.reshape(width, 256) for half_gu in (home_gu, pair_gu) for part in (half_gu[:16], half_gu[16:])],
        axis=1,
    )
    att_out, _ = scatter_sum(dot(att_low, w_out).astype(LOW))
    residual = inputs + att_out

    normed_two, norm_two_back = jax.vjp(layer_norm, residual)
    two_all = gather_rows(normed_two.astype(LOW))
    gu = dot(two_all, w_gu)
    gate = jnp.concatenate([gu[:, :256], gu[:, 512:768]], axis=1)
    up = jnp.concatenate([gu[:, 256:512], gu[:, 768:]], axis=1)
    gate_sig = jax.nn.sigmoid(gate)
    silu = gate * gate_sig
    hidden = (silu * up).astype(LOW)

    hidden_grad = dot_nt(grad_all, w_down)
    grad_gate = (hidden_grad * up * gate_sig * (1.0 + gate * (1.0 - gate_sig))).astype(LOW)
    grad_up = (hidden_grad * silu).astype(LOW)
    grad_gu = jnp.concatenate(
        [grad_gate[:, :256], grad_up[:, :256], grad_gate[:, 256:], grad_up[:, 256:]], axis=1
    )
    two_grad, begun = scatter_sum(dot_nt(grad_gu, w_gu).astype(LOW))
    hidden_later, grad_gu_later = lax.optimization_barrier((hidden, grad_gu, begun))[:2]
    grad_w_gu = dot_tn(two_all, grad_gu_later)
    gu_back = swap(grad_w_gu[:, 512:].astype(LOW), 1, 0)
    grad_w_down = dot_tn(hidden_later, grad_all)

    resid_grad = out_grad_low.astype(F32) + norm_two_back(two_grad)[0]
    resid_all = gather_rows(resid_grad.astype(LOW))
    gu_sum = (grad_w_gu[:, :512] + gu_back.astype(F32)).astype(LOW)
    down_came = return_halves(grad_w_down.reshape(4, tile_rows, width), lane_starts)

    part_slots = cap // 2
    send_to = owner_bits + 8 * (slot_in_owner // part_slots)
    send_row = slot_in_owner % part_slots
    place = jnp.stack([z_at, x_at])
    sends = place_mlp(gu_sum, down_came, send_to, send_row, place, 16, part_slots)

    att_grad = dot_nt(resid_all, w_out).astype(LOW)
    out_grad_came = return_halves(
        dot_tn(att_low, resid_all).reshape(1, tile_rows, width), lane_starts
    )
    query_grad, kv_grad, kv_grad_there = attend_back(
        query, kv_here, kv_there, att_grad, lse, masks, 4
    )
    kv_grad_back = swap(kv_grad_there, 1, 0)
    kv_grad = kv_grad + kv_grad_back.astype(F32)
    qkv_grad = jnp.concatenate(
        [
            rotate(query_grad, cosine, -sine),
            rotate(kv_grad[:, :128], cosine, -sine),
            kv_grad[:, 128:],
        ],
        axis=1,
    ).astype(LOW)
    qkv_back = swap(dot_tn(normed_all[:, half:], qkv_grad).astype(LOW), 1, 0)
    qkv_sum = (dot_tn(normed_all[:, :half], qkv_grad) + qkv_back.astype(F32)).astype(LOW)
    sends = place_attention(sends, qkv_sum, out_grad_came, send_to, send_row, place)

    qkv_grad_later, hidden_last = lax.optimization_barrier((qkv_grad, hidden, sends[0]))[:2]
    one_part = jnp.concatenate(
        [dot_nt(qkv_grad_later, w_qkv), dot_nt(qkv_grad_later, w_qkv_pair)], axis=1
    )
    down_part = dot(hidden_last, w_down)
    one_grad = from_cut_order(scatter_sum(one_part.astype(LOW), z_at)[0])
    input_grad = resid_grad + norm_back(one_grad)[0]
    input_grad = share_rows(input_grad.astype(LOW), wt).astype(F32)
    down, _ = scatter_sum(down_part.astype(LOW), z_at)
    output = share_rows((residual + down).astype(LOW), wt)

    slot_range = jnp.arange(cap, dtype=jnp.int32) + ctx * cap
    used = jnp.any(
        (owner_col * cap + slot_in_owner)[None, :] == slot_range[:, None], axis=1
    ).astype(jnp.int32)
    state, done = (master, moment_one, moment_two), ()
    for part in range(2):
        mine = sends[8 * part : 8 * part + 8]
        pieces = [mine[0]] + [swap(mine[k], k, 0) for k in range(1, 8)]
        done = tuple(update(state, pieces, lane_starts, used, part * part_slots, done))
    return (output, input_grad) + done


def choose_shards(*args):
    sizes = (lax.axis_size("ctx"), lax.axis_size("wt"), args[0].shape, args[4].shape[1:])
    if sizes == (8, 4, (256, 2048), (128, 2048)) and args[3].shape[0] == 64:
        return fast_shards(*args)
    return general_shards(*args)


def solution(mesh):
    placed = (
        P("ctx", None),
        P("ctx", None),
        P(),
        P(),
        P("ctx", None, "wt"),
        P("ctx", None, "wt"),
        P("ctx", None, "wt"),
    )
    return jax.shard_map(
        choose_shards,
        mesh=mesh,
        in_specs=placed,
        out_specs=(
            P("ctx", None),
            P("ctx", None),
            P("ctx", None, "wt"),
            P("ctx", None, "wt"),
            P("ctx", None, "wt"),
            P("ctx", None, "wt"),
        ),
        check_vma=False,
    )
```

```python
from functools import partial
import math

import jax
import jax.numpy as jnp
from jax import lax
from jax.experimental import pallas as pl
from jax.experimental.pallas import tpu as pltpu
from jax.sharding import PartitionSpec as P

HEAD_DIM = 128
STEP = 3


adam_beta = 0.5
learn_rate = 0.01
decay_rate = 0.1
adam_eps = 1e-08
norm_eps = 1e-05
neg_fill = -1e30
rope_base = 10000.0


def from_behind(x, axis, by):
    count = lax.axis_size(axis)
    pairs = [(i, i + by) for i in range(count) if 0 <= i + by < count]
    return lax.ppermute(x, axis, pairs)


def from_behind_2(value, axis, steps):
    count = lax.axis_size(axis)
    pairs = [(source, (source + steps) % count) for source in range(count)]
    return lax.ppermute(value, axis, pairs)


def layer_norm(values):
    center = values - jnp.mean(values, axis=-1, keepdims=True)
    spread = jnp.mean(center * center, axis=-1, keepdims=True)
    return center * lax.rsqrt(spread + norm_eps)


def rotary(values, positions):
    half_dim = values.shape[-1] // 2
    frequencies = rope_base ** (-jnp.arange(half_dim, dtype=jnp.float32) * (2.0 / values.shape[-1]))
    angles = positions.astype(jnp.float32)[:, None] * frequencies[None, :]
    cosine = jnp.cos(angles)[:, None, :]
    sine_vals = jnp.sin(angles)[:, None, :]
    first_half = values[..., :half_dim]
    second_half = values[..., half_dim:]
    return jnp.concatenate(
        [
            first_half * cosine - second_half * sine_vals,
            second_half * cosine + first_half * sine_vals,
        ],
        axis=-1,
    )


def doc_index(positions, doc_starts):
    return jnp.sum((positions[:, None] >= doc_starts[None, :]).astype(jnp.int32), axis=1) - 1


def heads_dot(spec, left, right):
    return jnp.einsum(spec, left, right, preferred_element_type=jnp.float32)


def general_shards(tokens, cotangent, doc_lengths, owners, master, moment_one, moment_two):
    n_ctx = lax.axis_size("ctx")
    n_wt = lax.axis_size("wt")
    ctx_index = lax.axis_index("ctx")
    tok_rows, width = tokens.shape
    cap_slots, tile_rows, tile_width = master.shape
    n_tiles = owners.shape[0]
    head_dim = HEAD_DIM
    owner_col = owners[:, 0]
    tile_ids = jnp.arange(n_tiles, dtype=jnp.int32)
    earlier = (owner_col[None, :] == owner_col[:, None]) & (tile_ids[None, :] < tile_ids[:, None])
    slot_ids = owner_col * cap_slots + jnp.sum(earlier.astype(jnp.int32), axis=1)
    every_slot = lax.all_gather(master.astype(jnp.bfloat16), "ctx", axis=0, tiled=True)
    flat_w = every_slot[slot_ids].reshape(-1)
    local_width = width // n_wt
    heads_local = local_width // head_dim
    part_q = width * local_width
    ff_local = (flat_w.shape[0] - 4 * part_q) // (3 * width)
    part_f = width * ff_local
    w_qkv = flat_w[: 3 * part_q].reshape(3, width, local_width)
    w_out = flat_w[3 * part_q : 4 * part_q].reshape(local_width, width)
    w_gateup = flat_w[4 * part_q : 4 * part_q + 2 * part_f].reshape(2, width, ff_local)
    w_down = flat_w[4 * part_q + 2 * part_f :].reshape(ff_local, width)
    positions = ctx_index * tok_rows + jnp.arange(tok_rows, dtype=jnp.int32)
    doc_starts = jnp.cumsum(doc_lengths) - doc_lengths
    q_docs = doc_index(positions, doc_starts)
    score_scale = 1.0 / math.sqrt(head_dim)
    inputs = tokens.astype(jnp.float32)
    normed, norm_back = jax.vjp(layer_norm, inputs)
    normed_low = normed.astype(jnp.bfloat16)
    qkv_vals = heads_dot("td,jde->jte", normed_low, w_qkv)
    shaped = qkv_vals.reshape(3, tok_rows, heads_local, head_dim)
    rope_here = partial(rotary, positions=positions)
    qk_rot, rope_back = jax.vjp(rope_here, jnp.concatenate([shaped[0], shaped[1]], axis=1))
    q_low = qk_rot[:, :heads_local].astype(jnp.bfloat16)
    k_low = qk_rot[:, heads_local:].astype(jnp.bfloat16)
    v_low = shaped[2].astype(jnp.bfloat16)

    def masked_scores(key_block, key_pos, key_docs):
        raw_scores = heads_dot("qhd,khd->hqk", q_low, key_block)
        visible_mask = (key_pos[None, :] <= positions[:, None]) & (
            key_docs[None, :] == q_docs[:, None]
        )
        return (jnp.where(visible_mask[None], raw_scores * score_scale, neg_fill), visible_mask)

    def over_blocks(kv_piece, first_row, update_fn, running):
        key_count = kv_piece[0].shape[0]
        block_len = math.gcd(key_count, 512)
        n_blocks = key_count // block_len
        split_kv = tuple(
            (member.reshape((n_blocks, block_len) + member.shape[1:]) for member in kv_piece)
        )

        def step_fn(block_state, inputs_here):
            block_idx, block_vals = inputs_here
            block_row = first_row + block_idx * block_len
            key_pos = block_row + jnp.arange(block_len, dtype=jnp.int32)
            key_docs = doc_index(key_pos, doc_starts)
            block_state = update_fn(block_state, block_vals, key_pos, key_docs, block_row)
            return (block_state, None)

        running, _ = lax.scan(step_fn, running, (jnp.arange(n_blocks, dtype=jnp.int32), split_kv))
        return running

    def norm_update(block_state, block_vals, key_pos, key_docs, block_row):
        row_top, row_total = block_state
        scores, visible_mask = masked_scores(block_vals[0], key_pos, key_docs)
        new_top = jnp.maximum(row_top, jnp.max(scores, axis=-1))
        weights_exp = jnp.where(visible_mask[None], jnp.exp(scores - new_top[:, :, None]), 0.0)
        return (new_top, row_total * jnp.exp(row_top - new_top) + jnp.sum(weights_exp, axis=-1))

    start_top = jnp.full((heads_local, tok_rows), neg_fill, jnp.float32)
    start_total = jnp.zeros((heads_local, tok_rows), jnp.float32)
    row_top, row_total = over_blocks(
        (lax.all_gather(k_low, "ctx", axis=0, tiled=True),),
        jnp.int32(0),
        norm_update,
        (start_top, start_total),
    )
    log_sum = row_top + jnp.log(row_total)

    def block_probs(key_block, key_pos, key_docs):
        scores, visible_mask = masked_scores(key_block, key_pos, key_docs)
        return jnp.where(visible_mask[None], jnp.exp(scores - log_sum[:, :, None]), 0.0)

    def value_update(block_state, block_vals, key_pos, key_docs, block_row):
        prob_vals = block_probs(block_vals[0], key_pos, key_docs)
        return block_state + heads_dot(
            "hqk,khd->qhd", prob_vals.astype(jnp.bfloat16), block_vals[1]
        )

    zero_heads = jnp.zeros((tok_rows, heads_local, head_dim), jnp.float32)
    attended = over_blocks(
        (
            lax.all_gather(k_low, "ctx", axis=0, tiled=True),
            lax.all_gather(v_low, "ctx", axis=0, tiled=True),
        ),
        jnp.int32(0),
        value_update,
        zero_heads,
    )
    att_low = attended.reshape(tok_rows, local_width).astype(jnp.bfloat16)
    attn_part = jnp.dot(att_low, w_out, preferred_element_type=jnp.float32)
    residual = inputs + lax.psum(attn_part.astype(jnp.bfloat16), "wt").astype(jnp.float32)
    normed_two, norm_two_back = jax.vjp(layer_norm, residual)
    normed_two_low = normed_two.astype(jnp.bfloat16)
    gateup_vals = heads_dot("td,jde->jte", normed_two_low, w_gateup)
    gate_vals = gateup_vals[0]
    up_vals = gateup_vals[1]
    gate_sig = jax.nn.sigmoid(gate_vals)
    silu_vals = gate_vals * gate_sig
    hidden_low = (silu_vals * up_vals).astype(jnp.bfloat16)
    mlp_part = jnp.dot(hidden_low, w_down, preferred_element_type=jnp.float32)
    output = (residual + lax.psum(mlp_part.astype(jnp.bfloat16), "wt").astype(jnp.float32)).astype(
        jnp.bfloat16
    )
    out_grad = cotangent.astype(jnp.float32)
    grad_down = heads_dot("tf,td->fd", hidden_low, cotangent)
    grad_hidden = heads_dot("td,fd->tf", cotangent, w_down)
    grad_gate = grad_hidden * up_vals * gate_sig * (1.0 + gate_vals * (1.0 - gate_sig))
    grad_up = grad_hidden * silu_vals
    grad_gu_low = jnp.stack([grad_gate, grad_up]).astype(jnp.bfloat16)
    grad_gateup = heads_dot("td,jte->jde", normed_two_low, grad_gu_low)
    norm_two_part = heads_dot("jte,jde->td", grad_gu_low, w_gateup)
    norm_two_grad = lax.psum(norm_two_part.astype(jnp.bfloat16), "wt").astype(jnp.float32)
    resid_grad = out_grad + norm_two_back(norm_two_grad)[0]
    resid_low = resid_grad.astype(jnp.bfloat16)
    grad_out = heads_dot("tc,td->cd", att_low, resid_low)
    att_grad = heads_dot("td,cd->tc", resid_low, w_out)
    att_grad_low = att_grad.astype(jnp.bfloat16).reshape(tok_rows, heads_local, head_dim)
    row_delta = jnp.sum(att_grad_low * attended, axis=-1).T

    def grad_block(block_vals, key_pos, key_docs):
        prob_vals = block_probs(block_vals[0], key_pos, key_docs)
        value_grad = heads_dot("hqk,qhd->khd", prob_vals.astype(jnp.bfloat16), att_grad_low)
        prob_grad = heads_dot("qhd,khd->hqk", att_grad_low, block_vals[1])
        raw_grad = (prob_vals * (prob_grad - row_delta[:, :, None]) * score_scale).astype(
            jnp.bfloat16
        )
        query_grad = heads_dot("hqk,khd->qhd", raw_grad, block_vals[0])
        key_grad = heads_dot("hqk,qhd->khd", raw_grad, q_low)
        return (query_grad, key_grad, value_grad)

    def add_rows(target, addend):
        return target + addend

    def cycle_step(turn_idx, cycle_state):
        query_acc, key_cur, value_cur, key_acc, value_acc = cycle_state
        anchor = (ctx_index - turn_idx) % n_ctx

        def cycle_update(block_state, block_vals, key_pos, key_docs, block_row):
            q_acc, k_acc, v_acc = block_state
            query_grad, key_grad, value_grad = grad_block(block_vals, key_pos, key_docs)
            return (q_acc + query_grad, add_rows(k_acc, key_grad), add_rows(v_acc, value_grad))

        query_acc, key_acc, value_acc = over_blocks(
            (key_cur, value_cur), anchor * tok_rows, cycle_update, (query_acc, key_acc, value_acc)
        )
        key_cur, value_cur = from_behind((key_cur, value_cur), "ctx", 1)
        key_acc, value_acc = (
            from_behind_2(key_acc.astype(jnp.bfloat16), "ctx", 1).astype(key_acc.dtype),
            from_behind_2(value_acc.astype(jnp.bfloat16), "ctx", 1).astype(value_acc.dtype),
        )
        return (query_acc, key_cur, value_cur, key_acc, value_acc)

    cycle_start = (zero_heads, k_low, v_low, zero_heads, zero_heads)
    query_acc, _, _, key_acc, value_acc = lax.fori_loop(0, n_ctx, cycle_step, cycle_start)
    qk_pre_grad = rope_back(jnp.concatenate([query_acc, key_acc], axis=1))[0]
    qkv_grad_low = jnp.stack(
        [
            qk_pre_grad[:, :heads_local].reshape(tok_rows, local_width),
            qk_pre_grad[:, heads_local:].reshape(tok_rows, local_width),
            value_acc.reshape(tok_rows, local_width),
        ]
    ).astype(jnp.bfloat16)
    grad_qkv = heads_dot("td,jte->jde", normed_low, qkv_grad_low)
    norm_one_part = heads_dot("jte,jde->td", qkv_grad_low, w_qkv)
    norm_one_grad = lax.psum(norm_one_part.astype(jnp.bfloat16), "wt").astype(jnp.float32)
    input_grad = resid_grad + norm_back(norm_one_grad)[0]
    grad_tiles = jnp.concatenate(
        [grad_qkv.reshape(-1), grad_out.reshape(-1), grad_gateup.reshape(-1), grad_down.reshape(-1)]
    ).reshape(n_tiles, tile_rows, tile_width)
    slot_range = jnp.arange(n_ctx * cap_slots, dtype=jnp.int32)
    matches = slot_ids[None, :] == slot_range[:, None]
    tile_of_slot = jnp.sum(jnp.where(matches, tile_ids[None, :], 0), axis=1)
    slot_used = jnp.any(matches, axis=1)
    slot_grads = lax.psum_scatter(
        jnp.where(slot_used[:, None, None], grad_tiles[tile_of_slot], 0.0).astype(jnp.bfloat16),
        "ctx",
        scatter_dimension=0,
        tiled=True,
    ).astype(jnp.float32)
    new_one = adam_beta * moment_one + (1.0 - adam_beta) * slot_grads
    new_two = adam_beta * moment_two + (1.0 - adam_beta) * slot_grads * slot_grads
    bias_one = 1.0 - adam_beta**STEP
    bias_two = 1.0 - adam_beta**STEP
    step_ratio = new_one / bias_one / (jnp.sqrt(new_two / bias_two) + adam_eps)
    new_master = master - learn_rate * (step_ratio + decay_rate * master)
    return (output, input_grad, new_master, new_one, new_two, new_master.astype(jnp.bfloat16))


AXES = ("ctx", "wt")
LOW = jnp.bfloat16
F32 = jnp.float32


def swap(value, ctx_bits, wt_bits):
    n_ctx, n_wt = lax.axis_size("ctx"), lax.axis_size("wt")
    pairs = [
        (c * n_wt + w, (c ^ ctx_bits) * n_wt + (w ^ wt_bits))
        for c in range(n_ctx)
        for w in range(n_wt)
    ]
    return lax.ppermute(value, AXES, pairs)


def dot(left, right):
    return jnp.dot(left, right, preferred_element_type=F32)


def dot_tn(left, right):
    return lax.dot_general(left, right, (((0,), (0,)), ((), ())), preferred_element_type=F32)


def dot_nt(left, right):
    return lax.dot_general(left, right, (((1,), (1,)), ((), ())), preferred_element_type=F32)


def lane_split(value, lane_starts):
    count, rows, width = value.shape
    homes = lane_starts.shape[0] // 2

    def body(starts, src, *outs):
        for home in range(homes):
            for half in range(2):
                start = pl.multiple_of(starts[2 * home + half], 128)
                outs[home][0, :, half * 128 : half * 128 + 128] = src[
                    0, :, pl.ds(start, 128)
                ].astype(LOW)

    return pl.pallas_call(
        body,
        grid_spec=pltpu.PrefetchScalarGridSpec(
            num_scalar_prefetch=1,
            grid=(count,),
            in_specs=[pl.BlockSpec((1, rows, width), lambda i, s: (i, 0, 0))],
            out_specs=[pl.BlockSpec((1, rows, 256), lambda i, s: (i, 0, 0))] * homes,
        ),
        out_shape=[jax.ShapeDtypeStruct((count, rows, 256), LOW)] * homes,
        name="lane_split",
    )(lane_starts, value)


def lane_join(own, other, lane_starts):
    homes, count, rows, _ = own.shape
    width = homes * 512

    def body(starts, own_ref, other_ref, out):
        for home in range(homes):
            for side, ref in ((0, own_ref), (1, other_ref)):
                for half in range(2):
                    start = pl.multiple_of(starts[4 * home + 2 * side + half], 128)
                    out[0, :, pl.ds(start, 128)] = ref[home, 0, :, half * 128 : half * 128 + 128]

    return pl.pallas_call(
        body,
        grid_spec=pltpu.PrefetchScalarGridSpec(
            num_scalar_prefetch=1,
            grid=(count,),
            in_specs=[
                pl.BlockSpec((homes, 1, rows, 256), lambda i, s: (0, i, 0, 0)),
                pl.BlockSpec(
                    (homes, 1, rows, 256), lambda i, s: (0, (i + count // 2) % count, 0, 0)
                ),
            ],
            out_specs=pl.BlockSpec((1, rows, width), lambda i, s: (i, 0, 0)),
        ),
        out_shape=jax.ShapeDtypeStruct((count, rows, width), LOW),
        name="lane_join",
    )(lane_starts, own, other)


def lane_halves(value, lane_starts):
    count, rows, width = value.shape
    homes = width // 512

    def body(starts, src, own_ref, other_ref):
        for home in range(homes):
            for side, ref in ((0, own_ref), (1, other_ref)):
                for half in range(2):
                    start = pl.multiple_of(starts[4 * home + 2 * side + half], 128)
                    ref[home, 0, :, half * 128 : half * 128 + 128] = src[
                        0, :, pl.ds(start, 128)
                    ].astype(ref.dtype)

    return pl.pallas_call(
        body,
        grid_spec=pltpu.PrefetchScalarGridSpec(
            num_scalar_prefetch=1,
            grid=(count,),
            in_specs=[pl.BlockSpec((1, rows, width), lambda i, s: (i, 0, 0))],
            out_specs=[
                pl.BlockSpec((homes, 1, rows, 256), lambda i, s: (0, i, 0, 0)),
                pl.BlockSpec(
                    (homes, 1, rows, 256), lambda i, s: (0, (i + count // 2) % count, 0, 0)
                ),
            ],
        ),
        out_shape=[
            jax.ShapeDtypeStruct((homes, count, rows, 256), dtype) for dtype in (F32, LOW)
        ],
        name="lane_halves",
    )(lane_starts, value)


def return_halves(grad, lane_starts):
    own, other = lane_halves(grad, lane_starts)
    back = swap(other, 1, 0)
    sums = [(own[m] + back[m].astype(F32)).astype(LOW) for m in range(4)]
    return [sums[0]] + [swap(sums[m], 2 * m, 0) for m in (1, 2, 3)]


VMEM_SPEC = pl.BlockSpec(memory_space=pltpu.VMEM)
SMEM_SPEC = pl.BlockSpec(memory_space=pltpu.SMEM)
ANY_SPEC = pl.BlockSpec(memory_space=pl.ANY)


def pick_qkv(came, picked, rows):
    n_src = len(came)

    def body(which, where, *refs):
        srcs, out = refs[:n_src], refs[n_src]

        def copy(tile, carry):
            for n in range(n_src):

                @pl.when(which[tile] == n)
                def _(n=n):
                    for half in range(2):
                        row = pl.multiple_of(half * 512 + (tile % 4) * 128, 128)
                        lane = pl.multiple_of((tile // 4) * 128, 128)
                        out[pl.ds(row, 128), pl.ds(lane, 128)] = srcs[n][
                            where[tile], :, half * 128 : half * 128 + 128
                        ]

            return carry

        lax.fori_loop(0, 12, copy, 0)

    return pl.pallas_call(
        body,
        in_specs=[SMEM_SPEC, SMEM_SPEC] + [VMEM_SPEC] * n_src,
        out_specs=VMEM_SPEC,
        out_shape=jax.ShapeDtypeStruct((1024, 384), LOW),
        name="pick_qkv",
    )(picked, rows, *came)


def row_gather(sources, picked, rows, sizes):
    total = sum(sizes)
    n_src = len(sources)

    def body(which, where, *refs):
        srcs, outs, sem = refs[:n_src], refs[n_src:-1], refs[-1]
        first = 0
        for out, size in zip(outs, sizes):

            def start(j, carry, out=out, first=first):
                t = first + j
                for n in range(n_src):

                    @pl.when(which[t] == n)
                    def _(n=n):
                        pltpu.make_async_copy(srcs[n].at[where[t]], out.at[j], sem.at[t]).start()

                return carry

            lax.fori_loop(0, size, start, 0)
            first += size
        first = 0
        for out, size in zip(outs, sizes):

            def finish(j, carry, out=out, first=first):
                pltpu.make_async_copy(srcs[0].at[0], out.at[j], sem.at[first + j]).wait()
                return carry

            lax.fori_loop(0, size, finish, 0)
            first += size

    tail = sources[0].shape[1:]
    return pl.pallas_call(
        body,
        in_specs=[SMEM_SPEC, SMEM_SPEC] + [VMEM_SPEC] * n_src,
        out_specs=[ANY_SPEC] * len(sizes),
        out_shape=[jax.ShapeDtypeStruct((size,) + tail, LOW) for size in sizes],
        scratch_shapes=[pltpu.SemaphoreType.DMA((total,))],
        name="row_gather",
    )(picked, rows, *sources)


def send_tile(src, tile, to, row, outs, sem):
    for n, out in enumerate(outs):

        @pl.when(to[tile] == n)
        def _(out=out):
            pltpu.make_async_copy(src, out.at[row[tile]], sem.at[tile]).start()


def place_mlp(gate_up, downs, to, row, place, count, size):
    def body(to_ref, row_ref, z_ref, gu_ref, *refs):
        down_refs, outs, sem = refs[:4], refs[4:-1], refs[-1]
        down_tile = lambda m, k: 48 + 4 * ((k + 2 * z_ref[1]) % 4) + (z_ref[0] ^ m)

        def start(j, carry):
            at = pl.ds(pl.multiple_of(128 * j, 128), 128)
            for half in range(2):
                src = gu_ref.at[at, pl.ds(256 * half, 256)]
                send_tile(src, 16 + 16 * half + j, to_ref, row_ref, outs, sem)
            return carry

        lax.fori_loop(0, 16, start, 0)
        for m in range(4):

            def start_down(k, carry, m=m):
                send_tile(down_refs[m].at[k], down_tile(m, k), to_ref, row_ref, outs, sem)
                return carry

            lax.fori_loop(0, 4, start_down, 0)

        def finish(tile, carry):
            pltpu.make_async_copy(down_refs[0].at[0], outs[0].at[0], sem.at[tile]).wait()
            return carry

        lax.fori_loop(16, 64, finish, 0)

    return pl.pallas_call(
        body,
        in_specs=[SMEM_SPEC] * 3 + [VMEM_SPEC] * 5,
        out_specs=[ANY_SPEC] * count,
        out_shape=[jax.ShapeDtypeStruct((size, 128, 256), LOW)] * count,
        scratch_shapes=[pltpu.SemaphoreType.DMA((64,))],
        name="place_mlp",
    )(to, row, place, gate_up, *downs)


def place_attention(buffers, qkv, outs_from, to, row, place):
    count = len(buffers)

    def body(to_ref, row_ref, z_ref, qkv_ref, *refs):
        out_refs, outs = refs[:4], refs[4 + count : 4 + 2 * count]
        tiles, sem = refs[-2:]

        def start(tile, carry):
            lane = pl.multiple_of((tile // 4) * 128, 128)
            for half in range(2):
                at = pl.ds(pl.multiple_of(half * 512 + (tile % 4) * 128, 128), 128)
                tiles[tile, :, half * 128 : half * 128 + 128] = qkv_ref[at, pl.ds(lane, 128)]
            return carry

        lax.fori_loop(0, 12, start, 0)

        def start_copy(tile, carry):
            send_tile(tiles.at[tile], tile, to_ref, row_ref, outs, sem)
            return carry

        for m in range(4):
            send_tile(out_refs[m].at[0], 12 + (z_ref[0] ^ m), to_ref, row_ref, outs, sem)
        lax.fori_loop(0, 12, start_copy, 0)

        def finish(tile, carry):
            pltpu.make_async_copy(tiles.at[0], outs[0].at[0], sem.at[tile]).wait()
            return carry

        lax.fori_loop(0, 16, finish, 0)

    return pl.pallas_call(
        body,
        in_specs=[SMEM_SPEC] * 3 + [VMEM_SPEC] * 5 + [ANY_SPEC] * count,
        out_specs=[ANY_SPEC] * count,
        out_shape=[jax.ShapeDtypeStruct(buf.shape, buf.dtype) for buf in buffers],
        scratch_shapes=[pltpu.VMEM((12, 128, 256), LOW), pltpu.SemaphoreType.DMA((16,))],
        input_output_aliases={8 + n: n for n in range(count)},
        name="place_attention",
    )(to, row, place, qkv, *outs_from, *buffers)


def after(value, *earlier):
    return lax.optimization_barrier((value,) + earlier)[0]


def key_scores(q, here, there, masks):
    qp, qd, kp, kd = masks
    raw = jnp.concatenate([dot_nt(q, here[:, :128]), dot_nt(q, there[:, :128])], axis=1)
    seen = (kp[...] <= qp[...]) & (kd[...] == qd[...])
    return jnp.where(seen, raw * (1.0 / math.sqrt(HEAD_DIM)), neg_fill)


def attend(query, here, there, masks, n_blocks):
    rows = query.shape[0]
    block = rows // n_blocks

    def body(q, kv, kv_there, qp, qd, kp, kd, out, lse):
        scores = key_scores(q[...], kv[...], kv_there[...], (qp, qd, kp, kd))
        top = jnp.max(scores, axis=1, keepdims=True)
        weights = jnp.exp(scores - top)
        total = jnp.sum(weights, axis=1, keepdims=True)
        probs = (weights * (1.0 / total)).astype(LOW)
        mixed = dot(probs[:, :rows], kv[:, 128:]) + dot(probs[:, rows:], kv_there[:, 128:])
        out[...] = mixed.astype(LOW)
        lse[...] = top + jnp.log(total)

    whole = lambda arr: pl.BlockSpec(arr.shape, lambda i: (0, 0))
    part = lambda arr: pl.BlockSpec((block, arr.shape[1]), lambda i: (i, 0))
    q_pos, q_doc, k_pos, k_doc = masks
    return pl.pallas_call(
        body,
        grid=(n_blocks,),
        in_specs=[
            part(query), whole(here), whole(there), part(q_pos), part(q_doc), whole(k_pos), whole(k_doc),
        ],
        out_specs=[
            pl.BlockSpec((block, HEAD_DIM), lambda i: (i, 0)),
            pl.BlockSpec((block, 1), lambda i: (i, 0)),
        ],
        out_shape=[
            jax.ShapeDtypeStruct((rows, HEAD_DIM), LOW),
            jax.ShapeDtypeStruct((rows, 1), F32),
        ],
        name="attend",
    )(query, here, there, *masks)


def attend_back(query, here, there, out_grad, lse, masks, n_blocks):
    rows = query.shape[0]
    block = rows // n_blocks

    def body(q, kv, kv_there, do, ls, qp, qd, kp, kd, dq, d_here, d_there, acc):
        step = pl.program_id(0)

        @pl.when(step == 0)
        def _():
            d_here[...] = jnp.zeros_like(d_here)
            acc[...] = jnp.zeros_like(acc)

        scores = key_scores(q[...], kv[...], kv_there[...], (qp, qd, kp, kd))
        probs = jnp.exp(scores - ls[...])
        prob_grad = jnp.concatenate(
            [dot_nt(do[...], kv[:, 128:]), dot_nt(do[...], kv_there[:, 128:])], axis=1
        )
        delta = jnp.sum(probs * prob_grad, axis=1, keepdims=True)
        score_grad = (probs * (prob_grad - delta) * (1.0 / math.sqrt(HEAD_DIM))).astype(LOW)
        probs_low = probs.astype(LOW)
        dq[...] = dot(score_grad[:, :rows], kv[:, :128]) + dot(
            score_grad[:, rows:], kv_there[:, :128]
        )
        for first, out in ((0, d_here), (rows, acc)):
            out[:, :128] += dot_tn(score_grad[:, first : first + rows], q[...])
            out[:, 128:] += dot_tn(probs_low[:, first : first + rows], do[...])

        @pl.when(step == n_blocks - 1)
        def _():
            d_there[...] = acc[...].astype(LOW)

    whole = lambda arr: pl.BlockSpec(arr.shape, lambda i: (0, 0))
    part = lambda arr: pl.BlockSpec((block, arr.shape[1]), lambda i: (i, 0))
    kept = pl.BlockSpec((rows, 2 * HEAD_DIM), lambda i: (0, 0))
    q_pos, q_doc, k_pos, k_doc = masks
    return pl.pallas_call(
        body,
        grid=(n_blocks,),
        in_specs=[
            part(query), whole(here), whole(there), part(out_grad), part(lse),
            part(q_pos), part(q_doc), whole(k_pos), whole(k_doc),
        ],
        out_specs=[pl.BlockSpec((block, HEAD_DIM), lambda i: (i, 0)), kept, kept],
        out_shape=[
            jax.ShapeDtypeStruct((rows, HEAD_DIM), F32),
            jax.ShapeDtypeStruct((rows, 2 * HEAD_DIM), F32),
            jax.ShapeDtypeStruct((rows, 2 * HEAD_DIM), LOW),
        ],
        scratch_shapes=[pltpu.VMEM((rows, 2 * HEAD_DIM), F32)],
        name="attend_back",
    )(query, here, there, out_grad, lse, *masks)


def update(state, pieces, lane_starts, used, first, done):
    rows, width = state[0].shape[1:]
    count, homes = pieces[0].shape[0], len(pieces)
    bias = 1.0 - adam_beta**STEP

    def body(starts, live, mas, one, two, *refs):
        grads, (new_mas, new_one, new_two, copy) = refs[:homes], refs[-4:]
        alive = live[pl.program_id(0) + first] > 0
        for home in range(homes):
            for half in range(2):
                at = (0, slice(None), pl.ds(pl.multiple_of(starts[2 * home + half], 128), 128))
                grad = grads[home][0, :, half * 128 : half * 128 + 128].astype(F32)
                grad = jnp.where(alive, grad, 0.0)
                mean = adam_beta * one[at] + (1.0 - adam_beta) * grad
                square = adam_beta * two[at] + (1.0 - adam_beta) * grad * grad
                ratio = (mean * (1.0 / bias)) / (jnp.sqrt(square * (1.0 / bias)) + adam_eps)
                old = mas[at]
                new = old - learn_rate * (ratio + decay_rate * old)
                new_mas[at] = new
                new_one[at] = mean
                new_two[at] = square
                copy[at] = new.astype(LOW)

    slot = pl.BlockSpec((1, rows, width), lambda i, s, u: (i + first, 0, 0))
    piece = pl.BlockSpec((1, rows, 256), lambda i, s, u: (i, 0, 0))
    shape = state[0].shape
    return pl.pallas_call(
        body,
        grid_spec=pltpu.PrefetchScalarGridSpec(
            num_scalar_prefetch=2,
            grid=(count,),
            in_specs=[slot] * 3 + [piece] * homes + [ANY_SPEC] * len(done),
            out_specs=[slot] * 4,
        ),
        out_shape=[jax.ShapeDtypeStruct(shape, F32)] * 3 + [jax.ShapeDtypeStruct(shape, LOW)],
        input_output_aliases={5 + homes + n: n for n in range(len(done))},
        name="update",
    )(lane_starts, used, *state, *pieces, *done)


def gather_rows(piece):
    near = [piece] + [swap(piece, 2 * k, 0) for k in (1, 2, 3)]
    blocks = []
    for part in near:
        pair = jnp.concatenate([part, swap(part, 0, 2)])
        blocks += [pair, swap(pair, 0, 1)]
    return jnp.concatenate(blocks)


def scatter_sum(partial_sum):
    quarter = partial_sum.shape[0] // 4
    half, rows = quarter // 2, quarter // 4
    kept = [None] * 4
    for k in (3, 2, 1, 0):
        chunk = partial_sum[quarter * k : quarter * (k + 1)]
        other = swap(chunk[half:].astype(LOW), 0, 1)
        pair = chunk[:half].astype(F32) + other.astype(F32)
        other = swap(pair[rows:].astype(LOW), 0, 2)
        kept[k] = pair[:rows] + other.astype(F32)
    total = kept[0]
    came = [swap(kept[k].astype(LOW), 2 * k, 0) for k in (3, 2, 1)]
    for part in came:
        total = total + part.astype(F32)
    return total, other


def share_rows(piece, wt_index):
    rows = piece.shape[0]
    out = jnp.zeros((4 * rows,) + piece.shape[1:], piece.dtype)
    over_y = swap(piece, 0, 2)
    for bits, part in ((0, piece), (2, over_y), (1, swap(piece, 0, 1)), (3, swap(over_y, 0, 1))):
        out = lax.dynamic_update_slice(out, part, ((wt_index ^ bits) * rows, 0))
    return out


def rotate(values, cosine, sine):
    half = values.shape[-1] // 2
    first, second = values[:, :half], values[:, half:]
    return jnp.concatenate([first * cosine - second * sine, second * cosine + first * sine], axis=1)


def fast_shards(tokens, cotangent, doc_lengths, owners, master, moment_one, moment_two):
    ctx, wt = lax.axis_index("ctx"), lax.axis_index("wt")
    z_at, x_at = ctx // 2, ctx % 2
    tok_rows, width = tokens.shape
    cap, tile_rows, _ = master.shape
    n_tiles = owners.shape[0]
    rows = tok_rows // 4
    bits = jnp.arange(4, dtype=jnp.int32)
    homes = jnp.arange(8, dtype=jnp.int32) ^ ctx
    lane_starts = (
        ((2 * (homes % 2))[:, None] + jnp.arange(2, dtype=jnp.int32)) * 4 + (homes // 2)[:, None]
    ).reshape(-1) * 128

    owner_col = owners[:, 0]
    tile_ids = jnp.arange(n_tiles, dtype=jnp.int32)
    earlier = (owner_col[None, :] == owner_col[:, None]) & (tile_ids[None, :] < tile_ids[:, None])
    slot_in_owner = jnp.sum(earlier.astype(jnp.int32), axis=1)
    owner_bits = owner_col ^ ctx

    def to_cut_order(values):
        cut_vals = values.reshape(-1, width // 4, 4).transpose(0, 2, 1).reshape(-1, width)
        flipped = jnp.concatenate([cut_vals[:, width // 2 :], cut_vals[:, : width // 2]], axis=1)
        return jnp.where(x_at == 0, cut_vals, flipped)

    def from_cut_order(values):
        flipped = jnp.concatenate([values[:, width // 2 :], values[:, : width // 2]], axis=1)
        cut_vals = jnp.where(x_at == 0, values, flipped)
        return cut_vals.reshape(-1, 4, width // 4).transpose(0, 2, 1).reshape(-1, width)

    inputs = lax.dynamic_slice(tokens, (wt * rows, 0), (rows, width)).astype(F32)
    normed, norm_back = jax.vjp(layer_norm, inputs)
    normed_cut = to_cut_order(normed.astype(LOW))
    normed_all = gather_rows(normed_cut)
    cut = lane_split(master, after(lane_starts, normed_cut))
    came = [cut[0]] + [swap(cut[k], k, 0) for k in range(1, 8)]
    out_grad_low = lax.dynamic_slice(cotangent, (wt * rows, 0), (rows, width))
    grad_all = gather_rows(out_grad_low)
    came[7], normed_all = lax.optimization_barrier((came[7], normed_all))
    w_qkv = pick_qkv(came, owner_bits[:12], slot_in_owner[:12])
    w_qkv_pair = swap(w_qkv, 1, 0)
    wanted = jnp.concatenate(
        [
            jnp.arange(16, 48, dtype=jnp.int32),
            12 + (z_at ^ bits),
            (48 + 4 * ((bits + 2 * x_at) % 4)[None, :] + (z_at ^ bits)[:, None]).reshape(-1),
        ]
    )
    wanted = after(wanted, w_qkv)
    home_gu, *sends = row_gather(
        came, owner_bits[wanted], slot_in_owner[wanted], [32] + [1] * 4 + [4] * 4
    )
    out_came = [sends[0]] + [swap(sends[m], 2 * m, 0) for m in (1, 2, 3)]
    down_here = [sends[4]] + [swap(sends[4 + m], 2 * m, 0) for m in (1, 2, 3)]
    down_here = jnp.stack(down_here)

    block_z = z_at ^ bits
    block_w = wt ^ jnp.array([0, 2, 1, 3], jnp.int32)

    def group_positions(x_index):
        starts = (2 * block_z + x_index)[:, None] * tok_rows + block_w[None, :] * rows
        return (starts.reshape(-1)[:, None] + jnp.arange(rows, dtype=jnp.int32)).reshape(-1)

    q_pos = group_positions(x_at)
    k_pos = jnp.concatenate([q_pos, group_positions(1 - x_at)])
    doc_starts = jnp.cumsum(doc_lengths) - doc_lengths
    q_doc, k_doc = doc_index(q_pos, doc_starts), doc_index(k_pos, doc_starts)
    masks = (q_pos[:, None], q_doc[:, None], k_pos[None, :], k_doc[None, :])
    freqs = rope_base ** (-jnp.arange(HEAD_DIM // 2, dtype=F32) * (2.0 / HEAD_DIM))
    angles = q_pos.astype(F32)[:, None] * freqs[None, :]
    cosine, sine = jnp.cos(angles), jnp.sin(angles)

    half = width // 2
    qkv = dot(normed_all[:, :half], w_qkv) + dot(normed_all[:, half:], w_qkv_pair)
    query = rotate(qkv[:, :128], cosine, sine).astype(LOW)
    kv_here = jnp.concatenate(
        [rotate(qkv[:, 128:256], cosine, sine).astype(LOW), qkv[:, 256:].astype(LOW)], axis=1
    )
    kv_there = swap(kv_here, 1, 0)
    out_here = after(jnp.stack(out_came), kv_here)
    out_there = swap(out_here, 1, 0)
    att_low, lse = attend(query, kv_here, kv_there, masks, 4)
    w_out = lane_join(out_here, out_there, lane_starts).reshape(tile_rows, width)

    pair_gu = swap(after(home_gu, kv_there), 1, 0)
    w_down = lane_join(down_here, swap(after(down_here, kv_there), 1, 0), lane_starts)
    w_down = w_down.reshape(512, width)
    w_gu = jnp.concatenate(
        [part.reshape(width, 256) for half_gu in (home_gu, pair_gu) for part in (half_gu[:16], half_gu[16:])],
        axis=1,
    )
    att_out, _ = scatter_sum(dot(att_low, w_out).astype(LOW))
    residual = inputs + att_out

    normed_two, norm_two_back = jax.vjp(layer_norm, residual)
    two_all = gather_rows(normed_two.astype(LOW))
    gu = dot(two_all, w_gu)
    gate = jnp.concatenate([gu[:, :256], gu[:, 512:768]], axis=1)
    up = jnp.concatenate([gu[:, 256:512], gu[:, 768:]], axis=1)
    gate_sig = jax.nn.sigmoid(gate)
    silu = gate * gate_sig
    hidden = (silu * up).astype(LOW)

    hidden_grad = dot_nt(grad_all, w_down)
    grad_gate = (hidden_grad * up * gate_sig * (1.0 + gate * (1.0 - gate_sig))).astype(LOW)
    grad_up = (hidden_grad * silu).astype(LOW)
    grad_gu = jnp.concatenate(
        [grad_gate[:, :256], grad_up[:, :256], grad_gate[:, 256:], grad_up[:, 256:]], axis=1
    )
    two_grad, begun = scatter_sum(dot_nt(grad_gu, w_gu).astype(LOW))
    hidden_later, grad_gu_later = lax.optimization_barrier((hidden, grad_gu, begun))[:2]
    grad_w_gu = dot_tn(two_all, grad_gu_later)
    grad_w_down = dot_tn(hidden_later, grad_all)
    gu_back = swap(grad_w_gu[:, 512:].astype(LOW), 1, 0)

    resid_grad = out_grad_low.astype(F32) + norm_two_back(two_grad)[0]
    resid_all = gather_rows(resid_grad.astype(LOW))
    down, _ = scatter_sum(dot(after(hidden, two_grad), w_down).astype(LOW))
    output = share_rows((residual + down).astype(LOW), wt)
    gu_sum = (grad_w_gu[:, :512] + gu_back.astype(F32)).astype(LOW)
    down_came = return_halves(grad_w_down.reshape(4, tile_rows, width), lane_starts)

    part_slots = cap // 2
    send_to = owner_bits + 8 * (slot_in_owner // part_slots)
    send_row = slot_in_owner % part_slots
    place = jnp.stack([z_at, x_at])
    sends = place_mlp(gu_sum, down_came, send_to, send_row, place, 16, part_slots)

    att_grad = dot_nt(resid_all, w_out).astype(LOW)
    out_grad_came = return_halves(
        dot_tn(att_low, resid_all).reshape(1, tile_rows, width), lane_starts
    )
    query_grad, kv_grad, kv_grad_there = attend_back(
        query, kv_here, kv_there, att_grad, lse, masks, 4
    )
    kv_grad_back = swap(kv_grad_there, 1, 0)
    kv_grad = kv_grad + kv_grad_back.astype(F32)
    qkv_grad = jnp.concatenate(
        [
            rotate(query_grad, cosine, -sine),
            rotate(kv_grad[:, :128], cosine, -sine),
            kv_grad[:, 128:],
        ],
        axis=1,
    ).astype(LOW)
    qkv_back = swap(dot_tn(normed_all[:, half:], qkv_grad).astype(LOW), 1, 0)
    qkv_sum = (dot_tn(normed_all[:, :half], qkv_grad) + qkv_back.astype(F32)).astype(LOW)
    sends = place_attention(sends, qkv_sum, out_grad_came, send_to, send_row, place)

    qkv_grad_later = after(qkv_grad, sends[0])
    one_part = jnp.concatenate(
        [dot_nt(qkv_grad_later, w_qkv), dot_nt(qkv_grad_later, w_qkv_pair)], axis=1
    )
    one_grad = from_cut_order(scatter_sum(one_part.astype(LOW))[0])
    input_grad = resid_grad + norm_back(one_grad)[0]
    input_grad = share_rows(input_grad.astype(LOW), wt).astype(F32)

    slot_range = jnp.arange(cap, dtype=jnp.int32) + ctx * cap
    used = jnp.any(
        (owner_col * cap + slot_in_owner)[None, :] == slot_range[:, None], axis=1
    ).astype(jnp.int32)
    state, done = (master, moment_one, moment_two), ()
    for part in range(2):
        mine = sends[8 * part : 8 * part + 8]
        pieces = [mine[0]] + [swap(mine[k], k, 0) for k in range(1, 8)]
        done = tuple(update(state, pieces, lane_starts, used, part * part_slots, done))
    return (output, input_grad) + done


def choose_shards(*args):
    sizes = (lax.axis_size("ctx"), lax.axis_size("wt"), args[0].shape, args[4].shape[1:])
    if sizes == (8, 4, (256, 2048), (128, 2048)) and args[3].shape[0] == 64:
        return fast_shards(*args)
    return general_shards(*args)


def solution(mesh):
    placed = (
        P("ctx", None),
        P("ctx", None),
        P(),
        P(),
        P("ctx", None, "wt"),
        P("ctx", None, "wt"),
        P("ctx", None, "wt"),
    )
    return jax.shard_map(
        choose_shards,
        mesh=mesh,
        in_specs=placed,
        out_specs=(
            P("ctx", None),
            P("ctx", None),
            P("ctx", None, "wt"),
            P("ctx", None, "wt"),
            P("ctx", None, "wt"),
            P("ctx", None, "wt"),
        ),
        check_vma=False,
    )
```

```python
from functools import partial
import math

import jax
import jax.numpy as jnp
from jax import lax
from jax.experimental import pallas as pl
from jax.experimental.pallas import tpu as pltpu
from jax.sharding import PartitionSpec as P

HEAD_DIM = 128
STEP = 3


adam_beta = 0.5
learn_rate = 0.01
decay_rate = 0.1
adam_eps = 1e-08
norm_eps = 1e-05
neg_fill = -1e30
rope_base = 10000.0


def from_behind(x, axis, by):
    count = lax.axis_size(axis)
    pairs = [(i, i + by) for i in range(count) if 0 <= i + by < count]
    return lax.ppermute(x, axis, pairs)


def from_behind_2(value, axis, steps):
    count = lax.axis_size(axis)
    pairs = [(source, (source + steps) % count) for source in range(count)]
    return lax.ppermute(value, axis, pairs)


def layer_norm(values):
    center = values - jnp.mean(values, axis=-1, keepdims=True)
    spread = jnp.mean(center * center, axis=-1, keepdims=True)
    return center * lax.rsqrt(spread + norm_eps)


def rotary(values, positions):
    half_dim = values.shape[-1] // 2
    frequencies = rope_base ** (-jnp.arange(half_dim, dtype=jnp.float32) * (2.0 / values.shape[-1]))
    angles = positions.astype(jnp.float32)[:, None] * frequencies[None, :]
    cosine = jnp.cos(angles)[:, None, :]
    sine_vals = jnp.sin(angles)[:, None, :]
    first_half = values[..., :half_dim]
    second_half = values[..., half_dim:]
    return jnp.concatenate(
        [
            first_half * cosine - second_half * sine_vals,
            second_half * cosine + first_half * sine_vals,
        ],
        axis=-1,
    )


def doc_index(positions, doc_starts):
    return jnp.sum((positions[:, None] >= doc_starts[None, :]).astype(jnp.int32), axis=1) - 1


def heads_dot(spec, left, right):
    return jnp.einsum(spec, left, right, preferred_element_type=jnp.float32)


def general_shards(tokens, cotangent, doc_lengths, owners, master, moment_one, moment_two):
    n_ctx = lax.axis_size("ctx")
    n_wt = lax.axis_size("wt")
    ctx_index = lax.axis_index("ctx")
    tok_rows, width = tokens.shape
    cap_slots, tile_rows, tile_width = master.shape
    n_tiles = owners.shape[0]
    head_dim = HEAD_DIM
    owner_col = owners[:, 0]
    tile_ids = jnp.arange(n_tiles, dtype=jnp.int32)
    earlier = (owner_col[None, :] == owner_col[:, None]) & (tile_ids[None, :] < tile_ids[:, None])
    slot_ids = owner_col * cap_slots + jnp.sum(earlier.astype(jnp.int32), axis=1)
    every_slot = lax.all_gather(master.astype(jnp.bfloat16), "ctx", axis=0, tiled=True)
    flat_w = every_slot[slot_ids].reshape(-1)
    local_width = width // n_wt
    heads_local = local_width // head_dim
    part_q = width * local_width
    ff_local = (flat_w.shape[0] - 4 * part_q) // (3 * width)
    part_f = width * ff_local
    w_qkv = flat_w[: 3 * part_q].reshape(3, width, local_width)
    w_out = flat_w[3 * part_q : 4 * part_q].reshape(local_width, width)
    w_gateup = flat_w[4 * part_q : 4 * part_q + 2 * part_f].reshape(2, width, ff_local)
    w_down = flat_w[4 * part_q + 2 * part_f :].reshape(ff_local, width)
    positions = ctx_index * tok_rows + jnp.arange(tok_rows, dtype=jnp.int32)
    doc_starts = jnp.cumsum(doc_lengths) - doc_lengths
    q_docs = doc_index(positions, doc_starts)
    score_scale = 1.0 / math.sqrt(head_dim)
    inputs = tokens.astype(jnp.float32)
    normed, norm_back = jax.vjp(layer_norm, inputs)
    normed_low = normed.astype(jnp.bfloat16)
    qkv_vals = heads_dot("td,jde->jte", normed_low, w_qkv)
    shaped = qkv_vals.reshape(3, tok_rows, heads_local, head_dim)
    rope_here = partial(rotary, positions=positions)
    qk_rot, rope_back = jax.vjp(rope_here, jnp.concatenate([shaped[0], shaped[1]], axis=1))
    q_low = qk_rot[:, :heads_local].astype(jnp.bfloat16)
    k_low = qk_rot[:, heads_local:].astype(jnp.bfloat16)
    v_low = shaped[2].astype(jnp.bfloat16)

    def masked_scores(key_block, key_pos, key_docs):
        raw_scores = heads_dot("qhd,khd->hqk", q_low, key_block)
        visible_mask = (key_pos[None, :] <= positions[:, None]) & (
            key_docs[None, :] == q_docs[:, None]
        )
        return (jnp.where(visible_mask[None], raw_scores * score_scale, neg_fill), visible_mask)

    def over_blocks(kv_piece, first_row, update_fn, running):
        key_count = kv_piece[0].shape[0]
        block_len = math.gcd(key_count, 512)
        n_blocks = key_count // block_len
        split_kv = tuple(
            (member.reshape((n_blocks, block_len) + member.shape[1:]) for member in kv_piece)
        )

        def step_fn(block_state, inputs_here):
            block_idx, block_vals = inputs_here
            block_row = first_row + block_idx * block_len
            key_pos = block_row + jnp.arange(block_len, dtype=jnp.int32)
            key_docs = doc_index(key_pos, doc_starts)
            block_state = update_fn(block_state, block_vals, key_pos, key_docs, block_row)
            return (block_state, None)

        running, _ = lax.scan(step_fn, running, (jnp.arange(n_blocks, dtype=jnp.int32), split_kv))
        return running

    def norm_update(block_state, block_vals, key_pos, key_docs, block_row):
        row_top, row_total = block_state
        scores, visible_mask = masked_scores(block_vals[0], key_pos, key_docs)
        new_top = jnp.maximum(row_top, jnp.max(scores, axis=-1))
        weights_exp = jnp.where(visible_mask[None], jnp.exp(scores - new_top[:, :, None]), 0.0)
        return (new_top, row_total * jnp.exp(row_top - new_top) + jnp.sum(weights_exp, axis=-1))

    start_top = jnp.full((heads_local, tok_rows), neg_fill, jnp.float32)
    start_total = jnp.zeros((heads_local, tok_rows), jnp.float32)
    row_top, row_total = over_blocks(
        (lax.all_gather(k_low, "ctx", axis=0, tiled=True),),
        jnp.int32(0),
        norm_update,
        (start_top, start_total),
    )
    log_sum = row_top + jnp.log(row_total)

    def block_probs(key_block, key_pos, key_docs):
        scores, visible_mask = masked_scores(key_block, key_pos, key_docs)
        return jnp.where(visible_mask[None], jnp.exp(scores - log_sum[:, :, None]), 0.0)

    def value_update(block_state, block_vals, key_pos, key_docs, block_row):
        prob_vals = block_probs(block_vals[0], key_pos, key_docs)
        return block_state + heads_dot(
            "hqk,khd->qhd", prob_vals.astype(jnp.bfloat16), block_vals[1]
        )

    zero_heads = jnp.zeros((tok_rows, heads_local, head_dim), jnp.float32)
    attended = over_blocks(
        (
            lax.all_gather(k_low, "ctx", axis=0, tiled=True),
            lax.all_gather(v_low, "ctx", axis=0, tiled=True),
        ),
        jnp.int32(0),
        value_update,
        zero_heads,
    )
    att_low = attended.reshape(tok_rows, local_width).astype(jnp.bfloat16)
    attn_part = jnp.dot(att_low, w_out, preferred_element_type=jnp.float32)
    residual = inputs + lax.psum(attn_part.astype(jnp.bfloat16), "wt").astype(jnp.float32)
    normed_two, norm_two_back = jax.vjp(layer_norm, residual)
    normed_two_low = normed_two.astype(jnp.bfloat16)
    gateup_vals = heads_dot("td,jde->jte", normed_two_low, w_gateup)
    gate_vals = gateup_vals[0]
    up_vals = gateup_vals[1]
    gate_sig = jax.nn.sigmoid(gate_vals)
    silu_vals = gate_vals * gate_sig
    hidden_low = (silu_vals * up_vals).astype(jnp.bfloat16)
    mlp_part = jnp.dot(hidden_low, w_down, preferred_element_type=jnp.float32)
    output = (residual + lax.psum(mlp_part.astype(jnp.bfloat16), "wt").astype(jnp.float32)).astype(
        jnp.bfloat16
    )
    out_grad = cotangent.astype(jnp.float32)
    grad_down = heads_dot("tf,td->fd", hidden_low, cotangent)
    grad_hidden = heads_dot("td,fd->tf", cotangent, w_down)
    grad_gate = grad_hidden * up_vals * gate_sig * (1.0 + gate_vals * (1.0 - gate_sig))
    grad_up = grad_hidden * silu_vals
    grad_gu_low = jnp.stack([grad_gate, grad_up]).astype(jnp.bfloat16)
    grad_gateup = heads_dot("td,jte->jde", normed_two_low, grad_gu_low)
    norm_two_part = heads_dot("jte,jde->td", grad_gu_low, w_gateup)
    norm_two_grad = lax.psum(norm_two_part.astype(jnp.bfloat16), "wt").astype(jnp.float32)
    resid_grad = out_grad + norm_two_back(norm_two_grad)[0]
    resid_low = resid_grad.astype(jnp.bfloat16)
    grad_out = heads_dot("tc,td->cd", att_low, resid_low)
    att_grad = heads_dot("td,cd->tc", resid_low, w_out)
    att_grad_low = att_grad.astype(jnp.bfloat16).reshape(tok_rows, heads_local, head_dim)
    row_delta = jnp.sum(att_grad_low * attended, axis=-1).T

    def grad_block(block_vals, key_pos, key_docs):
        prob_vals = block_probs(block_vals[0], key_pos, key_docs)
        value_grad = heads_dot("hqk,qhd->khd", prob_vals.astype(jnp.bfloat16), att_grad_low)
        prob_grad = heads_dot("qhd,khd->hqk", att_grad_low, block_vals[1])
        raw_grad = (prob_vals * (prob_grad - row_delta[:, :, None]) * score_scale).astype(
            jnp.bfloat16
        )
        query_grad = heads_dot("hqk,khd->qhd", raw_grad, block_vals[0])
        key_grad = heads_dot("hqk,qhd->khd", raw_grad, q_low)
        return (query_grad, key_grad, value_grad)

    def add_rows(target, addend):
        return target + addend

    def cycle_step(turn_idx, cycle_state):
        query_acc, key_cur, value_cur, key_acc, value_acc = cycle_state
        anchor = (ctx_index - turn_idx) % n_ctx

        def cycle_update(block_state, block_vals, key_pos, key_docs, block_row):
            q_acc, k_acc, v_acc = block_state
            query_grad, key_grad, value_grad = grad_block(block_vals, key_pos, key_docs)
            return (q_acc + query_grad, add_rows(k_acc, key_grad), add_rows(v_acc, value_grad))

        query_acc, key_acc, value_acc = over_blocks(
            (key_cur, value_cur), anchor * tok_rows, cycle_update, (query_acc, key_acc, value_acc)
        )
        key_cur, value_cur = from_behind((key_cur, value_cur), "ctx", 1)
        key_acc, value_acc = (
            from_behind_2(key_acc.astype(jnp.bfloat16), "ctx", 1).astype(key_acc.dtype),
            from_behind_2(value_acc.astype(jnp.bfloat16), "ctx", 1).astype(value_acc.dtype),
        )
        return (query_acc, key_cur, value_cur, key_acc, value_acc)

    cycle_start = (zero_heads, k_low, v_low, zero_heads, zero_heads)
    query_acc, _, _, key_acc, value_acc = lax.fori_loop(0, n_ctx, cycle_step, cycle_start)
    qk_pre_grad = rope_back(jnp.concatenate([query_acc, key_acc], axis=1))[0]
    qkv_grad_low = jnp.stack(
        [
            qk_pre_grad[:, :heads_local].reshape(tok_rows, local_width),
            qk_pre_grad[:, heads_local:].reshape(tok_rows, local_width),
            value_acc.reshape(tok_rows, local_width),
        ]
    ).astype(jnp.bfloat16)
    grad_qkv = heads_dot("td,jte->jde", normed_low, qkv_grad_low)
    norm_one_part = heads_dot("jte,jde->td", qkv_grad_low, w_qkv)
    norm_one_grad = lax.psum(norm_one_part.astype(jnp.bfloat16), "wt").astype(jnp.float32)
    input_grad = resid_grad + norm_back(norm_one_grad)[0]
    grad_tiles = jnp.concatenate(
        [grad_qkv.reshape(-1), grad_out.reshape(-1), grad_gateup.reshape(-1), grad_down.reshape(-1)]
    ).reshape(n_tiles, tile_rows, tile_width)
    slot_range = jnp.arange(n_ctx * cap_slots, dtype=jnp.int32)
    matches = slot_ids[None, :] == slot_range[:, None]
    tile_of_slot = jnp.sum(jnp.where(matches, tile_ids[None, :], 0), axis=1)
    slot_used = jnp.any(matches, axis=1)
    slot_grads = lax.psum_scatter(
        jnp.where(slot_used[:, None, None], grad_tiles[tile_of_slot], 0.0).astype(jnp.bfloat16),
        "ctx",
        scatter_dimension=0,
        tiled=True,
    ).astype(jnp.float32)
    new_one = adam_beta * moment_one + (1.0 - adam_beta) * slot_grads
    new_two = adam_beta * moment_two + (1.0 - adam_beta) * slot_grads * slot_grads
    bias_one = 1.0 - adam_beta**STEP
    bias_two = 1.0 - adam_beta**STEP
    step_ratio = new_one / bias_one / (jnp.sqrt(new_two / bias_two) + adam_eps)
    new_master = master - learn_rate * (step_ratio + decay_rate * master)
    return (output, input_grad, new_master, new_one, new_two, new_master.astype(jnp.bfloat16))


AXES = ("ctx", "wt")
LOW = jnp.bfloat16
F32 = jnp.float32


def swap(value, ctx_bits, wt_bits):
    n_ctx, n_wt = lax.axis_size("ctx"), lax.axis_size("wt")
    pairs = [
        (c * n_wt + w, (c ^ ctx_bits) * n_wt + (w ^ wt_bits))
        for c in range(n_ctx)
        for w in range(n_wt)
    ]
    return lax.ppermute(value, AXES, pairs)


def dot(left, right):
    return jnp.dot(left, right, preferred_element_type=F32)


def dot_tn(left, right):
    return lax.dot_general(left, right, (((0,), (0,)), ((), ())), preferred_element_type=F32)


def dot_nt(left, right):
    return lax.dot_general(left, right, (((1,), (1,)), ((), ())), preferred_element_type=F32)


def lane_split(value, lane_starts):
    count, rows, width = value.shape
    homes = lane_starts.shape[0] // 2

    def body(starts, src, *outs):
        for home in range(homes):
            for half in range(2):
                start = pl.multiple_of(starts[2 * home + half], 128)
                outs[home][0, :, half * 128 : half * 128 + 128] = src[
                    0, :, pl.ds(start, 128)
                ].astype(LOW)

    return pl.pallas_call(
        body,
        grid_spec=pltpu.PrefetchScalarGridSpec(
            num_scalar_prefetch=1,
            grid=(count,),
            in_specs=[pl.BlockSpec((1, rows, width), lambda i, s: (i, 0, 0))],
            out_specs=[pl.BlockSpec((1, rows, 256), lambda i, s: (i, 0, 0))] * homes,
        ),
        out_shape=[jax.ShapeDtypeStruct((count, rows, 256), LOW)] * homes,
        name="lane_split",
    )(lane_starts, value)


def lane_join(own, other, lane_starts):
    homes, count, rows, _ = own.shape
    width = homes * 512

    def body(starts, own_ref, other_ref, out):
        for home in range(homes):
            for side, ref in ((0, own_ref), (1, other_ref)):
                for half in range(2):
                    start = pl.multiple_of(starts[4 * home + 2 * side + half], 128)
                    out[0, :, pl.ds(start, 128)] = ref[home, 0, :, half * 128 : half * 128 + 128]

    return pl.pallas_call(
        body,
        grid_spec=pltpu.PrefetchScalarGridSpec(
            num_scalar_prefetch=1,
            grid=(count,),
            in_specs=[
                pl.BlockSpec((homes, 1, rows, 256), lambda i, s: (0, i, 0, 0)),
                pl.BlockSpec(
                    (homes, 1, rows, 256), lambda i, s: (0, (i + count // 2) % count, 0, 0)
                ),
            ],
            out_specs=pl.BlockSpec((1, rows, width), lambda i, s: (i, 0, 0)),
        ),
        out_shape=jax.ShapeDtypeStruct((count, rows, width), LOW),
        name="lane_join",
    )(lane_starts, own, other)


def lane_halves(value, lane_starts):
    count, rows, width = value.shape
    homes = width // 512

    def body(starts, src, own_ref, other_ref):
        for home in range(homes):
            for side, ref in ((0, own_ref), (1, other_ref)):
                for half in range(2):
                    start = pl.multiple_of(starts[4 * home + 2 * side + half], 128)
                    ref[home, 0, :, half * 128 : half * 128 + 128] = src[
                        0, :, pl.ds(start, 128)
                    ].astype(ref.dtype)

    return pl.pallas_call(
        body,
        grid_spec=pltpu.PrefetchScalarGridSpec(
            num_scalar_prefetch=1,
            grid=(count,),
            in_specs=[pl.BlockSpec((1, rows, width), lambda i, s: (i, 0, 0))],
            out_specs=[
                pl.BlockSpec((homes, 1, rows, 256), lambda i, s: (0, i, 0, 0)),
                pl.BlockSpec(
                    (homes, 1, rows, 256), lambda i, s: (0, (i + count // 2) % count, 0, 0)
                ),
            ],
        ),
        out_shape=[
            jax.ShapeDtypeStruct((homes, count, rows, 256), dtype) for dtype in (F32, LOW)
        ],
        name="lane_halves",
    )(lane_starts, value)


def return_halves(grad, lane_starts):
    own, other = lane_halves(grad, lane_starts)
    back = swap(other, 1, 0)
    sums = [(own[m] + back[m].astype(F32)).astype(LOW) for m in range(4)]
    return [sums[0]] + [swap(sums[m], 2 * m, 0) for m in (1, 2, 3)]


VMEM_SPEC = pl.BlockSpec(memory_space=pltpu.VMEM)
SMEM_SPEC = pl.BlockSpec(memory_space=pltpu.SMEM)
ANY_SPEC = pl.BlockSpec(memory_space=pl.ANY)


def pick_qkv(came, picked, rows):
    n_src = len(came)

    def body(which, where, *refs):
        srcs, out = refs[:n_src], refs[n_src]

        def copy(tile, carry):
            for n in range(n_src):

                @pl.when(which[tile] == n)
                def _(n=n):
                    for half in range(2):
                        row = pl.multiple_of(half * 512 + (tile % 4) * 128, 128)
                        lane = pl.multiple_of((tile // 4) * 128, 128)
                        out[pl.ds(row, 128), pl.ds(lane, 128)] = srcs[n][
                            where[tile], :, half * 128 : half * 128 + 128
                        ]

            return carry

        lax.fori_loop(0, 12, copy, 0)

    return pl.pallas_call(
        body,
        in_specs=[SMEM_SPEC, SMEM_SPEC] + [VMEM_SPEC] * n_src,
        out_specs=VMEM_SPEC,
        out_shape=jax.ShapeDtypeStruct((1024, 384), LOW),
        name="pick_qkv",
    )(picked, rows, *came)


def row_gather(sources, picked, rows, sizes):
    total = sum(sizes)
    n_src = len(sources)

    def body(which, where, *refs):
        srcs, outs, sem = refs[:n_src], refs[n_src:-1], refs[-1]
        first = 0
        for out, size in zip(outs, sizes):

            def start(j, carry, out=out, first=first):
                t = first + j
                for n in range(n_src):

                    @pl.when(which[t] == n)
                    def _(n=n):
                        pltpu.make_async_copy(srcs[n].at[where[t]], out.at[j], sem.at[t]).start()

                return carry

            lax.fori_loop(0, size, start, 0)
            first += size
        first = 0
        for out, size in zip(outs, sizes):

            def finish(j, carry, out=out, first=first):
                pltpu.make_async_copy(srcs[0].at[0], out.at[j], sem.at[first + j]).wait()
                return carry

            lax.fori_loop(0, size, finish, 0)
            first += size

    tail = sources[0].shape[1:]
    return pl.pallas_call(
        body,
        in_specs=[SMEM_SPEC, SMEM_SPEC] + [VMEM_SPEC] * n_src,
        out_specs=[ANY_SPEC] * len(sizes),
        out_shape=[jax.ShapeDtypeStruct((size,) + tail, LOW) for size in sizes],
        scratch_shapes=[pltpu.SemaphoreType.DMA((total,))],
        name="row_gather",
    )(picked, rows, *sources)


def send_tile(src, tile, to, row, outs, sem):
    for n, out in enumerate(outs):

        @pl.when(to[tile] == n)
        def _(out=out):
            pltpu.make_async_copy(src, out.at[row[tile]], sem.at[tile]).start()


def place_mlp(gate_up, downs, to, row, place, count, size):
    def body(to_ref, row_ref, z_ref, gu_ref, *refs):
        down_refs, outs, sem = refs[:4], refs[4:-1], refs[-1]
        down_tile = lambda m, k: 48 + 4 * ((k + 2 * z_ref[1]) % 4) + (z_ref[0] ^ m)

        def start(j, carry):
            at = pl.ds(pl.multiple_of(128 * j, 128), 128)
            for half in range(2):
                src = gu_ref.at[at, pl.ds(256 * half, 256)]
                send_tile(src, 16 + 16 * half + j, to_ref, row_ref, outs, sem)
            return carry

        lax.fori_loop(0, 16, start, 0)
        for m in range(4):

            def start_down(k, carry, m=m):
                send_tile(down_refs[m].at[k], down_tile(m, k), to_ref, row_ref, outs, sem)
                return carry

            lax.fori_loop(0, 4, start_down, 0)

        def finish(tile, carry):
            pltpu.make_async_copy(down_refs[0].at[0], outs[0].at[0], sem.at[tile]).wait()
            return carry

        lax.fori_loop(16, 64, finish, 0)

    return pl.pallas_call(
        body,
        in_specs=[SMEM_SPEC] * 3 + [VMEM_SPEC] * 5,
        out_specs=[ANY_SPEC] * count,
        out_shape=[jax.ShapeDtypeStruct((size, 128, 256), LOW)] * count,
        scratch_shapes=[pltpu.SemaphoreType.DMA((64,))],
        name="place_mlp",
    )(to, row, place, gate_up, *downs)


def place_attention(buffers, qkv, outs_from, to, row, place):
    count = len(buffers)

    def body(to_ref, row_ref, z_ref, qkv_ref, *refs):
        out_refs, outs = refs[:4], refs[4 + count : 4 + 2 * count]
        tiles, sem = refs[-2:]

        def start(tile, carry):
            lane = pl.multiple_of((tile // 4) * 128, 128)
            for half in range(2):
                at = pl.ds(pl.multiple_of(half * 512 + (tile % 4) * 128, 128), 128)
                tiles[tile, :, half * 128 : half * 128 + 128] = qkv_ref[at, pl.ds(lane, 128)]
            return carry

        lax.fori_loop(0, 12, start, 0)

        def start_copy(tile, carry):
            send_tile(tiles.at[tile], tile, to_ref, row_ref, outs, sem)
            return carry

        for m in range(4):
            send_tile(out_refs[m].at[0], 12 + (z_ref[0] ^ m), to_ref, row_ref, outs, sem)
        lax.fori_loop(0, 12, start_copy, 0)

        def finish(tile, carry):
            pltpu.make_async_copy(tiles.at[0], outs[0].at[0], sem.at[tile]).wait()
            return carry

        lax.fori_loop(0, 16, finish, 0)

    return pl.pallas_call(
        body,
        in_specs=[SMEM_SPEC] * 3 + [VMEM_SPEC] * 5 + [ANY_SPEC] * count,
        out_specs=[ANY_SPEC] * count,
        out_shape=[jax.ShapeDtypeStruct(buf.shape, buf.dtype) for buf in buffers],
        scratch_shapes=[pltpu.VMEM((12, 128, 256), LOW), pltpu.SemaphoreType.DMA((16,))],
        input_output_aliases={8 + n: n for n in range(count)},
        name="place_attention",
    )(to, row, place, qkv, *outs_from, *buffers)


def after(value, *earlier):
    return lax.optimization_barrier((value,) + earlier)[0]


def key_scores(q, here, there, masks):
    qp, qd, kp, kd = masks
    raw = jnp.concatenate([dot_nt(q, here[:, :128]), dot_nt(q, there[:, :128])], axis=1)
    seen = (kp[...] <= qp[...]) & (kd[...] == qd[...])
    return jnp.where(seen, raw * (1.0 / math.sqrt(HEAD_DIM)), neg_fill)


def attend(query, here, there, masks, n_blocks):
    rows = query.shape[0]
    block = rows // n_blocks

    def body(q, kv, kv_there, qp, qd, kp, kd, out, lse):
        scores = key_scores(q[...], kv[...], kv_there[...], (qp, qd, kp, kd))
        top = jnp.max(scores, axis=1, keepdims=True)
        weights = jnp.exp(scores - top)
        total = jnp.sum(weights, axis=1, keepdims=True)
        probs = (weights * (1.0 / total)).astype(LOW)
        mixed = dot(probs[:, :rows], kv[:, 128:]) + dot(probs[:, rows:], kv_there[:, 128:])
        out[...] = mixed.astype(LOW)
        lse[...] = top + jnp.log(total)

    whole = lambda arr: pl.BlockSpec(arr.shape, lambda i: (0, 0))
    part = lambda arr: pl.BlockSpec((block, arr.shape[1]), lambda i: (i, 0))
    q_pos, q_doc, k_pos, k_doc = masks
    return pl.pallas_call(
        body,
        grid=(n_blocks,),
        in_specs=[
            part(query), whole(here), whole(there), part(q_pos), part(q_doc), whole(k_pos), whole(k_doc),
        ],
        out_specs=[
            pl.BlockSpec((block, HEAD_DIM), lambda i: (i, 0)),
            pl.BlockSpec((block, 1), lambda i: (i, 0)),
        ],
        out_shape=[
            jax.ShapeDtypeStruct((rows, HEAD_DIM), LOW),
            jax.ShapeDtypeStruct((rows, 1), F32),
        ],
        name="attend",
    )(query, here, there, *masks)


def attend_back(query, here, there, out_grad, lse, masks, n_blocks):
    rows = query.shape[0]
    block = rows // n_blocks

    def body(q, kv, kv_there, do, ls, qp, qd, kp, kd, dq, d_here, d_there, acc):
        step = pl.program_id(0)

        @pl.when(step == 0)
        def _():
            d_here[...] = jnp.zeros_like(d_here)
            acc[...] = jnp.zeros_like(acc)

        scores = key_scores(q[...], kv[...], kv_there[...], (qp, qd, kp, kd))
        probs = jnp.exp(scores - ls[...])
        prob_grad = jnp.concatenate(
            [dot_nt(do[...], kv[:, 128:]), dot_nt(do[...], kv_there[:, 128:])], axis=1
        )
        delta = jnp.sum(probs * prob_grad, axis=1, keepdims=True)
        score_grad = (probs * (prob_grad - delta) * (1.0 / math.sqrt(HEAD_DIM))).astype(LOW)
        probs_low = probs.astype(LOW)
        dq[...] = dot(score_grad[:, :rows], kv[:, :128]) + dot(
            score_grad[:, rows:], kv_there[:, :128]
        )
        for first, out in ((0, d_here), (rows, acc)):
            out[:, :128] += dot_tn(score_grad[:, first : first + rows], q[...])
            out[:, 128:] += dot_tn(probs_low[:, first : first + rows], do[...])

        @pl.when(step == n_blocks - 1)
        def _():
            d_there[...] = acc[...].astype(LOW)

    whole = lambda arr: pl.BlockSpec(arr.shape, lambda i: (0, 0))
    part = lambda arr: pl.BlockSpec((block, arr.shape[1]), lambda i: (i, 0))
    kept = pl.BlockSpec((rows, 2 * HEAD_DIM), lambda i: (0, 0))
    q_pos, q_doc, k_pos, k_doc = masks
    return pl.pallas_call(
        body,
        grid=(n_blocks,),
        in_specs=[
            part(query), whole(here), whole(there), part(out_grad), part(lse),
            part(q_pos), part(q_doc), whole(k_pos), whole(k_doc),
        ],
        out_specs=[pl.BlockSpec((block, HEAD_DIM), lambda i: (i, 0)), kept, kept],
        out_shape=[
            jax.ShapeDtypeStruct((rows, HEAD_DIM), F32),
            jax.ShapeDtypeStruct((rows, 2 * HEAD_DIM), F32),
            jax.ShapeDtypeStruct((rows, 2 * HEAD_DIM), LOW),
        ],
        scratch_shapes=[pltpu.VMEM((rows, 2 * HEAD_DIM), F32)],
        name="attend_back",
    )(query, here, there, out_grad, lse, *masks)


def update(state, pieces, lane_starts, used, first, done):
    rows, width = state[0].shape[1:]
    count, homes = pieces[0].shape[0], len(pieces)
    bias = 1.0 - adam_beta**STEP

    def body(starts, live, mas, one, two, *refs):
        grads, (new_mas, new_one, new_two, copy) = refs[:homes], refs[-4:]
        alive = live[pl.program_id(0) + first] > 0
        for home in range(homes):
            for half in range(2):
                at = (0, slice(None), pl.ds(pl.multiple_of(starts[2 * home + half], 128), 128))
                grad = grads[home][0, :, half * 128 : half * 128 + 128].astype(F32)
                grad = jnp.where(alive, grad, 0.0)
                mean = adam_beta * one[at] + (1.0 - adam_beta) * grad
                square = adam_beta * two[at] + (1.0 - adam_beta) * grad * grad
                ratio = (mean * (1.0 / bias)) / (jnp.sqrt(square * (1.0 / bias)) + adam_eps)
                old = mas[at]
                new = old - learn_rate * (ratio + decay_rate * old)
                new_mas[at] = new
                new_one[at] = mean
                new_two[at] = square
                copy[at] = new.astype(LOW)

    slot = pl.BlockSpec((1, rows, width), lambda i, s, u: (i + first, 0, 0))
    piece = pl.BlockSpec((1, rows, 256), lambda i, s, u: (i, 0, 0))
    shape = state[0].shape
    return pl.pallas_call(
        body,
        grid_spec=pltpu.PrefetchScalarGridSpec(
            num_scalar_prefetch=2,
            grid=(count,),
            in_specs=[slot] * 3 + [piece] * homes + [ANY_SPEC] * len(done),
            out_specs=[slot] * 4,
        ),
        out_shape=[jax.ShapeDtypeStruct(shape, F32)] * 3 + [jax.ShapeDtypeStruct(shape, LOW)],
        input_output_aliases={5 + homes + n: n for n in range(len(done))},
        name="update",
    )(lane_starts, used, *state, *pieces, *done)


def stack_rows(blocks):
    rows, width = blocks[0].shape

    def body(*refs):
        for n, ref in enumerate(refs[:-1]):
            refs[-1][n * rows : (n + 1) * rows] = ref[...]

    return pl.pallas_call(
        body,
        in_specs=[VMEM_SPEC] * len(blocks),
        out_specs=VMEM_SPEC,
        out_shape=jax.ShapeDtypeStruct((len(blocks) * rows, width), LOW),
        name="stack_rows",
    )(*blocks)


def gather_rows(piece, stack=stack_rows):
    near = [piece] + [swap(piece, 2 * k, 0) for k in (1, 2, 3)]
    blocks = []
    for part in near:
        pair = jnp.concatenate([part, swap(part, 0, 2)])
        blocks += [pair, swap(pair, 0, 1)]
    return stack(blocks)


def scatter_sum(partial_sum):
    quarter = partial_sum.shape[0] // 4
    half, rows = quarter // 2, quarter // 4
    kept = [None] * 4
    for k in (3, 2, 1, 0):
        chunk = partial_sum[quarter * k : quarter * (k + 1)]
        other = swap(chunk[half:].astype(LOW), 0, 1)
        pair = chunk[:half].astype(F32) + other.astype(F32)
        other = swap(pair[rows:].astype(LOW), 0, 2)
        kept[k] = pair[:rows] + other.astype(F32)
    total = kept[0]
    came = [swap(kept[k].astype(LOW), 2 * k, 0) for k in (3, 2, 1)]
    for part in came:
        total = total + part.astype(F32)
    return total, other


def share_rows(piece, wt_index):
    rows = piece.shape[0]
    out = jnp.zeros((4 * rows,) + piece.shape[1:], piece.dtype)
    over_y = swap(piece, 0, 2)
    over_core, over_both = swap(piece, 0, 1), swap(over_y, 0, 1)
    for bits, part in ((0, piece), (2, over_y), (1, over_core), (3, over_both)):
        out = lax.dynamic_update_slice(out, part, ((wt_index ^ bits) * rows, 0))
    return out


def rotate(values, cosine, sine):
    half = values.shape[-1] // 2
    first, second = values[:, :half], values[:, half:]
    return jnp.concatenate([first * cosine - second * sine, second * cosine + first * sine], axis=1)


def fast_shards(tokens, cotangent, doc_lengths, owners, master, moment_one, moment_two):
    ctx, wt = lax.axis_index("ctx"), lax.axis_index("wt")
    z_at, x_at = ctx // 2, ctx % 2
    tok_rows, width = tokens.shape
    cap, tile_rows, _ = master.shape
    n_tiles = owners.shape[0]
    rows = tok_rows // 4
    bits = jnp.arange(4, dtype=jnp.int32)
    homes = jnp.arange(8, dtype=jnp.int32) ^ ctx
    lane_starts = (
        ((2 * (homes % 2))[:, None] + jnp.arange(2, dtype=jnp.int32)) * 4 + (homes // 2)[:, None]
    ).reshape(-1) * 128

    owner_col = owners[:, 0]
    tile_ids = jnp.arange(n_tiles, dtype=jnp.int32)
    earlier = (owner_col[None, :] == owner_col[:, None]) & (tile_ids[None, :] < tile_ids[:, None])
    slot_in_owner = jnp.sum(earlier.astype(jnp.int32), axis=1)
    owner_bits = owner_col ^ ctx

    def to_cut_order(values):
        cut_vals = values.reshape(-1, width // 4, 4).transpose(0, 2, 1).reshape(-1, width)
        flipped = jnp.concatenate([cut_vals[:, width // 2 :], cut_vals[:, : width // 2]], axis=1)
        return jnp.where(x_at == 0, cut_vals, flipped)

    def from_cut_order(values):
        flipped = jnp.concatenate([values[:, width // 2 :], values[:, : width // 2]], axis=1)
        cut_vals = jnp.where(x_at == 0, values, flipped)
        return cut_vals.reshape(-1, 4, width // 4).transpose(0, 2, 1).reshape(-1, width)

    inputs = lax.dynamic_slice(tokens, (wt * rows, 0), (rows, width)).astype(F32)
    normed, norm_back = jax.vjp(layer_norm, inputs)
    normed_cut = to_cut_order(normed.astype(LOW))
    normed_all = gather_rows(normed_cut, jnp.concatenate)
    cut = lane_split(master, after(lane_starts, normed_cut))
    came = [cut[0]] + [swap(cut[k], k, 0) for k in range(1, 8)]
    came[7], normed_all = lax.optimization_barrier((came[7], normed_all))
    w_qkv = pick_qkv(came, owner_bits[:12], slot_in_owner[:12])
    w_qkv_pair = swap(w_qkv, 1, 0)
    out_grad_low = lax.dynamic_slice(after(cotangent, w_qkv), (wt * rows, 0), (rows, width))
    grad_all = gather_rows(out_grad_low)
    wanted = jnp.concatenate(
        [
            jnp.arange(16, 48, dtype=jnp.int32),
            12 + (z_at ^ bits),
            (48 + 4 * ((bits + 2 * x_at) % 4)[None, :] + (z_at ^ bits)[:, None]).reshape(-1),
        ]
    )
    wanted = after(wanted, w_qkv)
    home_gu, *sends = row_gather(
        came, owner_bits[wanted], slot_in_owner[wanted], [32] + [1] * 4 + [4] * 4
    )
    out_came = [sends[0]] + [swap(sends[m], 2 * m, 0) for m in (1, 2, 3)]
    down_here = [sends[4]] + [swap(sends[4 + m], 2 * m, 0) for m in (1, 2, 3)]
    down_here = jnp.stack(down_here)

    block_z = z_at ^ bits
    block_w = wt ^ jnp.array([0, 2, 1, 3], jnp.int32)

    def group_positions(x_index):
        starts = (2 * block_z + x_index)[:, None] * tok_rows + block_w[None, :] * rows
        return (starts.reshape(-1)[:, None] + jnp.arange(rows, dtype=jnp.int32)).reshape(-1)

    q_pos = group_positions(x_at)
    k_pos = jnp.concatenate([q_pos, group_positions(1 - x_at)])
    doc_starts = jnp.cumsum(doc_lengths) - doc_lengths
    q_doc, k_doc = doc_index(q_pos, doc_starts), doc_index(k_pos, doc_starts)
    masks = (q_pos[:, None], q_doc[:, None], k_pos[None, :], k_doc[None, :])
    freqs = rope_base ** (-jnp.arange(HEAD_DIM // 2, dtype=F32) * (2.0 / HEAD_DIM))
    angles = q_pos.astype(F32)[:, None] * freqs[None, :]
    cosine, sine = jnp.cos(angles), jnp.sin(angles)

    half = width // 2
    qkv = dot(normed_all[:, :half], w_qkv) + dot(normed_all[:, half:], w_qkv_pair)
    query = rotate(qkv[:, :128], cosine, sine).astype(LOW)
    kv_here = jnp.concatenate(
        [rotate(qkv[:, 128:256], cosine, sine).astype(LOW), qkv[:, 256:].astype(LOW)], axis=1
    )
    kv_there = swap(kv_here, 1, 0)
    out_here = after(jnp.stack(out_came), kv_here)
    out_there = swap(out_here, 1, 0)
    att_low, lse = attend(query, kv_here, kv_there, masks, 4)
    w_out = lane_join(out_here, out_there, lane_starts).reshape(tile_rows, width)

    pair_gu = swap(after(home_gu, kv_there), 1, 0)
    w_down = lane_join(down_here, swap(after(down_here, kv_there), 1, 0), lane_starts)
    w_down = w_down.reshape(512, width)
    w_gu = jnp.concatenate(
        [part.reshape(width, 256) for half_gu in (home_gu, pair_gu) for part in (half_gu[:16], half_gu[16:])],
        axis=1,
    )
    att_out, _ = scatter_sum(dot(att_low, w_out).astype(LOW))
    residual = inputs + att_out

    normed_two, norm_two_back = jax.vjp(layer_norm, residual)
    two_all = gather_rows(normed_two.astype(LOW))
    gu = dot(two_all, w_gu)
    gate = jnp.concatenate([gu[:, :256], gu[:, 512:768]], axis=1)
    up = jnp.concatenate([gu[:, 256:512], gu[:, 768:]], axis=1)
    gate_sig = jax.nn.sigmoid(gate)
    silu = gate * gate_sig
    hidden = (silu * up).astype(LOW)

    hidden_grad = dot_nt(grad_all, w_down)
    grad_gate = (hidden_grad * up * gate_sig * (1.0 + gate * (1.0 - gate_sig))).astype(LOW)
    grad_up = (hidden_grad * silu).astype(LOW)
    grad_gu = jnp.concatenate(
        [grad_gate[:, :256], grad_up[:, :256], grad_gate[:, 256:], grad_up[:, 256:]], axis=1
    )
    two_grad, begun = scatter_sum(dot_nt(grad_gu, w_gu).astype(LOW))
    hidden_later, grad_gu_later = lax.optimization_barrier((hidden, grad_gu, begun))[:2]
    grad_w_gu = dot_tn(two_all, grad_gu_later)
    grad_w_down = dot_tn(hidden_later, grad_all)
    gu_back = swap(grad_w_gu[:, 512:].astype(LOW), 1, 0)

    resid_grad = out_grad_low.astype(F32) + norm_two_back(two_grad)[0]
    resid_all = gather_rows(resid_grad.astype(LOW))
    down, _ = scatter_sum(dot(after(hidden, two_grad), w_down).astype(LOW))
    output = share_rows((residual + down).astype(LOW), wt)
    gu_sum = (grad_w_gu[:, :512] + gu_back.astype(F32)).astype(LOW)
    down_came = return_halves(grad_w_down.reshape(4, tile_rows, width), lane_starts)

    part_slots = cap // 2
    send_to = owner_bits + 8 * (slot_in_owner // part_slots)
    send_row = slot_in_owner % part_slots
    place = jnp.stack([z_at, x_at])
    sends = place_mlp(gu_sum, down_came, send_to, send_row, place, 16, part_slots)

    att_grad = dot_nt(resid_all, w_out).astype(LOW)
    out_grad_came = return_halves(
        dot_tn(att_low, resid_all).reshape(1, tile_rows, width), lane_starts
    )
    query_grad, kv_grad, kv_grad_there = attend_back(
        query, kv_here, kv_there, att_grad, lse, masks, 4
    )
    kv_grad_back = swap(kv_grad_there, 1, 0)
    kv_grad = kv_grad + kv_grad_back.astype(F32)
    qkv_grad = jnp.concatenate(
        [
            rotate(query_grad, cosine, -sine),
            rotate(kv_grad[:, :128], cosine, -sine),
            kv_grad[:, 128:],
        ],
        axis=1,
    ).astype(LOW)
    qkv_back = swap(dot_tn(normed_all[:, half:], qkv_grad).astype(LOW), 1, 0)
    qkv_sum = (dot_tn(normed_all[:, :half], qkv_grad) + qkv_back.astype(F32)).astype(LOW)
    sends = place_attention(sends, qkv_sum, out_grad_came, send_to, send_row, place)

    qkv_grad_later = after(qkv_grad, sends[0])
    one_part = jnp.concatenate(
        [dot_nt(qkv_grad_later, w_qkv), dot_nt(qkv_grad_later, w_qkv_pair)], axis=1
    )
    one_grad = from_cut_order(scatter_sum(one_part.astype(LOW))[0])
    input_grad = resid_grad + norm_back(one_grad)[0]
    input_grad = share_rows(input_grad.astype(LOW), wt)
    input_grad = input_grad.astype(F32)

    slot_range = jnp.arange(cap, dtype=jnp.int32) + ctx * cap
    used = jnp.any(
        (owner_col * cap + slot_in_owner)[None, :] == slot_range[:, None], axis=1
    ).astype(jnp.int32)
    state = (master, moment_one, moment_two)
    first, second = [sends[0]], [sends[8]]
    first += [swap(sends[k], k, 0) for k in range(1, 8)]
    for k in range(1, 8):
        second.append(swap(after(sends[8 + k], first[k]), k, 0))
    done = update(state, first, lane_starts, used, 0, ())
    done = update(state, second, lane_starts, used, part_slots, tuple(done))
    return (output, input_grad) + tuple(done)


def choose_shards(*args):
    sizes = (lax.axis_size("ctx"), lax.axis_size("wt"), args[0].shape, args[4].shape[1:])
    if sizes == (8, 4, (256, 2048), (128, 2048)) and args[3].shape[0] == 64:
        return fast_shards(*args)
    return general_shards(*args)


def solution(mesh):
    placed = (
        P("ctx", None),
        P("ctx", None),
        P(),
        P(),
        P("ctx", None, "wt"),
        P("ctx", None, "wt"),
        P("ctx", None, "wt"),
    )
    return jax.shard_map(
        choose_shards,
        mesh=mesh,
        in_specs=placed,
        out_specs=(
            P("ctx", None),
            P("ctx", None),
            P("ctx", None, "wt"),
            P("ctx", None, "wt"),
            P("ctx", None, "wt"),
            P("ctx", None, "wt"),
        ),
        check_vma=False,
    )
```

```python
from functools import partial
import math

import jax
import jax.numpy as jnp
from jax import lax
from jax.experimental import pallas as pl
from jax.experimental.pallas import tpu as pltpu
from jax.sharding import PartitionSpec as P

HEAD_DIM = 128
STEP = 3


adam_beta = 0.5
learn_rate = 0.01
decay_rate = 0.1
adam_eps = 1e-08
norm_eps = 1e-05
neg_fill = -1e30
rope_base = 10000.0


def from_behind(x, axis, by):
    count = lax.axis_size(axis)
    pairs = [(i, i + by) for i in range(count) if 0 <= i + by < count]
    return lax.ppermute(x, axis, pairs)


def from_behind_2(value, axis, steps):
    count = lax.axis_size(axis)
    pairs = [(source, (source + steps) % count) for source in range(count)]
    return lax.ppermute(value, axis, pairs)


def layer_norm(values):
    center = values - jnp.mean(values, axis=-1, keepdims=True)
    spread = jnp.mean(center * center, axis=-1, keepdims=True)
    return center * lax.rsqrt(spread + norm_eps)


def rotary(values, positions):
    half_dim = values.shape[-1] // 2
    frequencies = rope_base ** (-jnp.arange(half_dim, dtype=jnp.float32) * (2.0 / values.shape[-1]))
    angles = positions.astype(jnp.float32)[:, None] * frequencies[None, :]
    cosine = jnp.cos(angles)[:, None, :]
    sine_vals = jnp.sin(angles)[:, None, :]
    first_half = values[..., :half_dim]
    second_half = values[..., half_dim:]
    return jnp.concatenate(
        [
            first_half * cosine - second_half * sine_vals,
            second_half * cosine + first_half * sine_vals,
        ],
        axis=-1,
    )


def doc_index(positions, doc_starts):
    return jnp.sum((positions[:, None] >= doc_starts[None, :]).astype(jnp.int32), axis=1) - 1


def heads_dot(spec, left, right):
    return jnp.einsum(spec, left, right, preferred_element_type=jnp.float32)


def general_shards(tokens, cotangent, doc_lengths, owners, master, moment_one, moment_two):
    n_ctx = lax.axis_size("ctx")
    n_wt = lax.axis_size("wt")
    ctx_index = lax.axis_index("ctx")
    tok_rows, width = tokens.shape
    cap_slots, tile_rows, tile_width = master.shape
    n_tiles = owners.shape[0]
    head_dim = HEAD_DIM
    owner_col = owners[:, 0]
    tile_ids = jnp.arange(n_tiles, dtype=jnp.int32)
    earlier = (owner_col[None, :] == owner_col[:, None]) & (tile_ids[None, :] < tile_ids[:, None])
    slot_ids = owner_col * cap_slots + jnp.sum(earlier.astype(jnp.int32), axis=1)
    every_slot = lax.all_gather(master.astype(jnp.bfloat16), "ctx", axis=0, tiled=True)
    flat_w = every_slot[slot_ids].reshape(-1)
    local_width = width // n_wt
    heads_local = local_width // head_dim
    part_q = width * local_width
    ff_local = (flat_w.shape[0] - 4 * part_q) // (3 * width)
    part_f = width * ff_local
    w_qkv = flat_w[: 3 * part_q].reshape(3, width, local_width)
    w_out = flat_w[3 * part_q : 4 * part_q].reshape(local_width, width)
    w_gateup = flat_w[4 * part_q : 4 * part_q + 2 * part_f].reshape(2, width, ff_local)
    w_down = flat_w[4 * part_q + 2 * part_f :].reshape(ff_local, width)
    positions = ctx_index * tok_rows + jnp.arange(tok_rows, dtype=jnp.int32)
    doc_starts = jnp.cumsum(doc_lengths) - doc_lengths
    q_docs = doc_index(positions, doc_starts)
    score_scale = 1.0 / math.sqrt(head_dim)
    inputs = tokens.astype(jnp.float32)
    normed, norm_back = jax.vjp(layer_norm, inputs)
    normed_low = normed.astype(jnp.bfloat16)
    qkv_vals = heads_dot("td,jde->jte", normed_low, w_qkv)
    shaped = qkv_vals.reshape(3, tok_rows, heads_local, head_dim)
    rope_here = partial(rotary, positions=positions)
    qk_rot, rope_back = jax.vjp(rope_here, jnp.concatenate([shaped[0], shaped[1]], axis=1))
    q_low = qk_rot[:, :heads_local].astype(jnp.bfloat16)
    k_low = qk_rot[:, heads_local:].astype(jnp.bfloat16)
    v_low = shaped[2].astype(jnp.bfloat16)

    def masked_scores(key_block, key_pos, key_docs):
        raw_scores = heads_dot("qhd,khd->hqk", q_low, key_block)
        visible_mask = (key_pos[None, :] <= positions[:, None]) & (
            key_docs[None, :] == q_docs[:, None]
        )
        return (jnp.where(visible_mask[None], raw_scores * score_scale, neg_fill), visible_mask)

    def over_blocks(kv_piece, first_row, update_fn, running):
        key_count = kv_piece[0].shape[0]
        block_len = math.gcd(key_count, 512)
        n_blocks = key_count // block_len
        split_kv = tuple(
            (member.reshape((n_blocks, block_len) + member.shape[1:]) for member in kv_piece)
        )

        def step_fn(block_state, inputs_here):
            block_idx, block_vals = inputs_here
            block_row = first_row + block_idx * block_len
            key_pos = block_row + jnp.arange(block_len, dtype=jnp.int32)
            key_docs = doc_index(key_pos, doc_starts)
            block_state = update_fn(block_state, block_vals, key_pos, key_docs, block_row)
            return (block_state, None)

        running, _ = lax.scan(step_fn, running, (jnp.arange(n_blocks, dtype=jnp.int32), split_kv))
        return running

    def norm_update(block_state, block_vals, key_pos, key_docs, block_row):
        row_top, row_total = block_state
        scores, visible_mask = masked_scores(block_vals[0], key_pos, key_docs)
        new_top = jnp.maximum(row_top, jnp.max(scores, axis=-1))
        weights_exp = jnp.where(visible_mask[None], jnp.exp(scores - new_top[:, :, None]), 0.0)
        return (new_top, row_total * jnp.exp(row_top - new_top) + jnp.sum(weights_exp, axis=-1))

    start_top = jnp.full((heads_local, tok_rows), neg_fill, jnp.float32)
    start_total = jnp.zeros((heads_local, tok_rows), jnp.float32)
    row_top, row_total = over_blocks(
        (lax.all_gather(k_low, "ctx", axis=0, tiled=True),),
        jnp.int32(0),
        norm_update,
        (start_top, start_total),
    )
    log_sum = row_top + jnp.log(row_total)

    def block_probs(key_block, key_pos, key_docs):
        scores, visible_mask = masked_scores(key_block, key_pos, key_docs)
        return jnp.where(visible_mask[None], jnp.exp(scores - log_sum[:, :, None]), 0.0)

    def value_update(block_state, block_vals, key_pos, key_docs, block_row):
        prob_vals = block_probs(block_vals[0], key_pos, key_docs)
        return block_state + heads_dot(
            "hqk,khd->qhd", prob_vals.astype(jnp.bfloat16), block_vals[1]
        )

    zero_heads = jnp.zeros((tok_rows, heads_local, head_dim), jnp.float32)
    attended = over_blocks(
        (
            lax.all_gather(k_low, "ctx", axis=0, tiled=True),
            lax.all_gather(v_low, "ctx", axis=0, tiled=True),
        ),
        jnp.int32(0),
        value_update,
        zero_heads,
    )
    att_low = attended.reshape(tok_rows, local_width).astype(jnp.bfloat16)
    attn_part = jnp.dot(att_low, w_out, preferred_element_type=jnp.float32)
    residual = inputs + lax.psum(attn_part.astype(jnp.bfloat16), "wt").astype(jnp.float32)
    normed_two, norm_two_back = jax.vjp(layer_norm, residual)
    normed_two_low = normed_two.astype(jnp.bfloat16)
    gateup_vals = heads_dot("td,jde->jte", normed_two_low, w_gateup)
    gate_vals = gateup_vals[0]
    up_vals = gateup_vals[1]
    gate_sig = jax.nn.sigmoid(gate_vals)
    silu_vals = gate_vals * gate_sig
    hidden_low = (silu_vals * up_vals).astype(jnp.bfloat16)
    mlp_part = jnp.dot(hidden_low, w_down, preferred_element_type=jnp.float32)
    output = (residual + lax.psum(mlp_part.astype(jnp.bfloat16), "wt").astype(jnp.float32)).astype(
        jnp.bfloat16
    )
    out_grad = cotangent.astype(jnp.float32)
    grad_down = heads_dot("tf,td->fd", hidden_low, cotangent)
    grad_hidden = heads_dot("td,fd->tf", cotangent, w_down)
    grad_gate = grad_hidden * up_vals * gate_sig * (1.0 + gate_vals * (1.0 - gate_sig))
    grad_up = grad_hidden * silu_vals
    grad_gu_low = jnp.stack([grad_gate, grad_up]).astype(jnp.bfloat16)
    grad_gateup = heads_dot("td,jte->jde", normed_two_low, grad_gu_low)
    norm_two_part = heads_dot("jte,jde->td", grad_gu_low, w_gateup)
    norm_two_grad = lax.psum(norm_two_part.astype(jnp.bfloat16), "wt").astype(jnp.float32)
    resid_grad = out_grad + norm_two_back(norm_two_grad)[0]
    resid_low = resid_grad.astype(jnp.bfloat16)
    grad_out = heads_dot("tc,td->cd", att_low, resid_low)
    att_grad = heads_dot("td,cd->tc", resid_low, w_out)
    att_grad_low = att_grad.astype(jnp.bfloat16).reshape(tok_rows, heads_local, head_dim)
    row_delta = jnp.sum(att_grad_low * attended, axis=-1).T

    def grad_block(block_vals, key_pos, key_docs):
        prob_vals = block_probs(block_vals[0], key_pos, key_docs)
        value_grad = heads_dot("hqk,qhd->khd", prob_vals.astype(jnp.bfloat16), att_grad_low)
        prob_grad = heads_dot("qhd,khd->hqk", att_grad_low, block_vals[1])
        raw_grad = (prob_vals * (prob_grad - row_delta[:, :, None]) * score_scale).astype(
            jnp.bfloat16
        )
        query_grad = heads_dot("hqk,khd->qhd", raw_grad, block_vals[0])
        key_grad = heads_dot("hqk,qhd->khd", raw_grad, q_low)
        return (query_grad, key_grad, value_grad)

    def add_rows(target, addend):
        return target + addend

    def cycle_step(turn_idx, cycle_state):
        query_acc, key_cur, value_cur, key_acc, value_acc = cycle_state
        anchor = (ctx_index - turn_idx) % n_ctx

        def cycle_update(block_state, block_vals, key_pos, key_docs, block_row):
            q_acc, k_acc, v_acc = block_state
            query_grad, key_grad, value_grad = grad_block(block_vals, key_pos, key_docs)
            return (q_acc + query_grad, add_rows(k_acc, key_grad), add_rows(v_acc, value_grad))

        query_acc, key_acc, value_acc = over_blocks(
            (key_cur, value_cur), anchor * tok_rows, cycle_update, (query_acc, key_acc, value_acc)
        )
        key_cur, value_cur = from_behind((key_cur, value_cur), "ctx", 1)
        key_acc, value_acc = (
            from_behind_2(key_acc.astype(jnp.bfloat16), "ctx", 1).astype(key_acc.dtype),
            from_behind_2(value_acc.astype(jnp.bfloat16), "ctx", 1).astype(value_acc.dtype),
        )
        return (query_acc, key_cur, value_cur, key_acc, value_acc)

    cycle_start = (zero_heads, k_low, v_low, zero_heads, zero_heads)
    query_acc, _, _, key_acc, value_acc = lax.fori_loop(0, n_ctx, cycle_step, cycle_start)
    qk_pre_grad = rope_back(jnp.concatenate([query_acc, key_acc], axis=1))[0]
    qkv_grad_low = jnp.stack(
        [
            qk_pre_grad[:, :heads_local].reshape(tok_rows, local_width),
            qk_pre_grad[:, heads_local:].reshape(tok_rows, local_width),
            value_acc.reshape(tok_rows, local_width),
        ]
    ).astype(jnp.bfloat16)
    grad_qkv = heads_dot("td,jte->jde", normed_low, qkv_grad_low)
    norm_one_part = heads_dot("jte,jde->td", qkv_grad_low, w_qkv)
    norm_one_grad = lax.psum(norm_one_part.astype(jnp.bfloat16), "wt").astype(jnp.float32)
    input_grad = resid_grad + norm_back(norm_one_grad)[0]
    grad_tiles = jnp.concatenate(
        [grad_qkv.reshape(-1), grad_out.reshape(-1), grad_gateup.reshape(-1), grad_down.reshape(-1)]
    ).reshape(n_tiles, tile_rows, tile_width)
    slot_range = jnp.arange(n_ctx * cap_slots, dtype=jnp.int32)
    matches = slot_ids[None, :] == slot_range[:, None]
    tile_of_slot = jnp.sum(jnp.where(matches, tile_ids[None, :], 0), axis=1)
    slot_used = jnp.any(matches, axis=1)
    slot_grads = lax.psum_scatter(
        jnp.where(slot_used[:, None, None], grad_tiles[tile_of_slot], 0.0).astype(jnp.bfloat16),
        "ctx",
        scatter_dimension=0,
        tiled=True,
    ).astype(jnp.float32)
    new_one = adam_beta * moment_one + (1.0 - adam_beta) * slot_grads
    new_two = adam_beta * moment_two + (1.0 - adam_beta) * slot_grads * slot_grads
    bias_one = 1.0 - adam_beta**STEP
    bias_two = 1.0 - adam_beta**STEP
    step_ratio = new_one / bias_one / (jnp.sqrt(new_two / bias_two) + adam_eps)
    new_master = master - learn_rate * (step_ratio + decay_rate * master)
    return (output, input_grad, new_master, new_one, new_two, new_master.astype(jnp.bfloat16))


AXES = ("ctx", "wt")
LOW = jnp.bfloat16
F32 = jnp.float32


def swap(value, ctx_bits, wt_bits):
    n_ctx, n_wt = lax.axis_size("ctx"), lax.axis_size("wt")
    pairs = [
        (c * n_wt + w, (c ^ ctx_bits) * n_wt + (w ^ wt_bits))
        for c in range(n_ctx)
        for w in range(n_wt)
    ]
    return lax.ppermute(value, AXES, pairs)


def dot(left, right):
    return jnp.dot(left, right, preferred_element_type=F32)


def dot_tn(left, right):
    return lax.dot_general(left, right, (((0,), (0,)), ((), ())), preferred_element_type=F32)


def dot_nt(left, right):
    return lax.dot_general(left, right, (((1,), (1,)), ((), ())), preferred_element_type=F32)


def lane_split(value, lane_starts):
    count, rows, width = value.shape
    homes = lane_starts.shape[0] // 2

    def body(starts, src, *outs):
        for home in range(homes):
            for half in range(2):
                start = pl.multiple_of(starts[2 * home + half], 128)
                outs[home][0, :, half * 128 : half * 128 + 128] = src[
                    0, :, pl.ds(start, 128)
                ].astype(LOW)

    return pl.pallas_call(
        body,
        grid_spec=pltpu.PrefetchScalarGridSpec(
            num_scalar_prefetch=1,
            grid=(count,),
            in_specs=[pl.BlockSpec((1, rows, width), lambda i, s: (i, 0, 0))],
            out_specs=[pl.BlockSpec((1, rows, 256), lambda i, s: (i, 0, 0))] * homes,
        ),
        out_shape=[jax.ShapeDtypeStruct((count, rows, 256), LOW)] * homes,
        name="lane_split",
    )(lane_starts, value)


def lane_join(own, other, lane_starts):
    homes, count, rows, _ = own.shape
    width = homes * 512

    def body(starts, own_ref, other_ref, out):
        for home in range(homes):
            for side, ref in ((0, own_ref), (1, other_ref)):
                for half in range(2):
                    start = pl.multiple_of(starts[4 * home + 2 * side + half], 128)
                    out[0, :, pl.ds(start, 128)] = ref[home, 0, :, half * 128 : half * 128 + 128]

    return pl.pallas_call(
        body,
        grid_spec=pltpu.PrefetchScalarGridSpec(
            num_scalar_prefetch=1,
            grid=(count,),
            in_specs=[
                pl.BlockSpec((homes, 1, rows, 256), lambda i, s: (0, i, 0, 0)),
                pl.BlockSpec(
                    (homes, 1, rows, 256), lambda i, s: (0, (i + count // 2) % count, 0, 0)
                ),
            ],
            out_specs=pl.BlockSpec((1, rows, width), lambda i, s: (i, 0, 0)),
        ),
        out_shape=jax.ShapeDtypeStruct((count, rows, width), LOW),
        name="lane_join",
    )(lane_starts, own, other)


def lane_halves(value, lane_starts):
    count, rows, width = value.shape
    homes = width // 512

    def body(starts, src, own_ref, other_ref):
        for home in range(homes):
            for side, ref in ((0, own_ref), (1, other_ref)):
                for half in range(2):
                    start = pl.multiple_of(starts[4 * home + 2 * side + half], 128)
                    ref[home, 0, :, half * 128 : half * 128 + 128] = src[
                        0, :, pl.ds(start, 128)
                    ].astype(ref.dtype)

    return pl.pallas_call(
        body,
        grid_spec=pltpu.PrefetchScalarGridSpec(
            num_scalar_prefetch=1,
            grid=(count,),
            in_specs=[pl.BlockSpec((1, rows, width), lambda i, s: (i, 0, 0))],
            out_specs=[
                pl.BlockSpec((homes, 1, rows, 256), lambda i, s: (0, i, 0, 0)),
                pl.BlockSpec(
                    (homes, 1, rows, 256), lambda i, s: (0, (i + count // 2) % count, 0, 0)
                ),
            ],
        ),
        out_shape=[
            jax.ShapeDtypeStruct((homes, count, rows, 256), dtype) for dtype in (F32, LOW)
        ],
        name="lane_halves",
    )(lane_starts, value)


def return_halves(grad, lane_starts):
    own, other = lane_halves(grad, lane_starts)
    back = swap(other, 1, 0)
    sums = [(own[m] + back[m].astype(F32)).astype(LOW) for m in range(4)]
    return [sums[0]] + [swap(sums[m], 2 * m, 0) for m in (1, 2, 3)]


def join_grads(query, kv, kv_back, cosine, sine):
    def body(q, here, there, cos, sin, out):
        def undo(values):
            return values * cos[...] + pltpu.roll(values, 64, 1) * sin[...]

        total = here[...] + there[...].astype(F32)
        out[:, :128] = undo(q[...]).astype(LOW)
        out[:, 128:256] = undo(total[:, :128]).astype(LOW)
        out[:, 256:] = total[:, 128:].astype(LOW)

    return pl.pallas_call(
        body,
        in_specs=[VMEM_SPEC] * 5,
        out_specs=VMEM_SPEC,
        out_shape=jax.ShapeDtypeStruct((query.shape[0], 384), LOW),
        name="join_grads",
    )(query, kv, kv_back, cosine, sine)


VMEM_SPEC = pl.BlockSpec(memory_space=pltpu.VMEM)
SMEM_SPEC = pl.BlockSpec(memory_space=pltpu.SMEM)
ANY_SPEC = pl.BlockSpec(memory_space=pl.ANY)


def pick_qkv(came, picked, rows):
    n_src = len(came)

    def body(which, where, *refs):
        srcs, out = refs[:n_src], refs[n_src]

        def copy(tile, carry):
            for n in range(n_src):

                @pl.when(which[tile] == n)
                def _(n=n):
                    for half in range(2):
                        row = pl.multiple_of(half * 512 + (tile % 4) * 128, 128)
                        lane = pl.multiple_of((tile // 4) * 128, 128)
                        out[pl.ds(row, 128), pl.ds(lane, 128)] = srcs[n][
                            where[tile], :, half * 128 : half * 128 + 128
                        ]

            return carry

        lax.fori_loop(0, 12, copy, 0)

    return pl.pallas_call(
        body,
        in_specs=[SMEM_SPEC, SMEM_SPEC] + [VMEM_SPEC] * n_src,
        out_specs=VMEM_SPEC,
        out_shape=jax.ShapeDtypeStruct((1024, 384), LOW),
        name="pick_qkv",
    )(picked, rows, *came)


def row_gather(sources, picked, rows, sizes):
    total = sum(sizes)
    n_src = len(sources)

    def body(which, where, *refs):
        srcs, outs, sem = refs[:n_src], refs[n_src:-1], refs[-1]
        first = 0
        for out, size in zip(outs, sizes):

            def start(j, carry, out=out, first=first):
                t = first + j
                for n in range(n_src):

                    @pl.when(which[t] == n)
                    def _(n=n):
                        pltpu.make_async_copy(srcs[n].at[where[t]], out.at[j], sem.at[t]).start()

                return carry

            lax.fori_loop(0, size, start, 0)
            first += size
        first = 0
        for out, size in zip(outs, sizes):

            def finish(j, carry, out=out, first=first):
                pltpu.make_async_copy(srcs[0].at[0], out.at[j], sem.at[first + j]).wait()
                return carry

            lax.fori_loop(0, size, finish, 0)
            first += size

    tail = sources[0].shape[1:]
    return pl.pallas_call(
        body,
        in_specs=[SMEM_SPEC, SMEM_SPEC] + [VMEM_SPEC] * n_src,
        out_specs=[ANY_SPEC] * len(sizes),
        out_shape=[jax.ShapeDtypeStruct((size,) + tail, LOW) for size in sizes],
        scratch_shapes=[pltpu.SemaphoreType.DMA((total,))],
        name="row_gather",
    )(picked, rows, *sources)


def send_tile(src, tile, to, row, outs, sem):
    for n, out in enumerate(outs):

        @pl.when(to[tile] == n)
        def _(out=out):
            pltpu.make_async_copy(src, out.at[row[tile]], sem.at[tile]).start()


def place_mlp(gate_up, downs, to, row, place, sizes):
    def body(to_ref, row_ref, z_ref, gu_ref, *refs):
        down_refs, outs, sem = refs[:4], refs[4:-1], refs[-1]
        down_tile = lambda m, k: 48 + 4 * ((k + 2 * z_ref[1]) % 4) + (z_ref[0] ^ m)

        def start(j, carry):
            at = pl.ds(pl.multiple_of(128 * j, 128), 128)
            for half in range(2):
                src = gu_ref.at[at, pl.ds(256 * half, 256)]
                send_tile(src, 16 + 16 * half + j, to_ref, row_ref, outs, sem)
            return carry

        lax.fori_loop(0, 16, start, 0)
        for m in range(4):

            def start_down(k, carry, m=m):
                send_tile(down_refs[m].at[k], down_tile(m, k), to_ref, row_ref, outs, sem)
                return carry

            lax.fori_loop(0, 4, start_down, 0)

        def finish(tile, carry):
            pltpu.make_async_copy(down_refs[0].at[0], outs[0].at[0], sem.at[tile]).wait()
            return carry

        lax.fori_loop(16, 64, finish, 0)

    return pl.pallas_call(
        body,
        in_specs=[SMEM_SPEC] * 3 + [VMEM_SPEC] * 5,
        out_specs=[ANY_SPEC] * len(sizes),
        out_shape=[jax.ShapeDtypeStruct((size, 128, 256), LOW) for size in sizes],
        scratch_shapes=[pltpu.SemaphoreType.DMA((64,))],
        name="place_mlp",
    )(to, row, place, gate_up, *downs)


def place_attention(buffers, qkv, outs_from, to, row, place):
    count = len(buffers)

    def body(to_ref, row_ref, z_ref, qkv_ref, *refs):
        out_refs, outs = refs[:4], refs[4 + count : 4 + 2 * count]
        tiles, sem = refs[-2:]

        def start(tile, carry):
            lane = pl.multiple_of((tile // 4) * 128, 128)
            for half in range(2):
                at = pl.ds(pl.multiple_of(half * 512 + (tile % 4) * 128, 128), 128)
                tiles[tile, :, half * 128 : half * 128 + 128] = qkv_ref[at, pl.ds(lane, 128)]
            return carry

        lax.fori_loop(0, 12, start, 0)

        def start_copy(tile, carry):
            send_tile(tiles.at[tile], tile, to_ref, row_ref, outs, sem)
            return carry

        for m in range(4):
            send_tile(out_refs[m].at[0], 12 + (z_ref[0] ^ m), to_ref, row_ref, outs, sem)
        lax.fori_loop(0, 12, start_copy, 0)

        def finish(tile, carry):
            pltpu.make_async_copy(tiles.at[0], outs[0].at[0], sem.at[tile]).wait()
            return carry

        lax.fori_loop(0, 16, finish, 0)

    return pl.pallas_call(
        body,
        in_specs=[SMEM_SPEC] * 3 + [VMEM_SPEC] * 5 + [ANY_SPEC] * count,
        out_specs=[ANY_SPEC] * count,
        out_shape=[jax.ShapeDtypeStruct(buf.shape, buf.dtype) for buf in buffers],
        scratch_shapes=[pltpu.VMEM((12, 128, 256), LOW), pltpu.SemaphoreType.DMA((16,))],
        input_output_aliases={8 + n: n for n in range(count)},
        name="place_attention",
    )(to, row, place, qkv, *outs_from, *buffers)


def after(value, *earlier):
    return lax.optimization_barrier((value,) + earlier)[0]


def key_scores(q, here, there, masks):
    qp, qd, kp, kd = masks
    raw = jnp.concatenate([dot_nt(q, here[:, :128]), dot_nt(q, there[:, :128])], axis=1)
    seen = (kp[...] <= qp[...]) & (kd[...] == qd[...])
    return jnp.where(seen, raw * (1.0 / math.sqrt(HEAD_DIM)), neg_fill)


def attend(query, here, there, masks, n_blocks):
    rows = query.shape[0]
    block = rows // n_blocks

    def body(q, kv, kv_there, qp, qd, kp, kd, out, lse):
        scores = key_scores(q[...], kv[...], kv_there[...], (qp, qd, kp, kd))
        top = jnp.max(scores, axis=1, keepdims=True)
        weights = jnp.exp(scores - top)
        total = jnp.sum(weights, axis=1, keepdims=True)
        probs = (weights * (1.0 / total)).astype(LOW)
        mixed = dot(probs[:, :rows], kv[:, 128:]) + dot(probs[:, rows:], kv_there[:, 128:])
        out[...] = mixed.astype(LOW)
        lse[...] = top + jnp.log(total)

    whole = lambda arr: pl.BlockSpec(arr.shape, lambda i: (0, 0))
    part = lambda arr: pl.BlockSpec((block, arr.shape[1]), lambda i: (i, 0))
    q_pos, q_doc, k_pos, k_doc = masks
    return pl.pallas_call(
        body,
        grid=(n_blocks,),
        in_specs=[
            part(query), whole(here), whole(there), part(q_pos), part(q_doc), whole(k_pos), whole(k_doc),
        ],
        out_specs=[
            pl.BlockSpec((block, HEAD_DIM), lambda i: (i, 0)),
            pl.BlockSpec((block, 1), lambda i: (i, 0)),
        ],
        out_shape=[
            jax.ShapeDtypeStruct((rows, HEAD_DIM), LOW),
            jax.ShapeDtypeStruct((rows, 1), F32),
        ],
        name="attend",
    )(query, here, there, *masks)


def attend_back(query, here, there, out_grad, lse, masks, n_blocks):
    rows = query.shape[0]
    block = rows // n_blocks

    def body(q, kv, kv_there, do, ls, qp, qd, kp, kd, dq, d_here, d_there, acc):
        step = pl.program_id(0)

        @pl.when(step == 0)
        def _():
            d_here[...] = jnp.zeros_like(d_here)
            acc[...] = jnp.zeros_like(acc)

        scores = key_scores(q[...], kv[...], kv_there[...], (qp, qd, kp, kd))
        probs = jnp.exp(scores - ls[...])
        prob_grad = jnp.concatenate(
            [dot_nt(do[...], kv[:, 128:]), dot_nt(do[...], kv_there[:, 128:])], axis=1
        )
        delta = jnp.sum(probs * prob_grad, axis=1, keepdims=True)
        score_grad = (probs * (prob_grad - delta) * (1.0 / math.sqrt(HEAD_DIM))).astype(LOW)
        probs_low = probs.astype(LOW)
        dq[...] = dot(score_grad[:, :rows], kv[:, :128]) + dot(
            score_grad[:, rows:], kv_there[:, :128]
        )
        for first, out in ((0, d_here), (rows, acc)):
            out[:, :128] += dot_tn(score_grad[:, first : first + rows], q[...])
            out[:, 128:] += dot_tn(probs_low[:, first : first + rows], do[...])

        @pl.when(step == n_blocks - 1)
        def _():
            d_there[...] = acc[...].astype(LOW)

    whole = lambda arr: pl.BlockSpec(arr.shape, lambda i: (0, 0))
    part = lambda arr: pl.BlockSpec((block, arr.shape[1]), lambda i: (i, 0))
    kept = pl.BlockSpec((rows, 2 * HEAD_DIM), lambda i: (0, 0))
    q_pos, q_doc, k_pos, k_doc = masks
    return pl.pallas_call(
        body,
        grid=(n_blocks,),
        in_specs=[
            part(query), whole(here), whole(there), part(out_grad), part(lse),
            part(q_pos), part(q_doc), whole(k_pos), whole(k_doc),
        ],
        out_specs=[pl.BlockSpec((block, HEAD_DIM), lambda i: (i, 0)), kept, kept],
        out_shape=[
            jax.ShapeDtypeStruct((rows, HEAD_DIM), F32),
            jax.ShapeDtypeStruct((rows, 2 * HEAD_DIM), F32),
            jax.ShapeDtypeStruct((rows, 2 * HEAD_DIM), LOW),
        ],
        scratch_shapes=[pltpu.VMEM((rows, 2 * HEAD_DIM), F32)],
        name="attend_back",
    )(query, here, there, out_grad, lse, *masks)


def update(state, pieces, lane_starts, used, first, done):
    rows, width = state[0].shape[1:]
    count, homes = pieces[0].shape[0], len(pieces)
    bias = 1.0 - adam_beta**STEP

    def body(starts, live, mas, one, two, *refs):
        grads, (new_mas, new_one, new_two, copy) = refs[:homes], refs[-4:]
        alive = live[pl.program_id(0) + first] > 0
        for home in range(homes):
            for half in range(2):
                at = (0, slice(None), pl.ds(pl.multiple_of(starts[2 * home + half], 128), 128))
                grad = grads[home][0, :, half * 128 : half * 128 + 128].astype(F32)
                grad = jnp.where(alive, grad, 0.0)
                mean = adam_beta * one[at] + (1.0 - adam_beta) * grad
                square = adam_beta * two[at] + (1.0 - adam_beta) * grad * grad
                ratio = (mean * (1.0 / bias)) / (jnp.sqrt(square * (1.0 / bias)) + adam_eps)
                old = mas[at]
                new = old - learn_rate * (ratio + decay_rate * old)
                new_mas[at] = new
                new_one[at] = mean
                new_two[at] = square
                copy[at] = new.astype(LOW)

    slot = pl.BlockSpec((1, rows, width), lambda i, s, u: (i + first, 0, 0))
    piece = pl.BlockSpec((1, rows, 256), lambda i, s, u: (i, 0, 0))
    shape = state[0].shape
    return pl.pallas_call(
        body,
        grid_spec=pltpu.PrefetchScalarGridSpec(
            num_scalar_prefetch=2,
            grid=(count,),
            in_specs=[slot] * 3 + [piece] * homes + [ANY_SPEC] * len(done),
            out_specs=[slot] * 4,
        ),
        out_shape=[jax.ShapeDtypeStruct(shape, F32)] * 3 + [jax.ShapeDtypeStruct(shape, LOW)],
        input_output_aliases={5 + homes + n: n for n in range(len(done))},
        name="update",
    )(lane_starts, used, *state, *pieces, *done)


def stack_rows(blocks):
    rows, width = blocks[0].shape

    def body(*refs):
        for n, ref in enumerate(refs[:-1]):
            refs[-1][n * rows : (n + 1) * rows] = ref[...]

    return pl.pallas_call(
        body,
        in_specs=[VMEM_SPEC] * len(blocks),
        out_specs=VMEM_SPEC,
        out_shape=jax.ShapeDtypeStruct((len(blocks) * rows, width), LOW),
        name="stack_rows",
    )(*blocks)


def gather_rows(piece):
    near = [piece] + [swap(piece, 2 * k, 0) for k in (1, 2, 3)]
    blocks = []
    for part in near:
        pair = jnp.concatenate([part, swap(part, 0, 2)])
        blocks += [pair, swap(pair, 0, 1)]
    return stack_rows(blocks)


def scatter_sum(partial_sum):
    quarter = partial_sum.shape[0] // 4
    half, rows = quarter // 2, quarter // 4
    kept = [None] * 4
    for k in (3, 2, 1, 0):
        chunk = partial_sum[quarter * k : quarter * (k + 1)]
        other = swap(chunk[half:].astype(LOW), 0, 1)
        pair = chunk[:half].astype(F32) + other.astype(F32)
        other = swap(pair[rows:].astype(LOW), 0, 2)
        kept[k] = pair[:rows] + other.astype(F32)
    total = kept[0]
    came = [swap(kept[k].astype(LOW), 2 * k, 0) for k in (3, 2, 1)]
    for part in came:
        total = total + part.astype(F32)
    return total, other


def share_rows(piece, wt_index):
    rows = piece.shape[0]
    out = jnp.zeros((4 * rows,) + piece.shape[1:], piece.dtype)
    over_y = swap(piece, 0, 2)
    over_core, over_both = swap(piece, 0, 1), swap(over_y, 0, 1)
    for bits, part in ((0, piece), (2, over_y), (1, over_core), (3, over_both)):
        out = lax.dynamic_update_slice(out, part, ((wt_index ^ bits) * rows, 0))
    return out


def rotate(values, cosine, sine):
    half = values.shape[-1] // 2
    first, second = values[:, :half], values[:, half:]
    return jnp.concatenate([first * cosine - second * sine, second * cosine + first * sine], axis=1)


def fast_shards(tokens, cotangent, doc_lengths, owners, master, moment_one, moment_two):
    ctx, wt = lax.axis_index("ctx"), lax.axis_index("wt")
    z_at, x_at = ctx // 2, ctx % 2
    tok_rows, width = tokens.shape
    cap, tile_rows, _ = master.shape
    n_tiles = owners.shape[0]
    rows = tok_rows // 4
    bits = jnp.arange(4, dtype=jnp.int32)
    homes = jnp.arange(8, dtype=jnp.int32) ^ ctx
    lane_starts = (
        ((2 * (homes % 2))[:, None] + jnp.arange(2, dtype=jnp.int32)) * 4 + (homes // 2)[:, None]
    ).reshape(-1) * 128

    owner_col = owners[:, 0]
    tile_ids = jnp.arange(n_tiles, dtype=jnp.int32)
    earlier = (owner_col[None, :] == owner_col[:, None]) & (tile_ids[None, :] < tile_ids[:, None])
    slot_in_owner = jnp.sum(earlier.astype(jnp.int32), axis=1)
    owner_bits = owner_col ^ ctx

    def to_cut_order(values):
        cut_vals = values.reshape(-1, width // 4, 4).transpose(0, 2, 1).reshape(-1, width)
        flipped = jnp.concatenate([cut_vals[:, width // 2 :], cut_vals[:, : width // 2]], axis=1)
        return jnp.where(x_at == 0, cut_vals, flipped)

    def from_cut_order(values):
        flipped = jnp.concatenate([values[:, width // 2 :], values[:, : width // 2]], axis=1)
        cut_vals = jnp.where(x_at == 0, values, flipped)
        return cut_vals.reshape(-1, 4, width // 4).transpose(0, 2, 1).reshape(-1, width)

    cut = lane_split(master, lane_starts)
    came = [cut[0]] + [swap(cut[k], k, 0) for k in range(1, 8)]
    tokens_later = after(tokens, cut[0])
    inputs = lax.dynamic_slice(tokens_later, (wt * rows, 0), (rows, width)).astype(F32)
    normed, norm_back = jax.vjp(layer_norm, inputs)
    normed_cut = to_cut_order(normed.astype(LOW))
    normed_all = gather_rows(after(normed_cut, came[4], came[5], came[6]))
    w_qkv = pick_qkv(came, owner_bits[:12], slot_in_owner[:12])
    w_qkv_pair = swap(w_qkv, 1, 0)
    out_grad_low = lax.dynamic_slice(after(cotangent, w_qkv_pair), (wt * rows, 0), (rows, width))
    grad_all = gather_rows(out_grad_low)
    wanted = jnp.concatenate(
        [
            jnp.arange(16, 48, dtype=jnp.int32),
            12 + (z_at ^ bits),
            (48 + 4 * ((bits + 2 * x_at) % 4)[None, :] + (z_at ^ bits)[:, None]).reshape(-1),
        ]
    )
    wanted = after(wanted, w_qkv)
    home_gate, home_up, *sends = row_gather(
        came, owner_bits[wanted], slot_in_owner[wanted], [16, 16] + [1] * 4 + [4] * 4
    )
    out_came = [sends[0]] + [swap(sends[m], 2 * m, 0) for m in (1, 2, 3)]
    down_here = [sends[4]] + [swap(sends[4 + m], 2 * m, 0) for m in (1, 2, 3)]
    down_here = jnp.stack(down_here)

    block_z = z_at ^ bits
    block_w = wt ^ jnp.array([0, 2, 1, 3], jnp.int32)

    def group_positions(x_index):
        starts = (2 * block_z + x_index)[:, None] * tok_rows + block_w[None, :] * rows
        return (starts.reshape(-1)[:, None] + jnp.arange(rows, dtype=jnp.int32)).reshape(-1)

    q_pos = group_positions(x_at)
    k_pos = jnp.concatenate([q_pos, group_positions(1 - x_at)])
    doc_starts = jnp.cumsum(doc_lengths) - doc_lengths
    q_doc, k_doc = doc_index(q_pos, doc_starts), doc_index(k_pos, doc_starts)
    masks = (q_pos[:, None], q_doc[:, None], k_pos[None, :], k_doc[None, :])
    freqs = rope_base ** (-jnp.arange(HEAD_DIM // 2, dtype=F32) * (2.0 / HEAD_DIM))
    angles = q_pos.astype(F32)[:, None] * freqs[None, :]
    cosine, sine = jnp.cos(angles), jnp.sin(angles)

    half = width // 2
    qkv = dot(normed_all[:, :half], w_qkv) + dot(normed_all[:, half:], w_qkv_pair)
    query = rotate(qkv[:, :128], cosine, sine).astype(LOW)
    kv_here = jnp.concatenate(
        [rotate(qkv[:, 128:256], cosine, sine).astype(LOW), qkv[:, 256:].astype(LOW)], axis=1
    )
    kv_there = swap(kv_here, 1, 0)
    out_here = after(jnp.stack(out_came), kv_here)
    out_there = swap(out_here, 1, 0)
    att_low, lse = attend(query, kv_here, kv_there, masks, 4)
    w_out = lane_join(out_here, out_there, lane_starts).reshape(tile_rows, width)

    gate_later, up_later = lax.optimization_barrier((home_gate, home_up, kv_there))[:2]
    pair_gate, pair_up = swap(gate_later, 1, 0), swap(up_later, 1, 0)
    down_there = swap(after(down_here, kv_there), 1, 0)
    w_down = lane_join(down_here, down_there, lane_starts).reshape(512, width)
    w_gu = jnp.concatenate(
        [part.reshape(width, 256) for part in (home_gate, home_up, pair_gate, pair_up)], axis=1
    )
    att_out, _ = scatter_sum(dot(att_low, w_out).astype(LOW))
    residual = inputs + att_out

    normed_two, norm_two_back = jax.vjp(layer_norm, residual)
    two_all = gather_rows(normed_two.astype(LOW))
    gu = dot(two_all, w_gu)
    gate = jnp.concatenate([gu[:, :256], gu[:, 512:768]], axis=1)
    up = jnp.concatenate([gu[:, 256:512], gu[:, 768:]], axis=1)
    gate_sig = jax.nn.sigmoid(gate)
    silu = gate * gate_sig
    hidden = (silu * up).astype(LOW)

    hidden_grad = dot_nt(grad_all, w_down)
    grad_gate = (hidden_grad * up * gate_sig * (1.0 + gate * (1.0 - gate_sig))).astype(LOW)
    grad_up = (hidden_grad * silu).astype(LOW)
    grad_gu = jnp.concatenate(
        [grad_gate[:, :256], grad_up[:, :256], grad_gate[:, 256:], grad_up[:, 256:]], axis=1
    )
    two_grad, begun = scatter_sum(dot_nt(grad_gu, w_gu).astype(LOW))
    hidden_later, grad_gu_later = lax.optimization_barrier((hidden, grad_gu, begun))[:2]
    grad_w_gu = dot_tn(two_all, grad_gu_later)
    gu_back = swap(grad_w_gu[:, 512:].astype(LOW), 1, 0)

    resid_grad = out_grad_low.astype(F32) + norm_two_back(two_grad)[0]
    resid_all = gather_rows(resid_grad.astype(LOW))
    grad_w_down = dot_tn(after(hidden_later, two_grad), grad_all)
    down, _ = scatter_sum(dot(after(hidden, two_grad), w_down).astype(LOW))
    output = share_rows((residual + down).astype(LOW), wt)
    gu_sum = (grad_w_gu[:, :512] + gu_back.astype(F32)).astype(LOW)
    down_came = return_halves(grad_w_down.reshape(4, tile_rows, width), lane_starts)

    part_slots = cap * 2 // 3
    send_to = owner_bits + 8 * (slot_in_owner // part_slots)
    send_row = slot_in_owner % part_slots
    place = jnp.stack([z_at, x_at])
    sends = place_mlp(
        gu_sum, down_came, send_to, send_row, place, [part_slots] * 8 + [cap - part_slots] * 8
    )

    att_grad = dot_nt(resid_all, w_out).astype(LOW)
    out_grad_came = return_halves(
        dot_tn(att_low, resid_all).reshape(1, tile_rows, width), lane_starts
    )
    query_grad, kv_grad, kv_grad_there = attend_back(
        query, kv_here, kv_there, att_grad, lse, masks, 4
    )
    kv_grad_back = swap(kv_grad_there, 1, 0)
    qkv_grad = join_grads(
        query_grad,
        kv_grad,
        kv_grad_back,
        jnp.concatenate([cosine, cosine], axis=1),
        jnp.concatenate([sine, -sine], axis=1),
    )
    qkv_back = swap(dot_tn(normed_all[:, half:], qkv_grad).astype(LOW), 1, 0)
    qkv_sum = (dot_tn(normed_all[:, :half], qkv_grad) + qkv_back.astype(F32)).astype(LOW)
    sends = place_attention(sends, qkv_sum, out_grad_came, send_to, send_row, place)

    qkv_grad_later = after(qkv_grad, sends[0])
    one_part = jnp.concatenate(
        [dot_nt(qkv_grad_later, w_qkv), dot_nt(qkv_grad_later, w_qkv_pair)], axis=1
    )
    one_grad = from_cut_order(scatter_sum(one_part.astype(LOW))[0])
    input_grad = resid_grad + norm_back(one_grad)[0]
    input_grad = share_rows(input_grad.astype(LOW), wt)
    input_grad = input_grad.astype(F32)

    slot_range = jnp.arange(cap, dtype=jnp.int32) + ctx * cap
    used = jnp.any(
        (owner_col * cap + slot_in_owner)[None, :] == slot_range[:, None], axis=1
    ).astype(jnp.int32)
    state = (master, moment_one, moment_two)
    first, second = [sends[0]], [sends[8]]
    first += [swap(sends[k], k, 0) for k in range(1, 8)]
    for k in range(1, 8):
        second.append(swap(after(sends[8 + k], first[k]), k, 0))
    done = update(state, first, lane_starts, used, 0, ())
    done = update(state, second, lane_starts, used, part_slots, tuple(done))
    return (output, input_grad) + tuple(done)


def choose_shards(*args):
    sizes = (lax.axis_size("ctx"), lax.axis_size("wt"), args[0].shape, args[4].shape[1:])
    if sizes == (8, 4, (256, 2048), (128, 2048)) and args[3].shape[0] == 64:
        return fast_shards(*args)
    return general_shards(*args)


def solution(mesh):
    placed = (
        P("ctx", None),
        P("ctx", None),
        P(),
        P(),
        P("ctx", None, "wt"),
        P("ctx", None, "wt"),
        P("ctx", None, "wt"),
    )
    return jax.shard_map(
        choose_shards,
        mesh=mesh,
        in_specs=placed,
        out_specs=(
            P("ctx", None),
            P("ctx", None),
            P("ctx", None, "wt"),
            P("ctx", None, "wt"),
            P("ctx", None, "wt"),
            P("ctx", None, "wt"),
        ),
        check_vma=False,
    )
```

```python
from functools import partial
import math

import jax
import jax.numpy as jnp
from jax import lax
from jax.experimental import pallas as pl
from jax.experimental.pallas import tpu as pltpu
from jax.sharding import PartitionSpec as P

HEAD_DIM = 128
STEP = 3


adam_beta = 0.5
learn_rate = 0.01
decay_rate = 0.1
adam_eps = 1e-08
norm_eps = 1e-05
neg_fill = -1e30
rope_base = 10000.0


def from_behind(x, axis, by):
    count = lax.axis_size(axis)
    pairs = [(i, i + by) for i in range(count) if 0 <= i + by < count]
    return lax.ppermute(x, axis, pairs)


def from_behind_2(value, axis, steps):
    count = lax.axis_size(axis)
    pairs = [(source, (source + steps) % count) for source in range(count)]
    return lax.ppermute(value, axis, pairs)


def layer_norm(values):
    center = values - jnp.mean(values, axis=-1, keepdims=True)
    spread = jnp.mean(center * center, axis=-1, keepdims=True)
    return center * lax.rsqrt(spread + norm_eps)


def rotary(values, positions):
    half_dim = values.shape[-1] // 2
    frequencies = rope_base ** (-jnp.arange(half_dim, dtype=jnp.float32) * (2.0 / values.shape[-1]))
    angles = positions.astype(jnp.float32)[:, None] * frequencies[None, :]
    cosine = jnp.cos(angles)[:, None, :]
    sine_vals = jnp.sin(angles)[:, None, :]
    first_half = values[..., :half_dim]
    second_half = values[..., half_dim:]
    return jnp.concatenate(
        [
            first_half * cosine - second_half * sine_vals,
            second_half * cosine + first_half * sine_vals,
        ],
        axis=-1,
    )


def doc_index(positions, doc_starts):
    return jnp.sum((positions[:, None] >= doc_starts[None, :]).astype(jnp.int32), axis=1) - 1


def heads_dot(spec, left, right):
    return jnp.einsum(spec, left, right, preferred_element_type=jnp.float32)


def general_shards(tokens, cotangent, doc_lengths, owners, master, moment_one, moment_two):
    n_ctx = lax.axis_size("ctx")
    n_wt = lax.axis_size("wt")
    ctx_index = lax.axis_index("ctx")
    tok_rows, width = tokens.shape
    cap_slots, tile_rows, tile_width = master.shape
    n_tiles = owners.shape[0]
    head_dim = HEAD_DIM
    owner_col = owners[:, 0]
    tile_ids = jnp.arange(n_tiles, dtype=jnp.int32)
    earlier = (owner_col[None, :] == owner_col[:, None]) & (tile_ids[None, :] < tile_ids[:, None])
    slot_ids = owner_col * cap_slots + jnp.sum(earlier.astype(jnp.int32), axis=1)
    every_slot = lax.all_gather(master.astype(jnp.bfloat16), "ctx", axis=0, tiled=True)
    flat_w = every_slot[slot_ids].reshape(-1)
    local_width = width // n_wt
    heads_local = local_width // head_dim
    part_q = width * local_width
    ff_local = (flat_w.shape[0] - 4 * part_q) // (3 * width)
    part_f = width * ff_local
    w_qkv = flat_w[: 3 * part_q].reshape(3, width, local_width)
    w_out = flat_w[3 * part_q : 4 * part_q].reshape(local_width, width)
    w_gateup = flat_w[4 * part_q : 4 * part_q + 2 * part_f].reshape(2, width, ff_local)
    w_down = flat_w[4 * part_q + 2 * part_f :].reshape(ff_local, width)
    positions = ctx_index * tok_rows + jnp.arange(tok_rows, dtype=jnp.int32)
    doc_starts = jnp.cumsum(doc_lengths) - doc_lengths
    q_docs = doc_index(positions, doc_starts)
    score_scale = 1.0 / math.sqrt(head_dim)
    inputs = tokens.astype(jnp.float32)
    normed, norm_back = jax.vjp(layer_norm, inputs)
    normed_low = normed.astype(jnp.bfloat16)
    qkv_vals = heads_dot("td,jde->jte", normed_low, w_qkv)
    shaped = qkv_vals.reshape(3, tok_rows, heads_local, head_dim)
    rope_here = partial(rotary, positions=positions)
    qk_rot, rope_back = jax.vjp(rope_here, jnp.concatenate([shaped[0], shaped[1]], axis=1))
    q_low = qk_rot[:, :heads_local].astype(jnp.bfloat16)
    k_low = qk_rot[:, heads_local:].astype(jnp.bfloat16)
    v_low = shaped[2].astype(jnp.bfloat16)

    def masked_scores(key_block, key_pos, key_docs):
        raw_scores = heads_dot("qhd,khd->hqk", q_low, key_block)
        visible_mask = (key_pos[None, :] <= positions[:, None]) & (
            key_docs[None, :] == q_docs[:, None]
        )
        return (jnp.where(visible_mask[None], raw_scores * score_scale, neg_fill), visible_mask)

    def over_blocks(kv_piece, first_row, update_fn, running):
        key_count = kv_piece[0].shape[0]
        block_len = math.gcd(key_count, 512)
        n_blocks = key_count // block_len
        split_kv = tuple(
            (member.reshape((n_blocks, block_len) + member.shape[1:]) for member in kv_piece)
        )

        def step_fn(block_state, inputs_here):
            block_idx, block_vals = inputs_here
            block_row = first_row + block_idx * block_len
            key_pos = block_row + jnp.arange(block_len, dtype=jnp.int32)
            key_docs = doc_index(key_pos, doc_starts)
            block_state = update_fn(block_state, block_vals, key_pos, key_docs, block_row)
            return (block_state, None)

        running, _ = lax.scan(step_fn, running, (jnp.arange(n_blocks, dtype=jnp.int32), split_kv))
        return running

    def norm_update(block_state, block_vals, key_pos, key_docs, block_row):
        row_top, row_total = block_state
        scores, visible_mask = masked_scores(block_vals[0], key_pos, key_docs)
        new_top = jnp.maximum(row_top, jnp.max(scores, axis=-1))
        weights_exp = jnp.where(visible_mask[None], jnp.exp(scores - new_top[:, :, None]), 0.0)
        return (new_top, row_total * jnp.exp(row_top - new_top) + jnp.sum(weights_exp, axis=-1))

    start_top = jnp.full((heads_local, tok_rows), neg_fill, jnp.float32)
    start_total = jnp.zeros((heads_local, tok_rows), jnp.float32)
    row_top, row_total = over_blocks(
        (lax.all_gather(k_low, "ctx", axis=0, tiled=True),),
        jnp.int32(0),
        norm_update,
        (start_top, start_total),
    )
    log_sum = row_top + jnp.log(row_total)

    def block_probs(key_block, key_pos, key_docs):
        scores, visible_mask = masked_scores(key_block, key_pos, key_docs)
        return jnp.where(visible_mask[None], jnp.exp(scores - log_sum[:, :, None]), 0.0)

    def value_update(block_state, block_vals, key_pos, key_docs, block_row):
        prob_vals = block_probs(block_vals[0], key_pos, key_docs)
        return block_state + heads_dot(
            "hqk,khd->qhd", prob_vals.astype(jnp.bfloat16), block_vals[1]
        )

    zero_heads = jnp.zeros((tok_rows, heads_local, head_dim), jnp.float32)
    attended = over_blocks(
        (
            lax.all_gather(k_low, "ctx", axis=0, tiled=True),
            lax.all_gather(v_low, "ctx", axis=0, tiled=True),
        ),
        jnp.int32(0),
        value_update,
        zero_heads,
    )
    att_low = attended.reshape(tok_rows, local_width).astype(jnp.bfloat16)
    attn_part = jnp.dot(att_low, w_out, preferred_element_type=jnp.float32)
    residual = inputs + lax.psum(attn_part.astype(jnp.bfloat16), "wt").astype(jnp.float32)
    normed_two, norm_two_back = jax.vjp(layer_norm, residual)
    normed_two_low = normed_two.astype(jnp.bfloat16)
    gateup_vals = heads_dot("td,jde->jte", normed_two_low, w_gateup)
    gate_vals = gateup_vals[0]
    up_vals = gateup_vals[1]
    gate_sig = jax.nn.sigmoid(gate_vals)
    silu_vals = gate_vals * gate_sig
    hidden_low = (silu_vals * up_vals).astype(jnp.bfloat16)
    mlp_part = jnp.dot(hidden_low, w_down, preferred_element_type=jnp.float32)
    output = (residual + lax.psum(mlp_part.astype(jnp.bfloat16), "wt").astype(jnp.float32)).astype(
        jnp.bfloat16
    )
    out_grad = cotangent.astype(jnp.float32)
    grad_down = heads_dot("tf,td->fd", hidden_low, cotangent)
    grad_hidden = heads_dot("td,fd->tf", cotangent, w_down)
    grad_gate = grad_hidden * up_vals * gate_sig * (1.0 + gate_vals * (1.0 - gate_sig))
    grad_up = grad_hidden * silu_vals
    grad_gu_low = jnp.stack([grad_gate, grad_up]).astype(jnp.bfloat16)
    grad_gateup = heads_dot("td,jte->jde", normed_two_low, grad_gu_low)
    norm_two_part = heads_dot("jte,jde->td", grad_gu_low, w_gateup)
    norm_two_grad = lax.psum(norm_two_part.astype(jnp.bfloat16), "wt").astype(jnp.float32)
    resid_grad = out_grad + norm_two_back(norm_two_grad)[0]
    resid_low = resid_grad.astype(jnp.bfloat16)
    grad_out = heads_dot("tc,td->cd", att_low, resid_low)
    att_grad = heads_dot("td,cd->tc", resid_low, w_out)
    att_grad_low = att_grad.astype(jnp.bfloat16).reshape(tok_rows, heads_local, head_dim)
    row_delta = jnp.sum(att_grad_low * attended, axis=-1).T

    def grad_block(block_vals, key_pos, key_docs):
        prob_vals = block_probs(block_vals[0], key_pos, key_docs)
        value_grad = heads_dot("hqk,qhd->khd", prob_vals.astype(jnp.bfloat16), att_grad_low)
        prob_grad = heads_dot("qhd,khd->hqk", att_grad_low, block_vals[1])
        raw_grad = (prob_vals * (prob_grad - row_delta[:, :, None]) * score_scale).astype(
            jnp.bfloat16
        )
        query_grad = heads_dot("hqk,khd->qhd", raw_grad, block_vals[0])
        key_grad = heads_dot("hqk,qhd->khd", raw_grad, q_low)
        return (query_grad, key_grad, value_grad)

    def add_rows(target, addend):
        return target + addend

    def cycle_step(turn_idx, cycle_state):
        query_acc, key_cur, value_cur, key_acc, value_acc = cycle_state
        anchor = (ctx_index - turn_idx) % n_ctx

        def cycle_update(block_state, block_vals, key_pos, key_docs, block_row):
            q_acc, k_acc, v_acc = block_state
            query_grad, key_grad, value_grad = grad_block(block_vals, key_pos, key_docs)
            return (q_acc + query_grad, add_rows(k_acc, key_grad), add_rows(v_acc, value_grad))

        query_acc, key_acc, value_acc = over_blocks(
            (key_cur, value_cur), anchor * tok_rows, cycle_update, (query_acc, key_acc, value_acc)
        )
        key_cur, value_cur = from_behind((key_cur, value_cur), "ctx", 1)
        key_acc, value_acc = (
            from_behind_2(key_acc.astype(jnp.bfloat16), "ctx", 1).astype(key_acc.dtype),
            from_behind_2(value_acc.astype(jnp.bfloat16), "ctx", 1).astype(value_acc.dtype),
        )
        return (query_acc, key_cur, value_cur, key_acc, value_acc)

    cycle_start = (zero_heads, k_low, v_low, zero_heads, zero_heads)
    query_acc, _, _, key_acc, value_acc = lax.fori_loop(0, n_ctx, cycle_step, cycle_start)
    qk_pre_grad = rope_back(jnp.concatenate([query_acc, key_acc], axis=1))[0]
    qkv_grad_low = jnp.stack(
        [
            qk_pre_grad[:, :heads_local].reshape(tok_rows, local_width),
            qk_pre_grad[:, heads_local:].reshape(tok_rows, local_width),
            value_acc.reshape(tok_rows, local_width),
        ]
    ).astype(jnp.bfloat16)
    grad_qkv = heads_dot("td,jte->jde", normed_low, qkv_grad_low)
    norm_one_part = heads_dot("jte,jde->td", qkv_grad_low, w_qkv)
    norm_one_grad = lax.psum(norm_one_part.astype(jnp.bfloat16), "wt").astype(jnp.float32)
    input_grad = resid_grad + norm_back(norm_one_grad)[0]
    grad_tiles = jnp.concatenate(
        [grad_qkv.reshape(-1), grad_out.reshape(-1), grad_gateup.reshape(-1), grad_down.reshape(-1)]
    ).reshape(n_tiles, tile_rows, tile_width)
    slot_range = jnp.arange(n_ctx * cap_slots, dtype=jnp.int32)
    matches = slot_ids[None, :] == slot_range[:, None]
    tile_of_slot = jnp.sum(jnp.where(matches, tile_ids[None, :], 0), axis=1)
    slot_used = jnp.any(matches, axis=1)
    slot_grads = lax.psum_scatter(
        jnp.where(slot_used[:, None, None], grad_tiles[tile_of_slot], 0.0).astype(jnp.bfloat16),
        "ctx",
        scatter_dimension=0,
        tiled=True,
    ).astype(jnp.float32)
    new_one = adam_beta * moment_one + (1.0 - adam_beta) * slot_grads
    new_two = adam_beta * moment_two + (1.0 - adam_beta) * slot_grads * slot_grads
    bias_one = 1.0 - adam_beta**STEP
    bias_two = 1.0 - adam_beta**STEP
    step_ratio = new_one / bias_one / (jnp.sqrt(new_two / bias_two) + adam_eps)
    new_master = master - learn_rate * (step_ratio + decay_rate * master)
    return (output, input_grad, new_master, new_one, new_two, new_master.astype(jnp.bfloat16))


AXES = ("ctx", "wt")
LOW = jnp.bfloat16
F32 = jnp.float32


def swap(value, ctx_bits, wt_bits):
    n_ctx, n_wt = lax.axis_size("ctx"), lax.axis_size("wt")
    pairs = [
        (c * n_wt + w, (c ^ ctx_bits) * n_wt + (w ^ wt_bits))
        for c in range(n_ctx)
        for w in range(n_wt)
    ]
    return lax.ppermute(value, AXES, pairs)


def dot(left, right):
    return jnp.dot(left, right, preferred_element_type=F32)


def dot_tn(left, right):
    return lax.dot_general(left, right, (((0,), (0,)), ((), ())), preferred_element_type=F32)


def dot_nt(left, right):
    return lax.dot_general(left, right, (((1,), (1,)), ((), ())), preferred_element_type=F32)


def lane_split(value, lane_starts):
    count, rows, width = value.shape
    homes = lane_starts.shape[0] // 2

    def body(starts, src, *outs):
        for home in range(homes):
            for half in range(2):
                start = pl.multiple_of(starts[2 * home + half], 128)
                outs[home][0, :, half * 128 : half * 128 + 128] = src[
                    0, :, pl.ds(start, 128)
                ].astype(LOW)

    return pl.pallas_call(
        body,
        grid_spec=pltpu.PrefetchScalarGridSpec(
            num_scalar_prefetch=1,
            grid=(count,),
            in_specs=[pl.BlockSpec((1, rows, width), lambda i, s: (i, 0, 0))],
            out_specs=[pl.BlockSpec((1, rows, 256), lambda i, s: (i, 0, 0))] * homes,
        ),
        out_shape=[jax.ShapeDtypeStruct((count, rows, 256), LOW)] * homes,
        name="lane_split",
    )(lane_starts, value)


def lane_join(own, other, lane_starts):
    homes, count, rows, _ = own.shape
    width = homes * 512

    def body(starts, own_ref, other_ref, out):
        for home in range(homes):
            for side, ref in ((0, own_ref), (1, other_ref)):
                for half in range(2):
                    start = pl.multiple_of(starts[4 * home + 2 * side + half], 128)
                    out[0, :, pl.ds(start, 128)] = ref[home, 0, :, half * 128 : half * 128 + 128]

    return pl.pallas_call(
        body,
        grid_spec=pltpu.PrefetchScalarGridSpec(
            num_scalar_prefetch=1,
            grid=(count,),
            in_specs=[
                pl.BlockSpec((homes, 1, rows, 256), lambda i, s: (0, i, 0, 0)),
                pl.BlockSpec(
                    (homes, 1, rows, 256), lambda i, s: (0, (i + count // 2) % count, 0, 0)
                ),
            ],
            out_specs=pl.BlockSpec((1, rows, width), lambda i, s: (i, 0, 0)),
        ),
        out_shape=jax.ShapeDtypeStruct((count, rows, width), LOW),
        name="lane_join",
    )(lane_starts, own, other)


def lane_halves(value, lane_starts):
    count, rows, width = value.shape
    homes = width // 512

    def body(starts, src, own_ref, other_ref):
        for home in range(homes):
            for side, ref in ((0, own_ref), (1, other_ref)):
                for half in range(2):
                    start = pl.multiple_of(starts[4 * home + 2 * side + half], 128)
                    ref[home, 0, :, half * 128 : half * 128 + 128] = src[
                        0, :, pl.ds(start, 128)
                    ].astype(ref.dtype)

    return pl.pallas_call(
        body,
        grid_spec=pltpu.PrefetchScalarGridSpec(
            num_scalar_prefetch=1,
            grid=(count,),
            in_specs=[pl.BlockSpec((1, rows, width), lambda i, s: (i, 0, 0))],
            out_specs=[
                pl.BlockSpec((homes, 1, rows, 256), lambda i, s: (0, i, 0, 0)),
                pl.BlockSpec(
                    (homes, 1, rows, 256), lambda i, s: (0, (i + count // 2) % count, 0, 0)
                ),
            ],
        ),
        out_shape=[
            jax.ShapeDtypeStruct((homes, count, rows, 256), dtype) for dtype in (F32, LOW)
        ],
        name="lane_halves",
    )(lane_starts, value)


def return_halves(grad, lane_starts):
    own, other = lane_halves(grad, lane_starts)
    back = swap(other, 1, 0)
    sums = [(own[m] + back[m].astype(F32)).astype(LOW) for m in range(4)]
    return [sums[0]] + [swap(sums[m], 2 * m, 0) for m in (1, 2, 3)]


def join_grads(query, kv, kv_back, cosine, sine):
    def body(q, here, there, cos, sin, out):
        def undo(values):
            return values * cos[...] + pltpu.roll(values, 64, 1) * sin[...]

        total = here[...] + there[...].astype(F32)
        out[:, :128] = undo(q[...]).astype(LOW)
        out[:, 128:256] = undo(total[:, :128]).astype(LOW)
        out[:, 256:] = total[:, 128:].astype(LOW)

    return pl.pallas_call(
        body,
        in_specs=[VMEM_SPEC] * 5,
        out_specs=VMEM_SPEC,
        out_shape=jax.ShapeDtypeStruct((query.shape[0], 384), LOW),
        name="join_grads",
    )(query, kv, kv_back, cosine, sine)


VMEM_SPEC = pl.BlockSpec(memory_space=pltpu.VMEM)
SMEM_SPEC = pl.BlockSpec(memory_space=pltpu.SMEM)
ANY_SPEC = pl.BlockSpec(memory_space=pl.ANY)


def pick_qkv(came, picked, rows):
    n_src = len(came)

    def body(which, where, *refs):
        srcs, out = refs[:n_src], refs[n_src]

        def copy(tile, carry):
            for n in range(n_src):

                @pl.when(which[tile] == n)
                def _(n=n):
                    for half in range(2):
                        row = pl.multiple_of(half * 512 + (tile % 4) * 128, 128)
                        lane = pl.multiple_of((tile // 4) * 128, 128)
                        out[pl.ds(row, 128), pl.ds(lane, 128)] = srcs[n][
                            where[tile], :, half * 128 : half * 128 + 128
                        ]

            return carry

        lax.fori_loop(0, 12, copy, 0)

    return pl.pallas_call(
        body,
        in_specs=[SMEM_SPEC, SMEM_SPEC] + [VMEM_SPEC] * n_src,
        out_specs=VMEM_SPEC,
        out_shape=jax.ShapeDtypeStruct((1024, 384), LOW),
        name="pick_qkv",
    )(picked, rows, *came)


def row_gather(sources, picked, rows, sizes):
    total = sum(sizes)
    n_src = len(sources)

    def body(which, where, *refs):
        srcs, outs, sem = refs[:n_src], refs[n_src:-1], refs[-1]
        first = 0
        for out, size in zip(outs, sizes):

            def start(j, carry, out=out, first=first):
                t = first + j
                for n in range(n_src):

                    @pl.when(which[t] == n)
                    def _(n=n):
                        pltpu.make_async_copy(srcs[n].at[where[t]], out.at[j], sem.at[t]).start()

                return carry

            lax.fori_loop(0, size, start, 0)
            first += size
        first = 0
        for out, size in zip(outs, sizes):

            def finish(j, carry, out=out, first=first):
                pltpu.make_async_copy(srcs[0].at[0], out.at[j], sem.at[first + j]).wait()
                return carry

            lax.fori_loop(0, size, finish, 0)
            first += size

    tail = sources[0].shape[1:]
    return pl.pallas_call(
        body,
        in_specs=[SMEM_SPEC, SMEM_SPEC] + [VMEM_SPEC] * n_src,
        out_specs=[ANY_SPEC] * len(sizes),
        out_shape=[jax.ShapeDtypeStruct((size,) + tail, LOW) for size in sizes],
        scratch_shapes=[pltpu.SemaphoreType.DMA((total,))],
        name="row_gather",
    )(picked, rows, *sources)


def send_tile(src, tile, to, row, outs, sem):
    for n, out in enumerate(outs):

        @pl.when(to[tile] == n)
        def _(out=out):
            pltpu.make_async_copy(src, out.at[row[tile]], sem.at[tile]).start()


def place_mlp(gate_up, downs, to, row, place, sizes):
    def body(to_ref, row_ref, z_ref, gu_ref, *refs):
        down_refs, outs, sem = refs[:4], refs[4:-1], refs[-1]
        down_tile = lambda m, k: 48 + 4 * ((k + 2 * z_ref[1]) % 4) + (z_ref[0] ^ m)

        def start(j, carry):
            at = pl.ds(pl.multiple_of(128 * j, 128), 128)
            for half in range(2):
                src = gu_ref.at[at, pl.ds(256 * half, 256)]
                send_tile(src, 16 + 16 * half + j, to_ref, row_ref, outs, sem)
            return carry

        lax.fori_loop(0, 16, start, 0)
        for m in range(4):

            def start_down(k, carry, m=m):
                send_tile(down_refs[m].at[k], down_tile(m, k), to_ref, row_ref, outs, sem)
                return carry

            lax.fori_loop(0, 4, start_down, 0)

        def finish(tile, carry):
            pltpu.make_async_copy(down_refs[0].at[0], outs[0].at[0], sem.at[tile]).wait()
            return carry

        lax.fori_loop(16, 64, finish, 0)

    return pl.pallas_call(
        body,
        in_specs=[SMEM_SPEC] * 3 + [VMEM_SPEC] * 5,
        out_specs=[ANY_SPEC] * len(sizes),
        out_shape=[jax.ShapeDtypeStruct((size, 128, 256), LOW) for size in sizes],
        scratch_shapes=[pltpu.SemaphoreType.DMA((64,))],
        name="place_mlp",
    )(to, row, place, gate_up, *downs)


def place_attention(buffers, qkv, outs_from, to, row, place):
    count = len(buffers)

    def body(to_ref, row_ref, z_ref, qkv_ref, *refs):
        out_refs, outs = refs[:4], refs[4 + count : 4 + 2 * count]
        tiles, sem = refs[-2:]

        def start(tile, carry):
            lane = pl.multiple_of((tile // 4) * 128, 128)
            for half in range(2):
                at = pl.ds(pl.multiple_of(half * 512 + (tile % 4) * 128, 128), 128)
                tiles[tile, :, half * 128 : half * 128 + 128] = qkv_ref[at, pl.ds(lane, 128)]
            return carry

        lax.fori_loop(0, 12, start, 0)

        def start_copy(tile, carry):
            send_tile(tiles.at[tile], tile, to_ref, row_ref, outs, sem)
            return carry

        for m in range(4):
            send_tile(out_refs[m].at[0], 12 + (z_ref[0] ^ m), to_ref, row_ref, outs, sem)
        lax.fori_loop(0, 12, start_copy, 0)

        def finish(tile, carry):
            pltpu.make_async_copy(tiles.at[0], outs[0].at[0], sem.at[tile]).wait()
            return carry

        lax.fori_loop(0, 16, finish, 0)

    return pl.pallas_call(
        body,
        in_specs=[SMEM_SPEC] * 3 + [VMEM_SPEC] * 5 + [ANY_SPEC] * count,
        out_specs=[ANY_SPEC] * count,
        out_shape=[jax.ShapeDtypeStruct(buf.shape, buf.dtype) for buf in buffers],
        scratch_shapes=[pltpu.VMEM((12, 128, 256), LOW), pltpu.SemaphoreType.DMA((16,))],
        input_output_aliases={8 + n: n for n in range(count)},
        name="place_attention",
    )(to, row, place, qkv, *outs_from, *buffers)


def after(value, *earlier):
    return lax.optimization_barrier((value,) + earlier)[0]


def key_scores(q, here, there, masks):
    qp, qd, kp, kd = masks
    raw = jnp.concatenate([dot_nt(q, here[:, :128]), dot_nt(q, there[:, :128])], axis=1)
    seen = (kp[...] <= qp[...]) & (kd[...] == qd[...])
    return jnp.where(seen, raw * (1.0 / math.sqrt(HEAD_DIM)), neg_fill)


def attend(query, here, there, masks, n_blocks):
    rows = query.shape[0]
    block = rows // n_blocks

    def body(q, kv, kv_there, qp, qd, kp, kd, out, lse):
        scores = key_scores(q[...], kv[...], kv_there[...], (qp, qd, kp, kd))
        top = jnp.max(scores, axis=1, keepdims=True)
        weights = jnp.exp(scores - top)
        total = jnp.sum(weights, axis=1, keepdims=True)
        probs = (weights * (1.0 / total)).astype(LOW)
        mixed = dot(probs[:, :rows], kv[:, 128:]) + dot(probs[:, rows:], kv_there[:, 128:])
        out[...] = mixed.astype(LOW)
        lse[...] = top + jnp.log(total)

    whole = lambda arr: pl.BlockSpec(arr.shape, lambda i: (0, 0))
    part = lambda arr: pl.BlockSpec((block, arr.shape[1]), lambda i: (i, 0))
    q_pos, q_doc, k_pos, k_doc = masks
    return pl.pallas_call(
        body,
        grid=(n_blocks,),
        in_specs=[
            part(query), whole(here), whole(there), part(q_pos), part(q_doc), whole(k_pos), whole(k_doc),
        ],
        out_specs=[
            pl.BlockSpec((block, HEAD_DIM), lambda i: (i, 0)),
            pl.BlockSpec((block, 1), lambda i: (i, 0)),
        ],
        out_shape=[
            jax.ShapeDtypeStruct((rows, HEAD_DIM), LOW),
            jax.ShapeDtypeStruct((rows, 1), F32),
        ],
        name="attend",
    )(query, here, there, *masks)


def attend_back(query, here, there, out_grad, lse, masks, n_blocks):
    rows = query.shape[0]
    block = rows // n_blocks

    def body(q, kv, kv_there, do, ls, qp, qd, kp, kd, dq, d_here, d_there, acc):
        step = pl.program_id(0)

        @pl.when(step == 0)
        def _():
            d_here[...] = jnp.zeros_like(d_here)
            acc[...] = jnp.zeros_like(acc)

        scores = key_scores(q[...], kv[...], kv_there[...], (qp, qd, kp, kd))
        probs = jnp.exp(scores - ls[...])
        prob_grad = jnp.concatenate(
            [dot_nt(do[...], kv[:, 128:]), dot_nt(do[...], kv_there[:, 128:])], axis=1
        )
        delta = jnp.sum(probs * prob_grad, axis=1, keepdims=True)
        score_grad = (probs * (prob_grad - delta) * (1.0 / math.sqrt(HEAD_DIM))).astype(LOW)
        probs_low = probs.astype(LOW)
        dq[...] = dot(score_grad[:, :rows], kv[:, :128]) + dot(
            score_grad[:, rows:], kv_there[:, :128]
        )
        for first, out in ((0, d_here), (rows, acc)):
            out[:, :128] += dot_tn(score_grad[:, first : first + rows], q[...])
            out[:, 128:] += dot_tn(probs_low[:, first : first + rows], do[...])

        @pl.when(step == n_blocks - 1)
        def _():
            d_there[...] = acc[...].astype(LOW)

    whole = lambda arr: pl.BlockSpec(arr.shape, lambda i: (0, 0))
    part = lambda arr: pl.BlockSpec((block, arr.shape[1]), lambda i: (i, 0))
    kept = pl.BlockSpec((rows, 2 * HEAD_DIM), lambda i: (0, 0))
    q_pos, q_doc, k_pos, k_doc = masks
    return pl.pallas_call(
        body,
        grid=(n_blocks,),
        in_specs=[
            part(query), whole(here), whole(there), part(out_grad), part(lse),
            part(q_pos), part(q_doc), whole(k_pos), whole(k_doc),
        ],
        out_specs=[pl.BlockSpec((block, HEAD_DIM), lambda i: (i, 0)), kept, kept],
        out_shape=[
            jax.ShapeDtypeStruct((rows, HEAD_DIM), F32),
            jax.ShapeDtypeStruct((rows, 2 * HEAD_DIM), F32),
            jax.ShapeDtypeStruct((rows, 2 * HEAD_DIM), LOW),
        ],
        scratch_shapes=[pltpu.VMEM((rows, 2 * HEAD_DIM), F32)],
        name="attend_back",
    )(query, here, there, out_grad, lse, *masks)


def update(state, pieces, lane_starts, used, first, done):
    rows, width = state[0].shape[1:]
    count, homes = pieces[0].shape[0], len(pieces)
    bias = 1.0 - adam_beta**STEP

    def body(starts, live, mas, one, two, *refs):
        grads, (new_mas, new_one, new_two, copy) = refs[:homes], refs[-4:]
        alive = live[pl.program_id(0) + first] > 0
        for home in range(homes):
            for half in range(2):
                at = (0, slice(None), pl.ds(pl.multiple_of(starts[2 * home + half], 128), 128))
                grad = grads[home][0, :, half * 128 : half * 128 + 128].astype(F32)
                grad = jnp.where(alive, grad, 0.0)
                mean = adam_beta * one[at] + (1.0 - adam_beta) * grad
                square = adam_beta * two[at] + (1.0 - adam_beta) * grad * grad
                ratio = (mean * (1.0 / bias)) / (jnp.sqrt(square * (1.0 / bias)) + adam_eps)
                old = mas[at]
                new = old - learn_rate * (ratio + decay_rate * old)
                new_mas[at] = new
                new_one[at] = mean
                new_two[at] = square
                copy[at] = new.astype(LOW)

    slot = pl.BlockSpec((1, rows, width), lambda i, s, u: (i + first, 0, 0))
    piece = pl.BlockSpec((1, rows, 256), lambda i, s, u: (i, 0, 0))
    shape = state[0].shape
    return pl.pallas_call(
        body,
        grid_spec=pltpu.PrefetchScalarGridSpec(
            num_scalar_prefetch=2,
            grid=(count,),
            in_specs=[slot] * 3 + [piece] * homes + [ANY_SPEC] * len(done),
            out_specs=[slot] * 4,
        ),
        out_shape=[jax.ShapeDtypeStruct(shape, F32)] * 3 + [jax.ShapeDtypeStruct(shape, LOW)],
        input_output_aliases={5 + homes + n: n for n in range(len(done))},
        name="update",
    )(lane_starts, used, *state, *pieces, *done)


def stack_rows(blocks):
    rows, width = blocks[0].shape

    def body(*refs):
        for n, ref in enumerate(refs[:-1]):
            refs[-1][n * rows : (n + 1) * rows] = ref[...]

    return pl.pallas_call(
        body,
        in_specs=[VMEM_SPEC] * len(blocks),
        out_specs=VMEM_SPEC,
        out_shape=jax.ShapeDtypeStruct((len(blocks) * rows, width), LOW),
        name="stack_rows",
    )(*blocks)


def gather_rows(piece):
    near = [piece] + [swap(piece, 2 * k, 0) for k in (1, 2, 3)]
    blocks = []
    for part in near:
        pair = jnp.concatenate([part, swap(part, 0, 2)])
        blocks += [pair, swap(pair, 0, 1)]
    return stack_rows(blocks), near[1:]


def scatter_sum(partial_sum):
    quarter = partial_sum.shape[0] // 4
    half, rows = quarter // 2, quarter // 4
    kept = [None] * 4
    for k in (3, 2, 1, 0):
        chunk = partial_sum[quarter * k : quarter * (k + 1)]
        other = swap(chunk[half:].astype(LOW), 0, 1)
        pair = chunk[:half].astype(F32) + other.astype(F32)
        other = swap(pair[rows:].astype(LOW), 0, 2)
        kept[k] = pair[:rows] + other.astype(F32)
    total = kept[0]
    came = [swap(kept[k].astype(LOW), 2 * k, 0) for k in (3, 2, 1)]
    for part in came:
        total = total + part.astype(F32)
    return total, other


def share_rows(piece, wt_index):
    rows = piece.shape[0]
    out = jnp.zeros((4 * rows,) + piece.shape[1:], piece.dtype)
    over_y = swap(piece, 0, 2)
    over_core, over_both = swap(piece, 0, 1), swap(over_y, 0, 1)
    for bits, part in ((0, piece), (2, over_y), (1, over_core), (3, over_both)):
        out = lax.dynamic_update_slice(out, part, ((wt_index ^ bits) * rows, 0))
    return out


def rotate(values, cosine, sine):
    half = values.shape[-1] // 2
    first, second = values[:, :half], values[:, half:]
    return jnp.concatenate([first * cosine - second * sine, second * cosine + first * sine], axis=1)


def fast_shards(tokens, cotangent, doc_lengths, owners, master, moment_one, moment_two):
    ctx, wt = lax.axis_index("ctx"), lax.axis_index("wt")
    z_at, x_at = ctx // 2, ctx % 2
    tok_rows, width = tokens.shape
    cap, tile_rows, _ = master.shape
    n_tiles = owners.shape[0]
    rows = tok_rows // 4
    bits = jnp.arange(4, dtype=jnp.int32)
    homes = jnp.arange(8, dtype=jnp.int32) ^ ctx
    lane_starts = (
        ((2 * (homes % 2))[:, None] + jnp.arange(2, dtype=jnp.int32)) * 4 + (homes // 2)[:, None]
    ).reshape(-1) * 128

    owner_col = owners[:, 0]
    tile_ids = jnp.arange(n_tiles, dtype=jnp.int32)
    earlier = (owner_col[None, :] == owner_col[:, None]) & (tile_ids[None, :] < tile_ids[:, None])
    slot_in_owner = jnp.sum(earlier.astype(jnp.int32), axis=1)
    owner_bits = owner_col ^ ctx

    def to_cut_order(values):
        cut_vals = values.reshape(-1, width // 4, 4).transpose(0, 2, 1).reshape(-1, width)
        flipped = jnp.concatenate([cut_vals[:, width // 2 :], cut_vals[:, : width // 2]], axis=1)
        return jnp.where(x_at == 0, cut_vals, flipped)

    def from_cut_order(values):
        flipped = jnp.concatenate([values[:, width // 2 :], values[:, : width // 2]], axis=1)
        cut_vals = jnp.where(x_at == 0, values, flipped)
        return cut_vals.reshape(-1, 4, width // 4).transpose(0, 2, 1).reshape(-1, width)

    cut = lane_split(master, lane_starts)
    came = [cut[0]] + [swap(cut[k], k, 0) for k in range(1, 8)]
    tokens_later = after(tokens, cut[0])
    inputs = lax.dynamic_slice(tokens_later, (wt * rows, 0), (rows, width)).astype(F32)
    normed, norm_back = jax.vjp(layer_norm, inputs)
    normed_cut = to_cut_order(normed.astype(LOW))
    normed_all, normed_came = gather_rows(after(normed_cut, came[4], came[5], came[6]))
    w_qkv = pick_qkv(came, owner_bits[:12], slot_in_owner[:12])
    w_qkv_pair = swap(w_qkv, 1, 0)
    out_grad_low = lax.dynamic_slice(cotangent, (wt * rows, 0), (rows, width))
    grad_all, _ = gather_rows(after(out_grad_low, w_qkv, *normed_came))
    wanted = jnp.concatenate(
        [
            jnp.arange(16, 48, dtype=jnp.int32),
            12 + (z_at ^ bits),
            (48 + 4 * ((bits + 2 * x_at) % 4)[None, :] + (z_at ^ bits)[:, None]).reshape(-1),
        ]
    )
    wanted = after(wanted, w_qkv)
    home_gate, home_up, *sends = row_gather(
        came, owner_bits[wanted], slot_in_owner[wanted], [16, 16] + [1] * 4 + [4] * 4
    )
    out_came = [sends[0]] + [swap(sends[m], 2 * m, 0) for m in (1, 2, 3)]
    down_here = [sends[4]] + [swap(sends[4 + m], 2 * m, 0) for m in (1, 2, 3)]
    down_here = jnp.stack(down_here)

    block_z = z_at ^ bits
    block_w = wt ^ jnp.array([0, 2, 1, 3], jnp.int32)

    def group_positions(x_index):
        starts = (2 * block_z + x_index)[:, None] * tok_rows + block_w[None, :] * rows
        return (starts.reshape(-1)[:, None] + jnp.arange(rows, dtype=jnp.int32)).reshape(-1)

    q_pos = group_positions(x_at)
    k_pos = jnp.concatenate([q_pos, group_positions(1 - x_at)])
    doc_starts = jnp.cumsum(doc_lengths) - doc_lengths
    q_doc, k_doc = doc_index(q_pos, doc_starts), doc_index(k_pos, doc_starts)
    masks = (q_pos[:, None], q_doc[:, None], k_pos[None, :], k_doc[None, :])
    freqs = rope_base ** (-jnp.arange(HEAD_DIM // 2, dtype=F32) * (2.0 / HEAD_DIM))
    angles = q_pos.astype(F32)[:, None] * freqs[None, :]
    cosine, sine = jnp.cos(angles), jnp.sin(angles)

    half = width // 2
    qkv = dot(normed_all[:, :half], w_qkv) + dot(normed_all[:, half:], w_qkv_pair)
    query = rotate(qkv[:, :128], cosine, sine).astype(LOW)
    kv_here = jnp.concatenate(
        [rotate(qkv[:, 128:256], cosine, sine).astype(LOW), qkv[:, 256:].astype(LOW)], axis=1
    )
    kv_there = swap(kv_here, 1, 0)
    out_here = after(jnp.stack(out_came), kv_here)
    out_there = swap(out_here, 1, 0)
    att_low, lse = attend(query, kv_here, kv_there, masks, 4)
    w_out = lane_join(out_here, out_there, lane_starts).reshape(tile_rows, width)

    gate_later, up_later = lax.optimization_barrier((home_gate, home_up, kv_there))[:2]
    pair_gate, pair_up = swap(gate_later, 1, 0), swap(up_later, 1, 0)
    down_there = swap(after(down_here, kv_there), 1, 0)
    w_down = lane_join(down_here, down_there, lane_starts).reshape(512, width)
    w_gu = jnp.concatenate(
        [part.reshape(width, 256) for part in (home_gate, home_up, pair_gate, pair_up)], axis=1
    )
    att_part = dot(att_low, w_out).astype(LOW)
    att_out, _ = scatter_sum(att_part)
    residual = inputs + att_out

    normed_two, norm_two_back = jax.vjp(layer_norm, residual)
    two_all, _ = gather_rows(normed_two.astype(LOW))
    gu = dot(two_all, w_gu)
    gate = jnp.concatenate([gu[:, :256], gu[:, 512:768]], axis=1)
    up = jnp.concatenate([gu[:, 256:512], gu[:, 768:]], axis=1)
    gate_sig = jax.nn.sigmoid(gate)
    silu = gate * gate_sig
    hidden = (silu * up).astype(LOW)

    hidden_grad = dot_nt(grad_all, w_down)
    grad_gate = (hidden_grad * up * gate_sig * (1.0 + gate * (1.0 - gate_sig))).astype(LOW)
    grad_up = (hidden_grad * silu).astype(LOW)
    grad_gu = jnp.concatenate(
        [grad_gate[:, :256], grad_up[:, :256], grad_gate[:, 256:], grad_up[:, 256:]], axis=1
    )
    two_grad, begun = scatter_sum(dot_nt(grad_gu, w_gu).astype(LOW))
    hidden_later = after(hidden, begun)
    grad_w_down = dot_tn(hidden_later, grad_all)

    resid_grad = out_grad_low.astype(F32) + norm_two_back(two_grad)[0]
    resid_all, _ = gather_rows(resid_grad.astype(LOW))
    grad_w_gu = dot_tn(two_all, after(grad_gu, two_grad))
    gu_back = swap(grad_w_gu[:, 512:].astype(LOW), 1, 0)
    down, _ = scatter_sum(dot(after(hidden, two_grad), w_down).astype(LOW))
    output = share_rows((residual + down).astype(LOW), wt)
    gu_sum = (grad_w_gu[:, :512] + gu_back.astype(F32)).astype(LOW)
    down_came = return_halves(grad_w_down.reshape(4, tile_rows, width), lane_starts)

    part_slots = cap * 2 // 3
    send_to = owner_bits + 8 * (slot_in_owner // part_slots)
    send_row = slot_in_owner % part_slots
    place = jnp.stack([z_at, x_at])
    sends = place_mlp(
        gu_sum, down_came, send_to, send_row, place, [part_slots] * 8 + [cap - part_slots] * 8
    )

    att_grad = dot_nt(resid_all, w_out).astype(LOW)
    out_grad_came = return_halves(
        dot_tn(att_low, resid_all).reshape(1, tile_rows, width), lane_starts
    )
    query_grad, kv_grad, kv_grad_there = attend_back(
        query, kv_here, kv_there, att_grad, lse, masks, 4
    )
    kv_grad_back = swap(kv_grad_there, 1, 0)
    qkv_grad = join_grads(
        query_grad,
        kv_grad,
        kv_grad_back,
        jnp.concatenate([cosine, cosine], axis=1),
        jnp.concatenate([sine, -sine], axis=1),
    )
    qkv_back = swap(dot_tn(normed_all[:, half:], qkv_grad).astype(LOW), 1, 0)
    qkv_sum = (dot_tn(normed_all[:, :half], qkv_grad) + qkv_back.astype(F32)).astype(LOW)
    sends = place_attention(sends, qkv_sum, out_grad_came, send_to, send_row, place)

    qkv_grad_later = after(qkv_grad, sends[0])
    one_part = jnp.concatenate(
        [dot_nt(qkv_grad_later, w_qkv), dot_nt(qkv_grad_later, w_qkv_pair)], axis=1
    )
    one_grad = from_cut_order(scatter_sum(one_part.astype(LOW))[0])
    input_grad = resid_grad + norm_back(one_grad)[0]
    input_grad = share_rows(input_grad.astype(LOW), wt)
    input_grad = input_grad.astype(F32)

    slot_range = jnp.arange(cap, dtype=jnp.int32) + ctx * cap
    used = jnp.any(
        (owner_col * cap + slot_in_owner)[None, :] == slot_range[:, None], axis=1
    ).astype(jnp.int32)
    state = (master, moment_one, moment_two)
    first, second = [sends[0]], [sends[8]]
    first += [swap(sends[k], k, 0) for k in range(1, 8)]
    for k in range(1, 8):
        second.append(swap(after(sends[8 + k], first[k]), k, 0))
    done = update(state, first, lane_starts, used, 0, ())
    done = update(state, second, lane_starts, used, part_slots, tuple(done))
    return (output, input_grad) + tuple(done)


def choose_shards(*args):
    sizes = (lax.axis_size("ctx"), lax.axis_size("wt"), args[0].shape, args[4].shape[1:])
    if sizes == (8, 4, (256, 2048), (128, 2048)) and args[3].shape[0] == 64:
        return fast_shards(*args)
    return general_shards(*args)


def solution(mesh):
    placed = (
        P("ctx", None),
        P("ctx", None),
        P(),
        P(),
        P("ctx", None, "wt"),
        P("ctx", None, "wt"),
        P("ctx", None, "wt"),
    )
    return jax.shard_map(
        choose_shards,
        mesh=mesh,
        in_specs=placed,
        out_specs=(
            P("ctx", None),
            P("ctx", None),
            P("ctx", None, "wt"),
            P("ctx", None, "wt"),
            P("ctx", None, "wt"),
            P("ctx", None, "wt"),
        ),
        check_vma=False,
    )
```

```python
from functools import partial
import math

import jax
import jax.numpy as jnp
from jax import lax
from jax.experimental import pallas as pl
from jax.experimental.pallas import tpu as pltpu
from jax.sharding import PartitionSpec as P

HEAD_DIM = 128
STEP = 3


adam_beta = 0.5
learn_rate = 0.01
decay_rate = 0.1
adam_eps = 1e-08
norm_eps = 1e-05
neg_fill = -1e30
rope_base = 10000.0


def from_behind(x, axis, by):
    count = lax.axis_size(axis)
    pairs = [(i, i + by) for i in range(count) if 0 <= i + by < count]
    return lax.ppermute(x, axis, pairs)


def from_behind_2(value, axis, steps):
    count = lax.axis_size(axis)
    pairs = [(source, (source + steps) % count) for source in range(count)]
    return lax.ppermute(value, axis, pairs)


def layer_norm(values):
    center = values - jnp.mean(values, axis=-1, keepdims=True)
    spread = jnp.mean(center * center, axis=-1, keepdims=True)
    return center * lax.rsqrt(spread + norm_eps)


def rotary(values, positions):
    half_dim = values.shape[-1] // 2
    frequencies = rope_base ** (-jnp.arange(half_dim, dtype=jnp.float32) * (2.0 / values.shape[-1]))
    angles = positions.astype(jnp.float32)[:, None] * frequencies[None, :]
    cosine = jnp.cos(angles)[:, None, :]
    sine_vals = jnp.sin(angles)[:, None, :]
    first_half = values[..., :half_dim]
    second_half = values[..., half_dim:]
    return jnp.concatenate(
        [
            first_half * cosine - second_half * sine_vals,
            second_half * cosine + first_half * sine_vals,
        ],
        axis=-1,
    )


def doc_index(positions, doc_starts):
    return jnp.sum((positions[:, None] >= doc_starts[None, :]).astype(jnp.int32), axis=1) - 1


def heads_dot(spec, left, right):
    return jnp.einsum(spec, left, right, preferred_element_type=jnp.float32)


def general_shards(tokens, cotangent, doc_lengths, owners, master, moment_one, moment_two):
    n_ctx = lax.axis_size("ctx")
    n_wt = lax.axis_size("wt")
    ctx_index = lax.axis_index("ctx")
    tok_rows, width = tokens.shape
    cap_slots, tile_rows, tile_width = master.shape
    n_tiles = owners.shape[0]
    head_dim = HEAD_DIM
    owner_col = owners[:, 0]
    tile_ids = jnp.arange(n_tiles, dtype=jnp.int32)
    earlier = (owner_col[None, :] == owner_col[:, None]) & (tile_ids[None, :] < tile_ids[:, None])
    slot_ids = owner_col * cap_slots + jnp.sum(earlier.astype(jnp.int32), axis=1)
    every_slot = lax.all_gather(master.astype(jnp.bfloat16), "ctx", axis=0, tiled=True)
    flat_w = every_slot[slot_ids].reshape(-1)
    local_width = width // n_wt
    heads_local = local_width // head_dim
    part_q = width * local_width
    ff_local = (flat_w.shape[0] - 4 * part_q) // (3 * width)
    part_f = width * ff_local
    w_qkv = flat_w[: 3 * part_q].reshape(3, width, local_width)
    w_out = flat_w[3 * part_q : 4 * part_q].reshape(local_width, width)
    w_gateup = flat_w[4 * part_q : 4 * part_q + 2 * part_f].reshape(2, width, ff_local)
    w_down = flat_w[4 * part_q + 2 * part_f :].reshape(ff_local, width)
    positions = ctx_index * tok_rows + jnp.arange(tok_rows, dtype=jnp.int32)
    doc_starts = jnp.cumsum(doc_lengths) - doc_lengths
    q_docs = doc_index(positions, doc_starts)
    score_scale = 1.0 / math.sqrt(head_dim)
    inputs = tokens.astype(jnp.float32)
    normed, norm_back = jax.vjp(layer_norm, inputs)
    normed_low = normed.astype(jnp.bfloat16)
    qkv_vals = heads_dot("td,jde->jte", normed_low, w_qkv)
    shaped = qkv_vals.reshape(3, tok_rows, heads_local, head_dim)
    rope_here = partial(rotary, positions=positions)
    qk_rot, rope_back = jax.vjp(rope_here, jnp.concatenate([shaped[0], shaped[1]], axis=1))
    q_low = qk_rot[:, :heads_local].astype(jnp.bfloat16)
    k_low = qk_rot[:, heads_local:].astype(jnp.bfloat16)
    v_low = shaped[2].astype(jnp.bfloat16)

    def masked_scores(key_block, key_pos, key_docs):
        raw_scores = heads_dot("qhd,khd->hqk", q_low, key_block)
        visible_mask = (key_pos[None, :] <= positions[:, None]) & (
            key_docs[None, :] == q_docs[:, None]
        )
        return (jnp.where(visible_mask[None], raw_scores * score_scale, neg_fill), visible_mask)

    def over_blocks(kv_piece, first_row, update_fn, running):
        key_count = kv_piece[0].shape[0]
        block_len = math.gcd(key_count, 512)
        n_blocks = key_count // block_len
        split_kv = tuple(
            (member.reshape((n_blocks, block_len) + member.shape[1:]) for member in kv_piece)
        )

        def step_fn(block_state, inputs_here):
            block_idx, block_vals = inputs_here
            block_row = first_row + block_idx * block_len
            key_pos = block_row + jnp.arange(block_len, dtype=jnp.int32)
            key_docs = doc_index(key_pos, doc_starts)
            block_state = update_fn(block_state, block_vals, key_pos, key_docs, block_row)
            return (block_state, None)

        running, _ = lax.scan(step_fn, running, (jnp.arange(n_blocks, dtype=jnp.int32), split_kv))
        return running

    def norm_update(block_state, block_vals, key_pos, key_docs, block_row):
        row_top, row_total = block_state
        scores, visible_mask = masked_scores(block_vals[0], key_pos, key_docs)
        new_top = jnp.maximum(row_top, jnp.max(scores, axis=-1))
        weights_exp = jnp.where(visible_mask[None], jnp.exp(scores - new_top[:, :, None]), 0.0)
        return (new_top, row_total * jnp.exp(row_top - new_top) + jnp.sum(weights_exp, axis=-1))

    start_top = jnp.full((heads_local, tok_rows), neg_fill, jnp.float32)
    start_total = jnp.zeros((heads_local, tok_rows), jnp.float32)
    row_top, row_total = over_blocks(
        (lax.all_gather(k_low, "ctx", axis=0, tiled=True),),
        jnp.int32(0),
        norm_update,
        (start_top, start_total),
    )
    log_sum = row_top + jnp.log(row_total)

    def block_probs(key_block, key_pos, key_docs):
        scores, visible_mask = masked_scores(key_block, key_pos, key_docs)
        return jnp.where(visible_mask[None], jnp.exp(scores - log_sum[:, :, None]), 0.0)

    def value_update(block_state, block_vals, key_pos, key_docs, block_row):
        prob_vals = block_probs(block_vals[0], key_pos, key_docs)
        return block_state + heads_dot(
            "hqk,khd->qhd", prob_vals.astype(jnp.bfloat16), block_vals[1]
        )

    zero_heads = jnp.zeros((tok_rows, heads_local, head_dim), jnp.float32)
    attended = over_blocks(
        (
            lax.all_gather(k_low, "ctx", axis=0, tiled=True),
            lax.all_gather(v_low, "ctx", axis=0, tiled=True),
        ),
        jnp.int32(0),
        value_update,
        zero_heads,
    )
    att_low = attended.reshape(tok_rows, local_width).astype(jnp.bfloat16)
    attn_part = jnp.dot(att_low, w_out, preferred_element_type=jnp.float32)
    residual = inputs + lax.psum(attn_part.astype(jnp.bfloat16), "wt").astype(jnp.float32)
    normed_two, norm_two_back = jax.vjp(layer_norm, residual)
    normed_two_low = normed_two.astype(jnp.bfloat16)
    gateup_vals = heads_dot("td,jde->jte", normed_two_low, w_gateup)
    gate_vals = gateup_vals[0]
    up_vals = gateup_vals[1]
    gate_sig = jax.nn.sigmoid(gate_vals)
    silu_vals = gate_vals * gate_sig
    hidden_low = (silu_vals * up_vals).astype(jnp.bfloat16)
    mlp_part = jnp.dot(hidden_low, w_down, preferred_element_type=jnp.float32)
    output = (residual + lax.psum(mlp_part.astype(jnp.bfloat16), "wt").astype(jnp.float32)).astype(
        jnp.bfloat16
    )
    out_grad = cotangent.astype(jnp.float32)
    grad_down = heads_dot("tf,td->fd", hidden_low, cotangent)
    grad_hidden = heads_dot("td,fd->tf", cotangent, w_down)
    grad_gate = grad_hidden * up_vals * gate_sig * (1.0 + gate_vals * (1.0 - gate_sig))
    grad_up = grad_hidden * silu_vals
    grad_gu_low = jnp.stack([grad_gate, grad_up]).astype(jnp.bfloat16)
    grad_gateup = heads_dot("td,jte->jde", normed_two_low, grad_gu_low)
    norm_two_part = heads_dot("jte,jde->td", grad_gu_low, w_gateup)
    norm_two_grad = lax.psum(norm_two_part.astype(jnp.bfloat16), "wt").astype(jnp.float32)
    resid_grad = out_grad + norm_two_back(norm_two_grad)[0]
    resid_low = resid_grad.astype(jnp.bfloat16)
    grad_out = heads_dot("tc,td->cd", att_low, resid_low)
    att_grad = heads_dot("td,cd->tc", resid_low, w_out)
    att_grad_low = att_grad.astype(jnp.bfloat16).reshape(tok_rows, heads_local, head_dim)
    row_delta = jnp.sum(att_grad_low * attended, axis=-1).T

    def grad_block(block_vals, key_pos, key_docs):
        prob_vals = block_probs(block_vals[0], key_pos, key_docs)
        value_grad = heads_dot("hqk,qhd->khd", prob_vals.astype(jnp.bfloat16), att_grad_low)
        prob_grad = heads_dot("qhd,khd->hqk", att_grad_low, block_vals[1])
        raw_grad = (prob_vals * (prob_grad - row_delta[:, :, None]) * score_scale).astype(
            jnp.bfloat16
        )
        query_grad = heads_dot("hqk,khd->qhd", raw_grad, block_vals[0])
        key_grad = heads_dot("hqk,qhd->khd", raw_grad, q_low)
        return (query_grad, key_grad, value_grad)

    def add_rows(target, addend):
        return target + addend

    def cycle_step(turn_idx, cycle_state):
        query_acc, key_cur, value_cur, key_acc, value_acc = cycle_state
        anchor = (ctx_index - turn_idx) % n_ctx

        def cycle_update(block_state, block_vals, key_pos, key_docs, block_row):
            q_acc, k_acc, v_acc = block_state
            query_grad, key_grad, value_grad = grad_block(block_vals, key_pos, key_docs)
            return (q_acc + query_grad, add_rows(k_acc, key_grad), add_rows(v_acc, value_grad))

        query_acc, key_acc, value_acc = over_blocks(
            (key_cur, value_cur), anchor * tok_rows, cycle_update, (query_acc, key_acc, value_acc)
        )
        key_cur, value_cur = from_behind((key_cur, value_cur), "ctx", 1)
        key_acc, value_acc = (
            from_behind_2(key_acc.astype(jnp.bfloat16), "ctx", 1).astype(key_acc.dtype),
            from_behind_2(value_acc.astype(jnp.bfloat16), "ctx", 1).astype(value_acc.dtype),
        )
        return (query_acc, key_cur, value_cur, key_acc, value_acc)

    cycle_start = (zero_heads, k_low, v_low, zero_heads, zero_heads)
    query_acc, _, _, key_acc, value_acc = lax.fori_loop(0, n_ctx, cycle_step, cycle_start)
    qk_pre_grad = rope_back(jnp.concatenate([query_acc, key_acc], axis=1))[0]
    qkv_grad_low = jnp.stack(
        [
            qk_pre_grad[:, :heads_local].reshape(tok_rows, local_width),
            qk_pre_grad[:, heads_local:].reshape(tok_rows, local_width),
            value_acc.reshape(tok_rows, local_width),
        ]
    ).astype(jnp.bfloat16)
    grad_qkv = heads_dot("td,jte->jde", normed_low, qkv_grad_low)
    norm_one_part = heads_dot("jte,jde->td", qkv_grad_low, w_qkv)
    norm_one_grad = lax.psum(norm_one_part.astype(jnp.bfloat16), "wt").astype(jnp.float32)
    input_grad = resid_grad + norm_back(norm_one_grad)[0]
    grad_tiles = jnp.concatenate(
        [grad_qkv.reshape(-1), grad_out.reshape(-1), grad_gateup.reshape(-1), grad_down.reshape(-1)]
    ).reshape(n_tiles, tile_rows, tile_width)
    slot_range = jnp.arange(n_ctx * cap_slots, dtype=jnp.int32)
    matches = slot_ids[None, :] == slot_range[:, None]
    tile_of_slot = jnp.sum(jnp.where(matches, tile_ids[None, :], 0), axis=1)
    slot_used = jnp.any(matches, axis=1)
    slot_grads = lax.psum_scatter(
        jnp.where(slot_used[:, None, None], grad_tiles[tile_of_slot], 0.0).astype(jnp.bfloat16),
        "ctx",
        scatter_dimension=0,
        tiled=True,
    ).astype(jnp.float32)
    new_one = adam_beta * moment_one + (1.0 - adam_beta) * slot_grads
    new_two = adam_beta * moment_two + (1.0 - adam_beta) * slot_grads * slot_grads
    bias_one = 1.0 - adam_beta**STEP
    bias_two = 1.0 - adam_beta**STEP
    step_ratio = new_one / bias_one / (jnp.sqrt(new_two / bias_two) + adam_eps)
    new_master = master - learn_rate * (step_ratio + decay_rate * master)
    return (output, input_grad, new_master, new_one, new_two, new_master.astype(jnp.bfloat16))


AXES = ("ctx", "wt")
LOW = jnp.bfloat16
F32 = jnp.float32


def swap(value, ctx_bits, wt_bits):
    n_ctx, n_wt = lax.axis_size("ctx"), lax.axis_size("wt")
    pairs = [
        (c * n_wt + w, (c ^ ctx_bits) * n_wt + (w ^ wt_bits))
        for c in range(n_ctx)
        for w in range(n_wt)
    ]
    return lax.ppermute(value, AXES, pairs)


def dot(left, right):
    return jnp.dot(left, right, preferred_element_type=F32)


def dot_tn(left, right):
    return lax.dot_general(left, right, (((0,), (0,)), ((), ())), preferred_element_type=F32)


def dot_nt(left, right):
    return lax.dot_general(left, right, (((1,), (1,)), ((), ())), preferred_element_type=F32)


def lane_split(value, lane_starts):
    count, rows, width = value.shape
    homes = lane_starts.shape[0] // 2

    def body(starts, src, *outs):
        for home in range(homes):
            for half in range(2):
                start = pl.multiple_of(starts[2 * home + half], 128)
                outs[home][0, :, half * 128 : half * 128 + 128] = src[
                    0, :, pl.ds(start, 128)
                ].astype(LOW)

    return pl.pallas_call(
        body,
        grid_spec=pltpu.PrefetchScalarGridSpec(
            num_scalar_prefetch=1,
            grid=(count,),
            in_specs=[pl.BlockSpec((1, rows, width), lambda i, s: (i, 0, 0))],
            out_specs=[pl.BlockSpec((1, rows, 256), lambda i, s: (i, 0, 0))] * homes,
        ),
        out_shape=[jax.ShapeDtypeStruct((count, rows, 256), LOW)] * homes,
        name="lane_split",
    )(lane_starts, value)


def lane_join(own, other, lane_starts):
    homes, count, rows, _ = own.shape
    width = homes * 512

    def body(starts, own_ref, other_ref, out):
        for home in range(homes):
            for side, ref in ((0, own_ref), (1, other_ref)):
                for half in range(2):
                    start = pl.multiple_of(starts[4 * home + 2 * side + half], 128)
                    out[0, :, pl.ds(start, 128)] = ref[home, 0, :, half * 128 : half * 128 + 128]

    return pl.pallas_call(
        body,
        grid_spec=pltpu.PrefetchScalarGridSpec(
            num_scalar_prefetch=1,
            grid=(count,),
            in_specs=[
                pl.BlockSpec((homes, 1, rows, 256), lambda i, s: (0, i, 0, 0)),
                pl.BlockSpec(
                    (homes, 1, rows, 256), lambda i, s: (0, (i + count // 2) % count, 0, 0)
                ),
            ],
            out_specs=pl.BlockSpec((1, rows, width), lambda i, s: (i, 0, 0)),
        ),
        out_shape=jax.ShapeDtypeStruct((count, rows, width), LOW),
        name="lane_join",
    )(lane_starts, own, other)


def lane_halves(value, lane_starts):
    count, rows, width = value.shape
    homes = width // 512

    def body(starts, src, own_ref, other_ref):
        for home in range(homes):
            for side, ref in ((0, own_ref), (1, other_ref)):
                for half in range(2):
                    start = pl.multiple_of(starts[4 * home + 2 * side + half], 128)
                    ref[home, 0, :, half * 128 : half * 128 + 128] = src[
                        0, :, pl.ds(start, 128)
                    ].astype(ref.dtype)

    return pl.pallas_call(
        body,
        grid_spec=pltpu.PrefetchScalarGridSpec(
            num_scalar_prefetch=1,
            grid=(count,),
            in_specs=[pl.BlockSpec((1, rows, width), lambda i, s: (i, 0, 0))],
            out_specs=[
                pl.BlockSpec((homes, 1, rows, 256), lambda i, s: (0, i, 0, 0)),
                pl.BlockSpec(
                    (homes, 1, rows, 256), lambda i, s: (0, (i + count // 2) % count, 0, 0)
                ),
            ],
        ),
        out_shape=[
            jax.ShapeDtypeStruct((homes, count, rows, 256), dtype) for dtype in (F32, LOW)
        ],
        name="lane_halves",
    )(lane_starts, value)


def return_halves(grad, lane_starts):
    own, other = lane_halves(grad, lane_starts)
    back = swap(other, 1, 0)
    sums = [(own[m] + back[m].astype(F32)).astype(LOW) for m in range(4)]
    return [sums[0]] + [swap(sums[m], 2 * m, 0) for m in (1, 2, 3)]


def join_grads(query, kv, kv_back, cosine, sine):
    def body(q, here, there, cos, sin, out):
        def undo(values):
            return values * cos[...] + pltpu.roll(values, 64, 1) * sin[...]

        total = here[...] + there[...].astype(F32)
        out[:, :128] = undo(q[...]).astype(LOW)
        out[:, 128:256] = undo(total[:, :128]).astype(LOW)
        out[:, 256:] = total[:, 128:].astype(LOW)

    return pl.pallas_call(
        body,
        in_specs=[VMEM_SPEC] * 5,
        out_specs=VMEM_SPEC,
        out_shape=jax.ShapeDtypeStruct((query.shape[0], 384), LOW),
        name="join_grads",
    )(query, kv, kv_back, cosine, sine)


VMEM_SPEC = pl.BlockSpec(memory_space=pltpu.VMEM)
SMEM_SPEC = pl.BlockSpec(memory_space=pltpu.SMEM)
ANY_SPEC = pl.BlockSpec(memory_space=pl.ANY)


def pick_qkv(came, picked, rows):
    n_src = len(came)

    def body(which, where, *refs):
        srcs, out = refs[:n_src], refs[n_src]

        def copy(tile, carry):
            for n in range(n_src):

                @pl.when(which[tile] == n)
                def _(n=n):
                    for half in range(2):
                        row = pl.multiple_of(half * 512 + (tile % 4) * 128, 128)
                        lane = pl.multiple_of((tile // 4) * 128, 128)
                        out[pl.ds(row, 128), pl.ds(lane, 128)] = srcs[n][
                            where[tile], :, half * 128 : half * 128 + 128
                        ]

            return carry

        lax.fori_loop(0, 12, copy, 0)

    return pl.pallas_call(
        body,
        in_specs=[SMEM_SPEC, SMEM_SPEC] + [VMEM_SPEC] * n_src,
        out_specs=VMEM_SPEC,
        out_shape=jax.ShapeDtypeStruct((1024, 384), LOW),
        name="pick_qkv",
    )(picked, rows, *came)


def row_gather(sources, picked, rows, sizes):
    total = sum(sizes)
    n_src = len(sources)

    def body(which, where, *refs):
        srcs, outs, sem = refs[:n_src], refs[n_src:-1], refs[-1]
        first = 0
        for out, size in zip(outs, sizes):

            def start(j, carry, out=out, first=first):
                t = first + j
                for n in range(n_src):

                    @pl.when(which[t] == n)
                    def _(n=n):
                        pltpu.make_async_copy(srcs[n].at[where[t]], out.at[j], sem.at[t]).start()

                return carry

            lax.fori_loop(0, size, start, 0)
            first += size
        first = 0
        for out, size in zip(outs, sizes):

            def finish(j, carry, out=out, first=first):
                pltpu.make_async_copy(srcs[0].at[0], out.at[j], sem.at[first + j]).wait()
                return carry

            lax.fori_loop(0, size, finish, 0)
            first += size

    tail = sources[0].shape[1:]
    return pl.pallas_call(
        body,
        in_specs=[SMEM_SPEC, SMEM_SPEC] + [VMEM_SPEC] * n_src,
        out_specs=[ANY_SPEC] * len(sizes),
        out_shape=[jax.ShapeDtypeStruct((size,) + tail, LOW) for size in sizes],
        scratch_shapes=[pltpu.SemaphoreType.DMA((total,))],
        name="row_gather",
    )(picked, rows, *sources)


def send_tile(src, tile, to, row, outs, sem):
    for n, out in enumerate(outs):

        @pl.when(to[tile] == n)
        def _(out=out):
            pltpu.make_async_copy(src, out.at[row[tile]], sem.at[tile]).start()


def place_mlp(gate_up, downs, to, row, place, sizes):
    def body(to_ref, row_ref, z_ref, gu_ref, *refs):
        down_refs, outs, sem = refs[:4], refs[4:-1], refs[-1]
        down_tile = lambda m, k: 48 + 4 * ((k + 2 * z_ref[1]) % 4) + (z_ref[0] ^ m)

        def start(j, carry):
            at = pl.ds(pl.multiple_of(128 * j, 128), 128)
            for half in range(2):
                src = gu_ref.at[at, pl.ds(256 * half, 256)]
                send_tile(src, 16 + 16 * half + j, to_ref, row_ref, outs, sem)
            return carry

        lax.fori_loop(0, 16, start, 0)
        for m in range(4):

            def start_down(k, carry, m=m):
                send_tile(down_refs[m].at[k], down_tile(m, k), to_ref, row_ref, outs, sem)
                return carry

            lax.fori_loop(0, 4, start_down, 0)

        def finish(tile, carry):
            pltpu.make_async_copy(down_refs[0].at[0], outs[0].at[0], sem.at[tile]).wait()
            return carry

        lax.fori_loop(16, 64, finish, 0)

    return pl.pallas_call(
        body,
        in_specs=[SMEM_SPEC] * 3 + [VMEM_SPEC] * 5,
        out_specs=[ANY_SPEC] * len(sizes),
        out_shape=[jax.ShapeDtypeStruct((size, 128, 256), LOW) for size in sizes],
        scratch_shapes=[pltpu.SemaphoreType.DMA((64,))],
        name="place_mlp",
    )(to, row, place, gate_up, *downs)


def place_attention(buffers, qkv, outs_from, to, row, place):
    count = len(buffers)

    def body(to_ref, row_ref, z_ref, qkv_ref, *refs):
        out_refs, outs = refs[:4], refs[4 + count : 4 + 2 * count]
        tiles, sem = refs[-2:]

        def start(tile, carry):
            lane = pl.multiple_of((tile // 4) * 128, 128)
            for half in range(2):
                at = pl.ds(pl.multiple_of(half * 512 + (tile % 4) * 128, 128), 128)
                tiles[tile, :, half * 128 : half * 128 + 128] = qkv_ref[at, pl.ds(lane, 128)]
            return carry

        lax.fori_loop(0, 12, start, 0)

        def start_copy(tile, carry):
            send_tile(tiles.at[tile], tile, to_ref, row_ref, outs, sem)
            return carry

        for m in range(4):
            send_tile(out_refs[m].at[0], 12 + (z_ref[0] ^ m), to_ref, row_ref, outs, sem)
        lax.fori_loop(0, 12, start_copy, 0)

        def finish(tile, carry):
            pltpu.make_async_copy(tiles.at[0], outs[0].at[0], sem.at[tile]).wait()
            return carry

        lax.fori_loop(0, 16, finish, 0)

    return pl.pallas_call(
        body,
        in_specs=[SMEM_SPEC] * 3 + [VMEM_SPEC] * 5 + [ANY_SPEC] * count,
        out_specs=[ANY_SPEC] * count,
        out_shape=[jax.ShapeDtypeStruct(buf.shape, buf.dtype) for buf in buffers],
        scratch_shapes=[pltpu.VMEM((12, 128, 256), LOW), pltpu.SemaphoreType.DMA((16,))],
        input_output_aliases={8 + n: n for n in range(count)},
        name="place_attention",
    )(to, row, place, qkv, *outs_from, *buffers)


def after(value, *earlier):
    return lax.optimization_barrier((value,) + earlier)[0]


def key_scores(q, here, there, masks):
    qp, qd, kp, kd = masks
    raw = jnp.concatenate([dot_nt(q, here[:, :128]), dot_nt(q, there[:, :128])], axis=1)
    seen = (kp[...] <= qp[...]) & (kd[...] == qd[...])
    return jnp.where(seen, raw * (1.0 / math.sqrt(HEAD_DIM)), neg_fill)


def attend(query, here, there, masks, n_blocks):
    rows = query.shape[0]
    block = rows // n_blocks

    def body(q, kv, kv_there, qp, qd, kp, kd, out, lse):
        scores = key_scores(q[...], kv[...], kv_there[...], (qp, qd, kp, kd))
        top = jnp.max(scores, axis=1, keepdims=True)
        weights = jnp.exp(scores - top)
        total = jnp.sum(weights, axis=1, keepdims=True)
        probs = (weights * (1.0 / total)).astype(LOW)
        mixed = dot(probs[:, :rows], kv[:, 128:]) + dot(probs[:, rows:], kv_there[:, 128:])
        out[...] = mixed.astype(LOW)
        lse[...] = top + jnp.log(total)

    whole = lambda arr: pl.BlockSpec(arr.shape, lambda i: (0, 0))
    part = lambda arr: pl.BlockSpec((block, arr.shape[1]), lambda i: (i, 0))
    q_pos, q_doc, k_pos, k_doc = masks
    return pl.pallas_call(
        body,
        grid=(n_blocks,),
        in_specs=[
            part(query), whole(here), whole(there), part(q_pos), part(q_doc), whole(k_pos), whole(k_doc),
        ],
        out_specs=[
            pl.BlockSpec((block, HEAD_DIM), lambda i: (i, 0)),
            pl.BlockSpec((block, 1), lambda i: (i, 0)),
        ],
        out_shape=[
            jax.ShapeDtypeStruct((rows, HEAD_DIM), LOW),
            jax.ShapeDtypeStruct((rows, 1), F32),
        ],
        name="attend",
    )(query, here, there, *masks)


def attend_back(query, here, there, out_grad, lse, masks, n_blocks):
    rows = query.shape[0]
    block = rows // n_blocks

    def body(q, kv, kv_there, do, ls, qp, qd, kp, kd, dq, d_here, d_there, acc):
        step = pl.program_id(0)

        @pl.when(step == 0)
        def _():
            d_here[...] = jnp.zeros_like(d_here)
            acc[...] = jnp.zeros_like(acc)

        scores = key_scores(q[...], kv[...], kv_there[...], (qp, qd, kp, kd))
        probs = jnp.exp(scores - ls[...])
        prob_grad = jnp.concatenate(
            [dot_nt(do[...], kv[:, 128:]), dot_nt(do[...], kv_there[:, 128:])], axis=1
        )
        delta = jnp.sum(probs * prob_grad, axis=1, keepdims=True)
        score_grad = (probs * (prob_grad - delta) * (1.0 / math.sqrt(HEAD_DIM))).astype(LOW)
        probs_low = probs.astype(LOW)
        dq[...] = dot(score_grad[:, :rows], kv[:, :128]) + dot(
            score_grad[:, rows:], kv_there[:, :128]
        )
        for first, out in ((0, d_here), (rows, acc)):
            out[:, :128] += dot_tn(score_grad[:, first : first + rows], q[...])
            out[:, 128:] += dot_tn(probs_low[:, first : first + rows], do[...])

        @pl.when(step == n_blocks - 1)
        def _():
            d_there[...] = acc[...].astype(LOW)

    whole = lambda arr: pl.BlockSpec(arr.shape, lambda i: (0, 0))
    part = lambda arr: pl.BlockSpec((block, arr.shape[1]), lambda i: (i, 0))
    kept = pl.BlockSpec((rows, 2 * HEAD_DIM), lambda i: (0, 0))
    q_pos, q_doc, k_pos, k_doc = masks
    return pl.pallas_call(
        body,
        grid=(n_blocks,),
        in_specs=[
            part(query), whole(here), whole(there), part(out_grad), part(lse),
            part(q_pos), part(q_doc), whole(k_pos), whole(k_doc),
        ],
        out_specs=[pl.BlockSpec((block, HEAD_DIM), lambda i: (i, 0)), kept, kept],
        out_shape=[
            jax.ShapeDtypeStruct((rows, HEAD_DIM), F32),
            jax.ShapeDtypeStruct((rows, 2 * HEAD_DIM), F32),
            jax.ShapeDtypeStruct((rows, 2 * HEAD_DIM), LOW),
        ],
        scratch_shapes=[pltpu.VMEM((rows, 2 * HEAD_DIM), F32)],
        name="attend_back",
    )(query, here, there, out_grad, lse, *masks)


def update(state, pieces, lane_starts, used, first, done):
    rows, width = state[0].shape[1:]
    count, homes = pieces[0].shape[0], len(pieces)
    bias = 1.0 - adam_beta**STEP

    def body(starts, live, mas, one, two, *refs):
        grads, (new_mas, new_one, new_two, copy) = refs[:homes], refs[-4:]
        alive = live[pl.program_id(0) + first] > 0
        for home in range(homes):
            for half in range(2):
                at = (0, slice(None), pl.ds(pl.multiple_of(starts[2 * home + half], 128), 128))
                grad = grads[home][0, :, half * 128 : half * 128 + 128].astype(F32)
                grad = jnp.where(alive, grad, 0.0)
                mean = adam_beta * (one[at] + grad)
                square = adam_beta * (two[at] + grad * grad)
                spread = square * (1.0 / bias)
                root = spread * lax.rsqrt(spread) + adam_eps
                step = mean * (learn_rate / bias) / root
                new = mas[at] * (1.0 - learn_rate * decay_rate) - step
                new_mas[at] = new
                new_one[at] = mean
                new_two[at] = square
                copy[at] = new.astype(LOW)

    slot = pl.BlockSpec((1, rows, width), lambda i, s, u: (i + first, 0, 0))
    piece = pl.BlockSpec((1, rows, 256), lambda i, s, u: (i, 0, 0))
    shape = state[0].shape
    return pl.pallas_call(
        body,
        grid_spec=pltpu.PrefetchScalarGridSpec(
            num_scalar_prefetch=2,
            grid=(count,),
            in_specs=[slot] * 3 + [piece] * homes + [ANY_SPEC] * len(done),
            out_specs=[slot] * 4,
        ),
        out_shape=[jax.ShapeDtypeStruct(shape, F32)] * 3 + [jax.ShapeDtypeStruct(shape, LOW)],
        input_output_aliases={5 + homes + n: n for n in range(len(done))},
        name="update",
    )(lane_starts, used, *state, *pieces, *done)


def stack_rows(blocks):
    rows, width = blocks[0].shape

    def body(*refs):
        for n, ref in enumerate(refs[:-1]):
            refs[-1][n * rows : (n + 1) * rows] = ref[...]

    return pl.pallas_call(
        body,
        in_specs=[VMEM_SPEC] * len(blocks),
        out_specs=VMEM_SPEC,
        out_shape=jax.ShapeDtypeStruct((len(blocks) * rows, width), LOW),
        name="stack_rows",
    )(*blocks)


def gather_rows(piece):
    near = [piece] + [swap(piece, 2 * k, 0) for k in (1, 2, 3)]
    blocks = []
    for part in near:
        pair = jnp.concatenate([part, swap(part, 0, 2)])
        blocks += [pair, swap(pair, 0, 1)]
    return stack_rows(blocks), near[1:]


def scatter_sum(partial_sum):
    quarter = partial_sum.shape[0] // 4
    half, rows = quarter // 2, quarter // 4
    kept = [None] * 4
    for k in (3, 2, 1, 0):
        chunk = partial_sum[quarter * k : quarter * (k + 1)]
        other = swap(chunk[half:].astype(LOW), 0, 1)
        pair = chunk[:half].astype(F32) + other.astype(F32)
        other = swap(pair[rows:].astype(LOW), 0, 2)
        kept[k] = pair[:rows] + other.astype(F32)
    total = kept[0]
    came = [swap(kept[k].astype(LOW), 2 * k, 0) for k in (3, 2, 1)]
    for part in came:
        total = total + part.astype(F32)
    return total, other


def share_rows(piece, wt_index):
    rows = piece.shape[0]
    out = jnp.zeros((4 * rows,) + piece.shape[1:], piece.dtype)
    over_y = swap(piece, 0, 2)
    over_core, over_both = swap(piece, 0, 1), swap(over_y, 0, 1)
    for bits, part in ((0, piece), (2, over_y), (1, over_core), (3, over_both)):
        out = lax.dynamic_update_slice(out, part, ((wt_index ^ bits) * rows, 0))
    return out


def rotate(values, cosine, sine):
    half = values.shape[-1] // 2
    first, second = values[:, :half], values[:, half:]
    return jnp.concatenate([first * cosine - second * sine, second * cosine + first * sine], axis=1)


def fast_shards(tokens, cotangent, doc_lengths, owners, master, moment_one, moment_two):
    ctx, wt = lax.axis_index("ctx"), lax.axis_index("wt")
    z_at, x_at = ctx // 2, ctx % 2
    tok_rows, width = tokens.shape
    cap, tile_rows, _ = master.shape
    n_tiles = owners.shape[0]
    rows = tok_rows // 4
    bits = jnp.arange(4, dtype=jnp.int32)
    homes = jnp.arange(8, dtype=jnp.int32) ^ ctx
    lane_starts = (
        ((2 * (homes % 2))[:, None] + jnp.arange(2, dtype=jnp.int32)) * 4 + (homes // 2)[:, None]
    ).reshape(-1) * 128

    owner_col = owners[:, 0]
    tile_ids = jnp.arange(n_tiles, dtype=jnp.int32)
    earlier = (owner_col[None, :] == owner_col[:, None]) & (tile_ids[None, :] < tile_ids[:, None])
    slot_in_owner = jnp.sum(earlier.astype(jnp.int32), axis=1)
    owner_bits = owner_col ^ ctx

    def to_cut_order(values):
        cut_vals = values.reshape(-1, width // 4, 4).transpose(0, 2, 1).reshape(-1, width)
        flipped = jnp.concatenate([cut_vals[:, width // 2 :], cut_vals[:, : width // 2]], axis=1)
        return jnp.where(x_at == 0, cut_vals, flipped)

    def from_cut_order(values):
        flipped = jnp.concatenate([values[:, width // 2 :], values[:, : width // 2]], axis=1)
        cut_vals = jnp.where(x_at == 0, values, flipped)
        return cut_vals.reshape(-1, 4, width // 4).transpose(0, 2, 1).reshape(-1, width)

    cut = lane_split(master, lane_starts)
    came = [cut[0]] + [swap(cut[k], k, 0) for k in range(1, 8)]
    tokens_later = after(tokens, cut[0])
    inputs = lax.dynamic_slice(tokens_later, (wt * rows, 0), (rows, width)).astype(F32)
    normed, norm_back = jax.vjp(layer_norm, inputs)
    normed_cut = to_cut_order(normed.astype(LOW))
    normed_all, normed_came = gather_rows(after(normed_cut, came[4], came[5]))
    w_qkv = pick_qkv(came, owner_bits[:12], slot_in_owner[:12])
    w_qkv_pair = swap(w_qkv, 1, 0)
    out_grad_low = lax.dynamic_slice(cotangent, (wt * rows, 0), (rows, width))
    grad_all, _ = gather_rows(after(out_grad_low, w_qkv, *normed_came))
    wanted = jnp.concatenate(
        [
            jnp.arange(16, 48, dtype=jnp.int32),
            12 + (z_at ^ bits),
            (48 + 4 * ((bits + 2 * x_at) % 4)[None, :] + (z_at ^ bits)[:, None]).reshape(-1),
        ]
    )
    wanted = after(wanted, w_qkv)
    home_gate, home_up, *sends = row_gather(
        came, owner_bits[wanted], slot_in_owner[wanted], [16, 16] + [1] * 4 + [4] * 4
    )
    out_came = [sends[0]] + [swap(sends[m], 2 * m, 0) for m in (1, 2, 3)]
    down_here = [sends[4]] + [swap(sends[4 + m], 2 * m, 0) for m in (1, 2, 3)]
    down_here = jnp.stack(down_here)

    block_z = z_at ^ bits
    block_w = wt ^ jnp.array([0, 2, 1, 3], jnp.int32)

    def group_positions(x_index):
        starts = (2 * block_z + x_index)[:, None] * tok_rows + block_w[None, :] * rows
        return (starts.reshape(-1)[:, None] + jnp.arange(rows, dtype=jnp.int32)).reshape(-1)

    q_pos = group_positions(x_at)
    k_pos = jnp.concatenate([q_pos, group_positions(1 - x_at)])
    doc_starts = jnp.cumsum(doc_lengths) - doc_lengths
    q_doc, k_doc = doc_index(q_pos, doc_starts), doc_index(k_pos, doc_starts)
    masks = (q_pos[:, None], q_doc[:, None], k_pos[None, :], k_doc[None, :])
    freqs = rope_base ** (-jnp.arange(HEAD_DIM // 2, dtype=F32) * (2.0 / HEAD_DIM))
    angles = q_pos.astype(F32)[:, None] * freqs[None, :]
    cosine, sine = jnp.cos(angles), jnp.sin(angles)

    half = width // 2
    qkv = dot(normed_all[:, :half], w_qkv) + dot(normed_all[:, half:], w_qkv_pair)
    query = rotate(qkv[:, :128], cosine, sine).astype(LOW)
    kv_here = jnp.concatenate(
        [rotate(qkv[:, 128:256], cosine, sine).astype(LOW), qkv[:, 256:].astype(LOW)], axis=1
    )
    kv_there = swap(kv_here, 1, 0)
    out_here = after(jnp.stack(out_came), kv_here)
    out_there = swap(out_here, 1, 0)
    att_low, lse = attend(query, kv_here, kv_there, masks, 4)
    w_out = lane_join(out_here, out_there, lane_starts).reshape(tile_rows, width)

    gate_later, up_later = lax.optimization_barrier((home_gate, home_up, kv_there))[:2]
    pair_gate, pair_up = swap(gate_later, 1, 0), swap(up_later, 1, 0)
    down_there = swap(after(down_here, kv_there), 1, 0)
    w_down = lane_join(down_here, down_there, lane_starts).reshape(512, width)
    w_gu = jnp.concatenate(
        [part.reshape(width, 256) for part in (home_gate, home_up, pair_gate, pair_up)], axis=1
    )
    att_part = dot(att_low, w_out).astype(LOW)
    att_out, _ = scatter_sum(att_part)
    residual = inputs + att_out

    normed_two, norm_two_back = jax.vjp(layer_norm, residual)
    two_all, _ = gather_rows(normed_two.astype(LOW))
    gu = dot(two_all, w_gu)
    gate = jnp.concatenate([gu[:, :256], gu[:, 512:768]], axis=1)
    up = jnp.concatenate([gu[:, 256:512], gu[:, 768:]], axis=1)
    gate_sig = jax.nn.sigmoid(gate)
    silu = gate * gate_sig
    hidden = (silu * up).astype(LOW)

    hidden_grad = dot_nt(grad_all, w_down)
    grad_gate = (hidden_grad * up * gate_sig * (1.0 + gate * (1.0 - gate_sig))).astype(LOW)
    grad_up = (hidden_grad * silu).astype(LOW)
    grad_gu = jnp.concatenate(
        [grad_gate[:, :256], grad_up[:, :256], grad_gate[:, 256:], grad_up[:, 256:]], axis=1
    )
    two_grad, begun = scatter_sum(dot_nt(grad_gu, w_gu).astype(LOW))
    hidden_later = after(hidden, begun)
    grad_w_down = dot_tn(hidden_later, grad_all)

    resid_grad = out_grad_low.astype(F32) + norm_two_back(two_grad)[0]
    resid_all, _ = gather_rows(resid_grad.astype(LOW))
    grad_w_gu = dot_tn(two_all, after(grad_gu, two_grad))
    gu_back = swap(grad_w_gu[:, 512:].astype(LOW), 1, 0)
    down, _ = scatter_sum(dot(after(hidden, two_grad), w_down).astype(LOW))
    output = share_rows((residual + down).astype(LOW), wt)
    gu_sum = (grad_w_gu[:, :512] + gu_back.astype(F32)).astype(LOW)
    down_came = return_halves(grad_w_down.reshape(4, tile_rows, width), lane_starts)

    part_slots = cap // 2 + 1
    send_to = owner_bits + 8 * (slot_in_owner // part_slots)
    send_row = slot_in_owner % part_slots
    place = jnp.stack([z_at, x_at])
    sends = place_mlp(
        gu_sum, down_came, send_to, send_row, place, [part_slots] * 8 + [cap - part_slots] * 8
    )

    att_grad = dot_nt(resid_all, w_out).astype(LOW)
    out_grad_came = return_halves(
        dot_tn(att_low, resid_all).reshape(1, tile_rows, width), lane_starts
    )
    query_grad, kv_grad, kv_grad_there = attend_back(
        query, kv_here, kv_there, att_grad, lse, masks, 4
    )
    kv_grad_back = swap(kv_grad_there, 1, 0)
    qkv_grad = join_grads(
        query_grad,
        kv_grad,
        kv_grad_back,
        jnp.concatenate([cosine, cosine], axis=1),
        jnp.concatenate([sine, -sine], axis=1),
    )
    qkv_back = swap(dot_tn(normed_all[:, half:], qkv_grad).astype(LOW), 1, 0)
    qkv_sum = (dot_tn(normed_all[:, :half], qkv_grad) + qkv_back.astype(F32)).astype(LOW)
    sends = place_attention(sends, qkv_sum, out_grad_came, send_to, send_row, place)

    qkv_grad_later = after(qkv_grad, sends[0])
    one_part = jnp.concatenate(
        [dot_nt(qkv_grad_later, w_qkv), dot_nt(qkv_grad_later, w_qkv_pair)], axis=1
    )
    one_grad = from_cut_order(scatter_sum(one_part.astype(LOW))[0])
    input_grad = resid_grad + norm_back(one_grad)[0]
    input_grad = share_rows(input_grad.astype(LOW), wt)
    input_grad = input_grad.astype(F32)

    slot_range = jnp.arange(cap, dtype=jnp.int32) + ctx * cap
    used = jnp.any(
        (owner_col * cap + slot_in_owner)[None, :] == slot_range[:, None], axis=1
    ).astype(jnp.int32)
    state = (master, moment_one, moment_two)
    first, second = [sends[0]], [sends[8]]
    first += [swap(sends[k], k, 0) for k in range(1, 8)]
    for k in range(1, 8):
        second.append(swap(after(sends[8 + k], first[k]), k, 0))
    done = update(state, first, lane_starts, used, 0, ())
    done = update(state, second, lane_starts, used, part_slots, tuple(done))
    return (output, input_grad) + tuple(done)


def choose_shards(*args):
    sizes = (lax.axis_size("ctx"), lax.axis_size("wt"), args[0].shape, args[4].shape[1:])
    if sizes == (8, 4, (256, 2048), (128, 2048)) and args[3].shape[0] == 64:
        return fast_shards(*args)
    return general_shards(*args)


def solution(mesh):
    placed = (
        P("ctx", None),
        P("ctx", None),
        P(),
        P(),
        P("ctx", None, "wt"),
        P("ctx", None, "wt"),
        P("ctx", None, "wt"),
    )
    return jax.shard_map(
        choose_shards,
        mesh=mesh,
        in_specs=placed,
        out_specs=(
            P("ctx", None),
            P("ctx", None),
            P("ctx", None, "wt"),
            P("ctx", None, "wt"),
            P("ctx", None, "wt"),
            P("ctx", None, "wt"),
        ),
        check_vma=False,
    )
```
